32 devices in a mesh: groups: 2 (over y), reach: 4 (over z), day: 2 (over x), head: 2 (over core).
Axes of the slice: x: 2, y: 2, z: 4, core: 2. Of those that a mesh axis runs over, the one named last changes fastest.
Arguments:
- inputs: bfloat16 [4, 8192, 256], P(('groups', 'day'), 'reach'), parts along dimension 0, may hold values from -8 to 8
- upstream: bfloat16 [4, 8192, 256], P(('groups', 'day'), 'reach'), parts along dimension 0, may hold values from -6 to 6
- query_weight: bfloat16 [256, 256], P(None, 'head'), may hold values from -0.375 to 0.375
- key_weight: bfloat16 [256, 256], P(None, 'head'), may hold values from -0.375 to 0.375
- value_weight: bfloat16 [256, 256], P(None, 'head'), may hold values from -0.375 to 0.375
- output_weight: bfloat16 [256, 256], P('head'), may hold values from -0.375 to 0.375
- partner: int32 [128], P('groups'), parts along dimension 0, may hold values from 0 to 63, as said below
- counts: int32 [128], P('groups'), parts along dimension 0, may hold values from 32 to 128, as said below
Outputs:
- delta_inputs: bfloat16 [4, 8192, 256], P(('groups', 'day'), 'reach', 'head'), parts along dimension 0
- delta_query_weight: float32 [512, 256], P('groups', 'head'), parts along dimension 0
- delta_key_weight: float32 [512, 256], P('groups', 'head'), parts along dimension 0
- delta_value_weight: float32 [512, 256], P('groups', 'head'), parts along dimension 0
- delta_output_weight: float32 [512, 256], P(('groups', 'head')), parts along dimension 0
The draws below stay inside these ranges and needn't reach their ends.
There are 2 independent parts, one for each index of `groups`. The reference program is written for one: setup_inputs(seed, part) draws one part's arguments, and reference() takes and returns one part's arrays. A program takes and returns all parts, laid end to end along the dimension named above; an argument that names none is the same for every part. Nothing has to cross between parts.
Inputs may be any that keep to these rules, and one draw needn't show every extreme that they name: Each block is the partner of exactly one block. Block b is held by reach index b // 16; at most 8 of the blocks held by one reach index have their partners held by one reach index. Reaches 0 to counts - 1 of a block are valid.
All inputs are finite; a program needn't handle non-finite values.
Results may differ from the reference program's by a relative error of at most 0.012.
The reference program's roundings to bfloat16 on the way count: a program that leaves them out, or rounds other values in their place, can miss the bound.
Values may be sent and summed in bfloat16 or wider, within the bound.
No kernel may reach another device: no remote copies, remote signals or barrier semaphores. Data moves between devices by JAX's collectives and lax.ppermute only.
A program may use at most 64 MiB of HBM per device.

```python
import math
import jax
import jax.numpy as jnp
from jax import lax

HEADS = 8
BLOCK = 128
BLK_DEV = 16
D = 256
DAYS = 2
NBLK = 64
REACHES = 8192
CAP = 8


def row_permutation(subkey):
    return jax.random.permutation(subkey, BLK_DEV)


def draw_partner(key, part):
    reach_total = NBLK // BLK_DEV
    half_count = reach_total // 2
    key_shift, key_send, key_recv = jax.random.split(key, 3)
    offsets = jax.random.permutation(key_shift, reach_total)[:half_count]
    send_order = jax.vmap(row_permutation)(jax.random.split(key_send, reach_total))
    recv_order = jax.vmap(row_permutation)(jax.random.split(key_recv, reach_total))
    slot_index = jnp.arange(BLK_DEV, dtype=jnp.int32)
    group_index = slot_index // CAP
    within_group = slot_index % CAP
    receiver = jnp.arange(reach_total, dtype=jnp.int32)[:, None]
    sources = (receiver + offsets[group_index][None, :]) % reach_total
    source_slot = jnp.broadcast_to((group_index * CAP + within_group)[None, :], (reach_total, BLK_DEV))
    source_local = send_order[sources, source_slot]
    targets = receiver * BLK_DEV + recv_order
    chosen = sources * BLK_DEV + source_local
    result = jnp.zeros((NBLK,), jnp.int32).at[targets.reshape(-1)].set(chosen.reshape(-1).astype(jnp.int32))
    return result.astype(jnp.int32)


def draw_counts(key, part):
    key_draw, key_pick = jax.random.split(key)
    values = jax.random.randint(key_draw, (NBLK,), BLOCK // 4, BLOCK + 1).astype(jnp.int32)
    picked = jax.random.permutation(key_pick, NBLK)
    values = values.at[picked[0]].set(BLOCK)
    values = values.at[picked[1]].set(BLOCK // 4)
    return values.astype(jnp.int32)


def draw_inputs(key, part):
    key_base = jax.random.fold_in(key, 0)
    base = jax.random.normal(key_base, (DAYS, REACHES, D), jnp.float32)
    return jnp.clip(base, -4.0, 4.0).astype(jnp.bfloat16)


def shard_levels(rng, dims, shards, low, largest):
    factor_of, own = 1.0, jax.random.fold_in(rng, 6)
    for axis_at, shards_of in shards:
        draws = jnp.exp(jax.random.uniform(jax.random.fold_in(own, axis_at), (shards_of,), jnp.float32, low / len(shards), largest / len(shards)))
        factor_of = factor_of * jnp.repeat(draws, dims[axis_at] // shards_of).reshape([-1 if axis == axis_at else 1 for axis in range(len(dims))])
    return factor_of


def gaussian(stream_key, shape, scale, bound, cuts=(), held_as=jnp.bfloat16):
    values = scale * jax.random.normal(stream_key, shape, jnp.float32)
    if cuts:
        values = values * shard_levels(stream_key, shape, cuts, -0.22, 0.18)
    return jnp.clip(values, -bound, bound).astype(held_as)


def setup_inputs(seed: int = 0, part: int = 0) -> dict:
    splits = jax.random.split(jax.random.key(seed), 9)
    own_keys = jax.random.split(jax.random.fold_in(splits[8], part), 9)
    inputs = draw_inputs(jax.random.fold_in(jax.random.fold_in(splits[8], part), 71), part)
    upstream = gaussian(own_keys[1], (DAYS, REACHES, D), 1.0, 6.0, ((0, 2), (1, 4)))
    query_weight = gaussian(splits[2], (D, D), D ** -0.5, 0.375, ((1, 2),))
    key_weight = gaussian(splits[3], (D, D), D ** -0.5, 0.375, ((1, 2),))
    value_weight = gaussian(splits[4], (D, D), D ** -0.5, 0.375, ((1, 2),))
    output_weight = gaussian(splits[5], (D, D), D ** -0.5, 0.375, ((0, 2),))
    partner = draw_partner(jax.random.fold_in(jax.random.fold_in(splits[8], part), 71), part)
    counts = draw_counts(jax.random.fold_in(jax.random.fold_in(splits[8], part), 71), part)
    return {"inputs": inputs, "upstream": upstream, "query_weight": query_weight, "key_weight": key_weight, "value_weight": value_weight, "output_weight": output_weight, "partner": partner, "counts": counts}


def attend(queries, keys, values, valid, back_out, heads):
    item_count, block_rows, width = queries.shape
    head_size = width // heads
    factor = head_size ** -0.5
    query_heads = queries.astype(jnp.float32).reshape(item_count, block_rows, heads, head_size)
    key_heads = keys.astype(jnp.float32).reshape(item_count, -1, heads, head_size)
    value_heads = values.astype(jnp.float32).reshape(item_count, -1, heads, head_size)
    logits = jnp.einsum("gqhd,gkhd->ghqk", query_heads, key_heads) * factor
    logits = jnp.where(valid[:, None, None, :], logits, -1e30)
    highest = jnp.max(logits, axis=-1, keepdims=True)
    raised = jnp.exp(logits - highest)
    weights = raised / jnp.sum(raised, axis=-1, keepdims=True)
    weights_low = weights.astype(jnp.bfloat16).astype(jnp.float32)
    outputs = jnp.einsum("ghqk,gkhd->gqhd", weights_low, value_heads).astype(jnp.bfloat16)
    back_heads = back_out.astype(jnp.float32).reshape(item_count, block_rows, heads, head_size)
    back_weights = jnp.einsum("gqhd,gkhd->ghqk", back_heads, value_heads)
    centered = back_weights - jnp.sum(weights * back_weights, axis=-1, keepdims=True)
    back_logits = (weights * centered * factor).astype(jnp.bfloat16).astype(jnp.float32)
    back_query = jnp.einsum("ghqk,gkhd->gqhd", back_logits, key_heads)
    back_key = jnp.einsum("ghqk,gqhd->gkhd", back_logits, query_heads)
    back_value = jnp.einsum("ghqk,gqhd->gkhd", weights_low, back_heads)
    return (outputs.reshape(item_count, block_rows, width),
            back_query.reshape(item_count, block_rows, width),
            back_key.reshape(item_count, -1, width),
            back_value.reshape(item_count, -1, width))


def split_terms(terms, block_rows):
    return (terms[:, :block_rows],
            terms[:, block_rows:2 * block_rows].astype(jnp.bfloat16),
            terms[:, 2 * block_rows:].astype(jnp.bfloat16))


def reference(inputs, upstream, query_weight, key_weight, value_weight, output_weight, partner, counts):
    day_count, reach_count, width = inputs.shape
    block_rows = BLOCK
    block_count = reach_count // block_rows
    block_shape = (day_count, block_count, block_rows, width)
    flat_in = inputs.reshape(-1, width)
    flat_up = upstream.reshape(-1, width)
    queries = jnp.dot(flat_in, query_weight, preferred_element_type=jnp.float32).astype(jnp.bfloat16).reshape(block_shape)
    keys = jnp.dot(flat_in, key_weight, preferred_element_type=jnp.float32).astype(jnp.bfloat16).reshape(block_shape)
    values = jnp.dot(flat_in, value_weight, preferred_element_type=jnp.float32).astype(jnp.bfloat16).reshape(block_shape)
    back_out = jnp.dot(flat_up, output_weight.T, preferred_element_type=jnp.float32).astype(jnp.bfloat16).reshape(block_shape)
    positions = jnp.arange(block_rows, dtype=jnp.int32)
    own_valid = positions[None, :] < counts[:, None]
    partner_valid = own_valid[partner]
    day_valid = jnp.arange(day_count, dtype=jnp.int32) > 0
    mask_shape = (day_count, block_count, block_rows)
    valid = jnp.concatenate([jnp.broadcast_to(own_valid[None], mask_shape),
                             jnp.broadcast_to(partner_valid[None], mask_shape),
                             own_valid[None] & day_valid[:, None, None]], axis=-1)
    all_keys = jnp.concatenate([keys, keys[:, partner], jnp.concatenate([jnp.zeros_like(keys[:1]), keys[:-1]], 0)], 2)
    all_values = jnp.concatenate([values, values[:, partner], jnp.concatenate([jnp.zeros_like(values[:1]), values[:-1]], 0)], 2)
    item_count = day_count * block_count
    per_group = math.gcd(item_count, 32)

    def grouped(array):
        return array.reshape((item_count // per_group, per_group) + array.shape[2:])

    def one_group(pieces):
        query_g, key_g, value_g, valid_g, back_g = pieces
        outputs, back_query, back_key, back_value = attend(query_g, key_g, value_g, valid_g, back_g, HEADS)
        return (outputs, back_query.astype(jnp.bfloat16)) + split_terms(back_key, block_rows) + split_terms(back_value, block_rows)

    results = lax.map(one_group, (grouped(queries), grouped(all_keys), grouped(all_values), grouped(valid), grouped(back_out)))
    outputs = results[0].reshape(-1, width)
    back_query = results[1].reshape(-1, width)

    def combine(own_part, partner_part, prior_part):
        own_part = own_part.reshape(block_shape)
        partner_part = partner_part.reshape(block_shape)
        prior_part = prior_part.reshape(block_shape)
        from_partner = jnp.zeros(block_shape, jnp.bfloat16).at[:, partner].set(partner_part)
        from_next = jnp.concatenate([prior_part[1:], jnp.zeros_like(prior_part[:1])], 0)
        total = own_part + from_partner.astype(jnp.float32) + from_next.astype(jnp.float32)
        return total.astype(jnp.bfloat16).reshape(-1, width)

    back_key = combine(results[2], results[3], results[4])
    back_value = combine(results[5], results[6], results[7])
    delta_inputs = (jnp.dot(back_query, query_weight.T, preferred_element_type=jnp.float32)
                    + jnp.dot(back_key, key_weight.T, preferred_element_type=jnp.float32)
                    + jnp.dot(back_value, value_weight.T, preferred_element_type=jnp.float32))
    delta_inputs = delta_inputs.astype(jnp.bfloat16).reshape(inputs.shape)
    delta_query_weight = jnp.dot(flat_in.T, back_query, preferred_element_type=jnp.float32)
    delta_key_weight = jnp.dot(flat_in.T, back_key, preferred_element_type=jnp.float32)
    delta_value_weight = jnp.dot(flat_in.T, back_value, preferred_element_type=jnp.float32)
    delta_output_weight = jnp.dot(outputs.T, flat_up, preferred_element_type=jnp.float32)
    return (delta_inputs, delta_query_weight, delta_key_weight, delta_value_weight, delta_output_weight)
```

```python
import jax
import jax.numpy as jnp
from jax import lax
from jax.experimental import pallas as pl
from jax.experimental.pallas import tpu as pltpu
from jax.sharding import PartitionSpec as P

HD = 32
BLOCK = 128
GROUP = 128
CORES = 2
F32 = jnp.float32
BF16 = jnp.bfloat16
LOG2E = 1.4426950408889634


class Layout:
    def __init__(self, blocks_dev, reach_total):
        self.blocks = blocks_dev
        self.items = blocks_dev // CORES
        self.reach = reach_total
        self.slots = max(1, blocks_dev // reach_total)
        self.block_of = 0
        self.recv_of = self.items
        self.count_own = 2 * self.items
        self.count_partner = 3 * self.items
        self.owner_of = 4 * self.items
        self.item_of = self.owner_of + blocks_dev
        self.home_of = self.item_of + blocks_dev
        self.core = self.home_of + blocks_dev
        self.later_day = self.core + 1
        self.size = -(-(self.core + 2) // 128) * 128


def prepare_kernel(lay, partner, counts, where, inputs, sent, prior, tab, start, used, picks, sems):
    bd, slots = lay.blocks, lay.slots
    reach_pos, core = where[0], where[1]

    def clear(index, carry):
        used[index] = 0
        start[index] = 0
        return carry

    lax.fori_loop(0, lay.reach, clear, 0, unroll=True)

    def count(index, carry):
        source = lax.div(partner[reach_pos * bd + index], bd)
        start[source] = start[source] + 1
        return carry

    lax.fori_loop(0, bd, count, 0)

    def prefix(index, total):
        here = start[index]
        start[index] = total
        return total + here

    lax.fori_loop(0, lay.reach, prefix, jnp.int32(0))

    def assign(index, carry):
        wanted = partner[reach_pos * bd + index]
        source = lax.div(wanted, bd)
        rank = used[source]
        used[source] = rank + 1
        place = start[source] + rank
        owner = lax.bitwise_and(place, 1)
        item = lax.div(place, 2)
        slot = jnp.minimum(lax.div(rank, 2), slots - 1)
        tab[lay.owner_of + index] = owner
        tab[lay.item_of + index] = item

        @pl.when(owner == core)
        def _():
            tab[lay.block_of + item] = index
            tab[lay.recv_of + item] = source * slots + slot
            tab[lay.count_own + item] = counts[reach_pos * bd + index]
            tab[lay.count_partner + item] = counts[wanted]

        return carry

    lax.fori_loop(0, bd, assign, 0)
    tab[lay.core] = core
    tab[lay.later_day] = where[2]

    def clear_picks(index, carry):
        picks[index] = 0
        return carry

    lax.fori_loop(0, lay.reach * slots, clear_picks, 0)

    def one_reach(peer, carry):
        def before(index, total):
            source = lax.div(partner[peer * bd + index], bd)
            return total + jnp.where(source < reach_pos, 1, 0)

        base = lax.fori_loop(0, bd, before, jnp.int32(0), unroll=True)

        def serve(index, rank):
            wanted = partner[peer * bd + index]
            hit = lax.div(wanted, bd) == reach_pos

            @pl.when(hit)
            def _():
                owner = lax.bitwise_and(base + rank, 1)
                slot = jnp.minimum(lax.div(rank, 2), slots - 1)
                local = lax.rem(wanted, bd)
                tab[lay.home_of + local] = (peer * CORES + owner) * slots + slot

                @pl.when(owner == core)
                def _():
                    picks[peer * slots + slot] = local

            return rank + jnp.where(hit, 1, 0)

        lax.fori_loop(0, bd, serve, jnp.int32(0))
        return carry

    lax.fori_loop(0, lay.reach, one_reach, 0)

    copies = []
    for place in range(lay.reach * slots):
        copies.append(
            pltpu.make_async_copy(inputs.at[picks[place]], sent.at[place], sems.at[place])
        )
    for item in range(lay.items):
        copies.append(
            pltpu.make_async_copy(
                inputs.at[tab[lay.block_of + item]],
                prior.at[item],
                sems.at[lay.reach * slots + item],
            )
        )
    for copy in copies:
        copy.start()
    for copy in copies:
        copy.wait()


def dot(left, right):
    return lax.dot_general(left, right, (((1,), (0,)), ((), ())), preferred_element_type=F32)


def dot_t(left, right):
    return lax.dot_general(left, right, (((1,), (1,)), ((), ())), preferred_element_type=F32)


def attention_kernel(
    lay,
    tab,
    own_ref,
    up_ref,
    partner_ref,
    prior_ref,
    mine_ref,
    other_ref,
    keep_ref,
    swap_ref,
    same_ref,
    cross_ref,
    home_ref,
    grad_mine_ref,
    grad_other_ref,
):
    item = pl.program_id(0)
    core = tab[lay.core]
    factor = HD ** (-0.5)
    own, up = own_ref[0], up_ref[0]
    key_inputs = jnp.concatenate([own, partner_ref[0], prior_ref[0]], axis=0)
    width = own.shape[1]

    @pl.when(item == 0)
    def _():
        grad_mine_ref[...] = jnp.zeros_like(grad_mine_ref)
        grad_other_ref[...] = jnp.zeros_like(grad_other_ref)

    def eye(size):
        rows = lax.broadcasted_iota(jnp.int32, (size, size), 0)
        cols = lax.broadcasted_iota(jnp.int32, (size, size), 1)
        return jnp.where(rows == cols, 1.0, 0.0).astype(BF16)

    query_t = jnp.concatenate([mine_ref[256:384, :], other_ref[256:384, :]], axis=0)
    output_w = jnp.concatenate([mine_ref[384:512, :], other_ref[384:512, :]], axis=0)
    queries = dot_t(own, query_t)
    back_out = dot_t(up, output_w)
    key_inputs_t = dot_t(eye(width), key_inputs).astype(BF16)

    count_own = tab[lay.count_own + item]
    count_partner = tab[lay.count_partner + item]
    count_prior = count_own * tab[lay.later_day]
    rows = lax.broadcasted_iota(jnp.int32, (BLOCK, 2 * BLOCK), 0)
    valid = jnp.concatenate([rows < count_own, rows < count_partner, rows < count_prior], axis=0)
    lane_head = lax.broadcasted_iota(jnp.int32, (BLOCK, GROUP), 1) // HD

    back_inputs = None
    outputs_t, back_query_t = [], []
    for group, (weights_ref, grad_ref) in enumerate(
        ((mine_ref, grad_mine_ref), (other_ref, grad_other_ref))
    ):
        kv_t = weights_ref[0:256, :]
        kv = dot_t(key_inputs, kv_t).astype(BF16)
        kv_cols = dot_t(kv_t, key_inputs).astype(BF16)
        keys, values = kv[:, :GROUP], kv[:, GROUP:]
        group_queries = queries[:, group * GROUP : (group + 1) * GROUP]
        group_back = back_out[:, group * GROUP : (group + 1) * GROUP]
        back_keys = back_values = None
        for pair in range(GROUP // HD // 2):
            heads = (2 * pair, 2 * pair + 1)
            query_pair = jnp.concatenate(
                [jnp.where(lane_head == h, group_queries, 0.0) for h in heads], axis=0
            ).astype(BF16)
            back_pair = jnp.concatenate(
                [jnp.where(lane_head == h, group_back, 0.0) for h in heads], axis=0
            ).astype(BF16)
            logits = jnp.where(valid, dot_t(keys, query_pair), -1e30)
            highest = jnp.max(logits, axis=0, keepdims=True)
            raised = jnp.exp2((logits - highest) * (factor * LOG2E))
            scale = 1.0 / jnp.sum(raised, axis=0, keepdims=True)
            weights = raised * scale
            weights_low = weights.astype(BF16)
            back_weights = dot_t(values, back_pair)
            center = jnp.sum(weights * back_weights, axis=0, keepdims=True)
            back_logits = (weights * ((back_weights - center) * factor)).astype(BF16)
            pair_values = dot(weights_low, back_pair)
            pair_keys = dot(back_logits, query_pair)
            back_values = pair_values if back_values is None else back_values + pair_values
            back_keys = pair_keys if back_keys is None else back_keys + pair_keys
            first = 2 * pair * HD
            out_t = dot(kv_cols[GROUP + first : GROUP + first + 2 * HD, :], weights_low)
            query_grad_t = dot(kv_cols[first : first + 2 * HD, :], back_logits)
            for h in range(2):
                lanes = slice(h * BLOCK, (h + 1) * BLOCK)
                outputs_t.append(out_t[h * HD : (h + 1) * HD, lanes])
                back_query_t.append(query_grad_t[h * HD : (h + 1) * HD, lanes])
        back_kv = jnp.concatenate([back_keys, back_values], axis=1).astype(BF16)
        term = dot(back_kv, kv_t)
        back_inputs = term if back_inputs is None else back_inputs + term
        grad_ref[0:256, :] += dot(key_inputs_t, back_kv)

    outputs_t = jnp.concatenate(outputs_t, axis=0).astype(BF16)
    back_query_t = jnp.concatenate(back_query_t, axis=0).astype(BF16)
    query_grad = dot(back_query_t, own)
    output_grad = dot(outputs_t, up)
    grad_mine_ref[256:384, :] += query_grad[:GROUP]
    grad_other_ref[256:384, :] += query_grad[GROUP:]
    grad_mine_ref[384:512, :] += output_grad[:GROUP]
    grad_other_ref[384:512, :] += output_grad[GROUP:]
    back_query = dot_t(eye(BLOCK), back_query_t).astype(BF16)
    own_term = back_inputs[:BLOCK] + dot(back_query, query_t)
    partner_term = back_inputs[BLOCK : 2 * BLOCK].astype(BF16)
    prior_term = back_inputs[2 * BLOCK :]
    half = width // 2
    first_core = core == 0
    keep_ref[0] = jnp.where(first_core, own_term[:, :half], own_term[:, half:])
    swap_ref[0] = jnp.where(first_core, own_term[:, half:], own_term[:, :half])
    same_ref[0] = jnp.where(first_core, prior_term[:, :half], prior_term[:, half:]).astype(BF16)
    cross_ref[0] = jnp.where(first_core, prior_term[:, half:], prior_term[:, :half]).astype(BF16)
    home_ref[0, 0, 0] = partner_term[:, :half]
    home_ref[0, 1, 0] = partner_term[:, half:]


def gather_kernel(lay, tab, keep, swapped, same, cross, home, out):
    core = tab[lay.core]

    def one(block, carry):
        item = tab[lay.item_of + block]
        mine = tab[lay.owner_of + block] == core
        total = jnp.where(mine, keep[item], swapped[item])
        total += jnp.where(mine, same[item].astype(F32), cross[item].astype(F32))
        total += home[tab[lay.home_of + block]].astype(F32)
        out[block] = total.astype(BF16)
        return carry

    lax.fori_loop(0, lay.blocks, one, 0)


def on_device(
    inputs, upstream, query_weight, key_weight, value_weight, output_weight, partner, counts
):
    days_dev, rows_dev, width = inputs.shape
    assert days_dev == 1 and width == 2 * GROUP
    blocks_dev = rows_dev // BLOCK
    reach_total = lax.axis_size("reach")
    day_total = lax.axis_size("day")
    assert lax.axis_size("head") == CORES
    lay = Layout(blocks_dev, reach_total)
    half = width // 2
    in_blocks = inputs.reshape(blocks_dev, BLOCK, width)
    up_blocks = upstream.reshape(blocks_dev, BLOCK, width)
    where = jnp.stack(
        [
            lax.axis_index("reach"),
            lax.axis_index("head"),
            (lax.axis_index("day") > 0).astype(jnp.int32),
        ]
    )
    pack = jnp.concatenate([key_weight.T, value_weight.T, query_weight.T, output_weight], axis=0)
    swap_cores = [(0, 1), (1, 0)]
    pack_other = lax.ppermute(pack, "head", swap_cores)

    smem = pl.BlockSpec(memory_space=pltpu.SMEM)
    anywhere = pl.BlockSpec(memory_space=pl.ANY)
    in_vmem = pl.BlockSpec(memory_space=pltpu.VMEM)
    send_count = lay.reach * lay.slots
    sent, prior, tab = pl.pallas_call(
        lambda *refs: prepare_kernel(lay, *refs),
        out_shape=(
            jax.ShapeDtypeStruct((send_count, BLOCK, width), BF16),
            jax.ShapeDtypeStruct((lay.items, BLOCK, width), BF16),
            jax.ShapeDtypeStruct((lay.size,), jnp.int32),
        ),
        in_specs=[smem, smem, smem, anywhere],
        out_specs=(anywhere, anywhere, smem),
        scratch_shapes=[
            pltpu.SMEM((lay.reach,), jnp.int32),
            pltpu.SMEM((lay.reach,), jnp.int32),
            pltpu.SMEM((send_count,), jnp.int32),
            pltpu.SemaphoreType.DMA((send_count + lay.items,)),
        ],
        name="prepare",
    )(partner, counts, where, in_blocks)

    received = lax.all_to_all(
        sent.reshape(lay.reach, lay.slots * BLOCK, width), "reach", 0, 0, tiled=True
    ).reshape(send_count, BLOCK, width)
    prior_inputs = lax.ppermute(prior, "day", [(d, d + 1) for d in range(day_total - 1)])

    def at_item(item, tab):
        return (item, 0, 0)

    def at_block(item, tab):
        return (tab[lay.block_of + item], 0, 0)

    def at_recv(item, tab):
        return (tab[lay.recv_of + item], 0, 0)

    def at_home(item, tab):
        place = tab[lay.recv_of + item]
        return (lax.div(place, lay.slots), 0, lax.rem(place, lay.slots), 0, 0)

    def fixed(item, tab):
        return (0, 0)

    full_block = (1, BLOCK, width)
    half_block = (1, BLOCK, half)
    weights_block = (4 * GROUP, width)
    flops = 2 * lay.items * (23 * BLOCK * width * width + 24 * BLOCK * 3 * BLOCK * 512)
    keep, swap, same, cross, home, grad_mine, grad_other = pl.pallas_call(
        lambda *refs: attention_kernel(lay, *refs),
        grid_spec=pltpu.PrefetchScalarGridSpec(
            num_scalar_prefetch=1,
            grid=(lay.items,),
            in_specs=[
                pl.BlockSpec(full_block, at_block),
                pl.BlockSpec(full_block, at_block),
                pl.BlockSpec(full_block, at_recv),
                pl.BlockSpec(full_block, at_item),
                pl.BlockSpec(weights_block, fixed),
                pl.BlockSpec(weights_block, fixed),
            ],
            out_specs=(
                pl.BlockSpec(half_block, at_item),
                pl.BlockSpec(half_block, at_item),
                pl.BlockSpec(half_block, at_item),
                pl.BlockSpec(half_block, at_item),
                pl.BlockSpec((1, CORES, 1, BLOCK, half), at_home),
                pl.BlockSpec(weights_block, fixed),
                pl.BlockSpec(weights_block, fixed),
            ),
        ),
        out_shape=(
            jax.ShapeDtypeStruct((lay.items, BLOCK, half), F32),
            jax.ShapeDtypeStruct((lay.items, BLOCK, half), F32),
            jax.ShapeDtypeStruct((lay.items, BLOCK, half), BF16),
            jax.ShapeDtypeStruct((lay.items, BLOCK, half), BF16),
            jax.ShapeDtypeStruct((lay.reach, CORES, lay.slots, BLOCK, half), BF16),
            jax.ShapeDtypeStruct(weights_block, F32),
            jax.ShapeDtypeStruct(weights_block, F32),
        ),
        compiler_params=pltpu.CompilerParams(vmem_limit_bytes=32 << 20),
        cost_estimate=pl.CostEstimate(
            flops=flops, bytes_accessed=8 << 20, transcendentals=lay.items * 8 * BLOCK * 3 * BLOCK
        ),
        name="attention",
    )(tab, in_blocks, up_blocks, received, prior_inputs, pack, pack_other)

    came_home = lax.all_to_all(
        home.reshape(lay.reach * CORES, lay.slots * BLOCK, half),
        ("reach", "head"),
        0,
        0,
        tiled=True,
    ).reshape(lay.reach * CORES * lay.slots, BLOCK, half)
    grad_swapped = lax.ppermute(grad_other, "head", swap_cores)
    swapped = lax.ppermute(swap, "head", swap_cores)
    same_came = lax.ppermute(
        same, "day", [(d + 1, d) for d in range(day_total - 1)]
    )
    cross_came = lax.ppermute(
        cross,
        ("day", "head"),
        [
            ((d + 1) * CORES + c, d * CORES + 1 - c)
            for d in range(day_total - 1)
            for c in range(CORES)
        ],
    )
    parts = lay.reach * day_total
    grad_rows = 4 * GROUP
    shares = (grad_mine + grad_swapped).astype(BF16).reshape(parts, grad_rows // parts, width)
    shares = lax.all_to_all(shares, ("reach", "day"), 0, 0, tiled=True)
    share = jnp.sum(shares.astype(F32), axis=0)
    grads = lax.all_gather(share, ("reach", "day"), axis=0, tiled=True)

    back_blocks = pl.pallas_call(
        lambda *refs: gather_kernel(lay, *refs),
        out_shape=jax.ShapeDtypeStruct((blocks_dev, BLOCK, half), BF16),
        in_specs=[smem] + [in_vmem] * 5,
        out_specs=in_vmem,
        compiler_params=pltpu.CompilerParams(vmem_limit_bytes=16 << 20),
        name="assemble",
    )(tab, keep, swapped, same_came, cross_came, came_home)
    return (
        back_blocks.reshape(1, rows_dev, half),
        grads[256:384].T,
        grads[0:256, :GROUP],
        grads[0:256, GROUP:],
        grads[384:512],
    )


def solution(mesh):
    placed = (
        P(("groups", "day"), "reach", None),
        P(("groups", "day"), "reach", None),
        P(None, "head"),
        P(None, "head"),
        P(None, "head"),
        P("head", None),
        P("groups"),
        P("groups"),
    )
    return jax.shard_map(
        on_device,
        mesh=mesh,
        in_specs=placed,
        out_specs=(
            P(("groups", "day"), "reach", "head"),
            P("groups", "head"),
            P("groups", "head"),
            P("groups", "head"),
            P(("groups", "head"), None),
        ),
        check_vma=False,
    )
```

```python
import jax
import jax.numpy as jnp
from jax import lax
from jax.experimental import pallas as pl
from jax.experimental.pallas import tpu as pltpu
from jax.sharding import PartitionSpec as P

HD = 32
BLOCK = 128
GROUP = 128
CORES = 2
CHUNKS = 2
WORKERS = CORES * CHUNKS
F32 = jnp.float32
BF16 = jnp.bfloat16
LOG2E = 1.4426950408889634


class Layout:
    def __init__(self, blocks_dev, reach_total):
        self.blocks = blocks_dev
        self.items = blocks_dev // CORES
        self.chunk_items = self.items // CHUNKS
        self.reach = reach_total
        self.slots = max(1, 2 * blocks_dev // reach_total // WORKERS)
        self.places = reach_total * self.slots
        self.block_of = 0
        self.recv_of = self.items
        self.count_own = 2 * self.items
        self.count_partner = 3 * self.items
        self.owner_of = 4 * self.items
        self.item_of = self.owner_of + blocks_dev
        self.home_of = self.item_of + blocks_dev
        self.chunk_of = self.home_of + blocks_dev
        self.core = self.chunk_of + blocks_dev
        self.later_day = self.core + 1
        self.size = -(-(self.core + 2) // 128) * 128


def prepare_kernel(lay, partner, counts, where, inputs, sent_a, sent_b, prior, tab, start, used, picks):
    bd, slots = lay.blocks, lay.slots
    reach_pos, core = where[0], where[1]

    def clear(index, carry):
        used[index] = 0
        start[index] = 0
        return carry

    lax.fori_loop(0, lay.reach, clear, 0, unroll=True)

    def count(index, carry):
        source = lax.div(partner[reach_pos * bd + index], bd)
        start[source] = start[source] + 1
        return carry

    lax.fori_loop(0, bd, count, 0)

    def prefix(index, total):
        here = start[index]
        start[index] = total
        return total + here

    lax.fori_loop(0, lay.reach, prefix, jnp.int32(0))

    def assign(index, carry):
        wanted = partner[reach_pos * bd + index]
        source = lax.div(wanted, bd)
        rank = used[source]
        used[source] = rank + 1
        place = start[source] + rank
        owner = lax.rem(place, CORES)
        chunk = lax.rem(lax.div(place, CORES), CHUNKS)
        item = chunk * lay.chunk_items + lax.div(place, WORKERS)
        slot = jnp.minimum(lax.div(rank, WORKERS), slots - 1)
        tab[lay.owner_of + index] = owner
        tab[lay.item_of + index] = lax.div(place, WORKERS) * CHUNKS + chunk

        @pl.when(owner == core)
        def _():
            tab[lay.block_of + item] = index
            tab[lay.recv_of + item] = source * slots + slot
            tab[lay.count_own + item] = counts[reach_pos * bd + index]
            tab[lay.count_partner + item] = counts[wanted]

        return carry

    lax.fori_loop(0, bd, assign, 0)
    tab[lay.core] = core
    tab[lay.later_day] = where[2]

    def clear_picks(index, carry):
        picks[index] = 0
        return carry

    lax.fori_loop(0, CHUNKS * lay.places, clear_picks, 0)

    def one_reach(peer, carry):
        def before(index, total):
            source = lax.div(partner[peer * bd + index], bd)
            return total + jnp.where(source < reach_pos, 1, 0)

        base = lax.fori_loop(0, bd, before, jnp.int32(0), unroll=True)

        def serve(index, rank):
            wanted = partner[peer * bd + index]
            hit = lax.div(wanted, bd) == reach_pos

            @pl.when(hit)
            def _():
                place = base + rank
                owner = lax.rem(place, CORES)
                chunk = lax.rem(lax.div(place, CORES), CHUNKS)
                slot = jnp.minimum(lax.div(rank, WORKERS), slots - 1)
                local = lax.rem(wanted, bd)
                tab[lay.home_of + local] = (peer * CORES + owner) * slots + slot
                tab[lay.chunk_of + local] = chunk

                @pl.when(owner == core)
                def _():
                    picks[chunk * lay.places + peer * slots + slot] = local

            return rank + jnp.where(hit, 1, 0)

        lax.fori_loop(0, bd, serve, jnp.int32(0))
        return carry

    lax.fori_loop(0, lay.reach, one_reach, 0)

    def pick_a(place, carry):
        sent_a[place] = inputs[picks[place]]
        return carry

    def pick_b(place, carry):
        sent_b[place] = inputs[picks[lay.places + place]]
        return carry

    def pick_prior(item, carry):
        prior[item] = inputs[tab[lay.block_of + item]]
        return carry

    lax.fori_loop(0, lay.places, pick_a, 0)
    lax.fori_loop(0, lay.places, pick_b, 0)
    lax.fori_loop(0, lay.items, pick_prior, 0)


def dot(left, right):
    return lax.dot_general(left, right, (((1,), (0,)), ((), ())), preferred_element_type=F32)


def dot_t(left, right):
    return lax.dot_general(left, right, (((1,), (1,)), ((), ())), preferred_element_type=F32)


def attention_kernel(
    lay,
    chunk,
    tab,
    own_ref,
    up_ref,
    partner_ref,
    prior_ref,
    mine_ref,
    other_ref,
    *refs,
):
    if chunk:
        start_mine_ref, start_other_ref = refs[0], refs[1]
        carried_refs = refs[2:6]
        refs = refs[6:]
    keep_ref, swap_ref, same_ref, cross_ref, home_ref, grad_mine_ref, grad_other_ref = refs
    step = pl.program_id(0)
    item = step + chunk * lay.chunk_items
    core = tab[lay.core]
    factor = HD ** (-0.5)
    own, up = own_ref[0], up_ref[0]
    key_inputs = jnp.concatenate([own, partner_ref[0], prior_ref[0]], axis=0)
    width = own.shape[1]

    @pl.when(step == 0)
    def _():
        if chunk:
            grad_mine_ref[...] = start_mine_ref[...]
            grad_other_ref[...] = start_other_ref[...]
        else:
            grad_mine_ref[...] = jnp.zeros_like(grad_mine_ref)
            grad_other_ref[...] = jnp.zeros_like(grad_other_ref)

    def eye(size):
        rows = lax.broadcasted_iota(jnp.int32, (size, size), 0)
        cols = lax.broadcasted_iota(jnp.int32, (size, size), 1)
        return jnp.where(rows == cols, 1.0, 0.0).astype(BF16)

    query_t = jnp.concatenate([mine_ref[256:384, :], other_ref[256:384, :]], axis=0)
    output_w = jnp.concatenate([mine_ref[384:512, :], other_ref[384:512, :]], axis=0)
    queries = dot_t(own, query_t)
    back_out = dot_t(up, output_w)
    key_inputs_t = dot_t(eye(width), key_inputs).astype(BF16)

    count_own = tab[lay.count_own + item]
    count_partner = tab[lay.count_partner + item]
    count_prior = count_own * tab[lay.later_day]
    rows = lax.broadcasted_iota(jnp.int32, (BLOCK, 2 * BLOCK), 0)
    valid = jnp.concatenate([rows < count_own, rows < count_partner, rows < count_prior], axis=0)
    lane_head = lax.broadcasted_iota(jnp.int32, (BLOCK, GROUP), 1) // HD

    back_inputs = None
    outputs_t, back_query_t = [], []
    for group, (weights_ref, grad_ref) in enumerate(
        ((mine_ref, grad_mine_ref), (other_ref, grad_other_ref))
    ):
        kv_t = weights_ref[0:256, :]
        kv = dot_t(key_inputs, kv_t).astype(BF16)
        kv_cols = dot_t(kv_t, key_inputs).astype(BF16)
        keys, values = kv[:, :GROUP], kv[:, GROUP:]
        group_queries = queries[:, group * GROUP : (group + 1) * GROUP]
        group_back = back_out[:, group * GROUP : (group + 1) * GROUP]
        back_keys = back_values = None
        for pair in range(GROUP // HD // 2):
            heads = (2 * pair, 2 * pair + 1)
            query_pair = jnp.concatenate(
                [jnp.where(lane_head == h, group_queries, 0.0) for h in heads], axis=0
            ).astype(BF16)
            back_pair = jnp.concatenate(
                [jnp.where(lane_head == h, group_back, 0.0) for h in heads], axis=0
            ).astype(BF16)
            logits = jnp.where(valid, dot_t(keys, query_pair), -1e30)
            highest = jnp.max(logits, axis=0, keepdims=True)
            raised = jnp.exp2((logits - highest) * (factor * LOG2E))
            scale = 1.0 / jnp.sum(raised, axis=0, keepdims=True)
            weights = raised * scale
            weights_low = weights.astype(BF16)
            back_weights = dot_t(values, back_pair)
            center = jnp.sum(weights * back_weights, axis=0, keepdims=True)
            back_logits = (weights * ((back_weights - center) * factor)).astype(BF16)
            pair_values = dot(weights_low, back_pair)
            pair_keys = dot(back_logits, query_pair)
            back_values = pair_values if back_values is None else back_values + pair_values
            back_keys = pair_keys if back_keys is None else back_keys + pair_keys
            first = 2 * pair * HD
            out_t = dot(kv_cols[GROUP + first : GROUP + first + 2 * HD, :], weights_low)
            query_grad_t = dot(kv_cols[first : first + 2 * HD, :], back_logits)
            for h in range(2):
                lanes = slice(h * BLOCK, (h + 1) * BLOCK)
                outputs_t.append(out_t[h * HD : (h + 1) * HD, lanes])
                back_query_t.append(query_grad_t[h * HD : (h + 1) * HD, lanes])
        back_kv = jnp.concatenate([back_keys, back_values], axis=1).astype(BF16)
        term = dot(back_kv, kv_t)
        back_inputs = term if back_inputs is None else back_inputs + term
        grad_ref[0:256, :] += dot(key_inputs_t, back_kv)

    outputs_t = jnp.concatenate(outputs_t, axis=0).astype(BF16)
    back_query_t = jnp.concatenate(back_query_t, axis=0).astype(BF16)
    query_grad = dot(back_query_t, own)
    output_grad = dot(outputs_t, up)
    grad_mine_ref[256:384, :] += query_grad[:GROUP]
    grad_other_ref[256:384, :] += query_grad[GROUP:]
    grad_mine_ref[384:512, :] += output_grad[:GROUP]
    grad_other_ref[384:512, :] += output_grad[GROUP:]
    back_query = dot_t(eye(BLOCK), back_query_t).astype(BF16)
    own_term = back_inputs[:BLOCK] + dot(back_query, query_t)
    partner_term = back_inputs[BLOCK : 2 * BLOCK].astype(BF16)
    prior_term = back_inputs[2 * BLOCK :]
    half = width // 2
    first_core = core == 0
    terms = (
        jnp.where(first_core, own_term[:, :half], own_term[:, half:]),
        jnp.where(first_core, own_term[:, half:], own_term[:, :half]),
        jnp.where(first_core, prior_term[:, :half], prior_term[:, half:]).astype(BF16),
        jnp.where(first_core, prior_term[:, half:], prior_term[:, :half]).astype(BF16),
    )
    for place, (term_ref, term) in enumerate(zip((keep_ref, swap_ref, same_ref, cross_ref), terms)):
        if chunk:
            term_ref[0, 0] = carried_refs[place][0]
            term_ref[0, 1] = term
        else:
            term_ref[0] = term
    home_ref[0, 0, 0] = partner_term[:, :half]
    home_ref[0, 1, 0] = partner_term[:, half:]


def gather_kernel(lay, tab, keep, swapped, same, cross, home_a, home_b, out):
    core = tab[lay.core]

    def one(block, carry):
        item = tab[lay.item_of + block]
        mine = tab[lay.owner_of + block] == core
        place = tab[lay.home_of + block]
        first = tab[lay.chunk_of + block] == 0
        total = jnp.where(mine, keep[item], swapped[item])
        total += jnp.where(mine, same[item].astype(F32), cross[item].astype(F32))
        total += jnp.where(first, home_a[place].astype(F32), home_b[place].astype(F32))
        out[block] = total.astype(BF16)
        return carry

    lax.fori_loop(0, lay.blocks, one, 0)


def attend(lay, chunk, tab, in_blocks, up_blocks, received, prior_inputs, pack, pack_other, carried):
    width = in_blocks.shape[-1]
    half = width // 2
    offset = chunk * lay.chunk_items

    def at_item(step, tab):
        return (offset + step, 0, 0)

    def at_block(step, tab):
        return (tab[lay.block_of + offset + step], 0, 0)

    def at_recv(step, tab):
        return (tab[lay.recv_of + offset + step], 0, 0)

    def at_home(step, tab):
        place = tab[lay.recv_of + offset + step]
        return (lax.div(place, lay.slots), 0, lax.rem(place, lay.slots), 0, 0)

    def fixed(step, tab):
        return (0, 0)

    full_block = (1, BLOCK, width)
    half_block = (1, BLOCK, half)
    weights_block = (4 * GROUP, width)
    in_specs = [
        pl.BlockSpec(full_block, at_block),
        pl.BlockSpec(full_block, at_block),
        pl.BlockSpec(full_block, at_recv),
        pl.BlockSpec(full_block, at_item),
        pl.BlockSpec(weights_block, fixed),
        pl.BlockSpec(weights_block, fixed),
    ]
    operands = [in_blocks, up_blocks, received, prior_inputs, pack, pack_other]
    term_shape = (lay.chunk_items, BLOCK, half)
    term_spec = pl.BlockSpec(half_block, lambda step, tab: (step, 0, 0))
    if chunk:
        in_specs += [pl.BlockSpec(weights_block, fixed)] * 2 + [term_spec] * 4
        operands += [carried[5], carried[6]] + list(carried[:4])
        term_shape = (lay.chunk_items, CHUNKS, BLOCK, half)
        term_spec = pl.BlockSpec((1, CHUNKS, BLOCK, half), lambda step, tab: (step, 0, 0, 0))
    pieces = lay.chunk_items
    flops = 2 * pieces * (23 * BLOCK * width * width + 24 * BLOCK * 3 * BLOCK * 512)
    return pl.pallas_call(
        lambda *refs: attention_kernel(lay, chunk, *refs),
        grid_spec=pltpu.PrefetchScalarGridSpec(
            num_scalar_prefetch=1,
            grid=(pieces,),
            in_specs=in_specs,
            out_specs=(
                *[term_spec] * 4,
                pl.BlockSpec((1, CORES, 1, BLOCK, half), at_home),
                pl.BlockSpec(weights_block, fixed),
                pl.BlockSpec(weights_block, fixed),
            ),
        ),
        out_shape=(
            jax.ShapeDtypeStruct(term_shape, F32),
            jax.ShapeDtypeStruct(term_shape, F32),
            jax.ShapeDtypeStruct(term_shape, BF16),
            jax.ShapeDtypeStruct(term_shape, BF16),
            jax.ShapeDtypeStruct((lay.reach, CORES, lay.slots, BLOCK, half), BF16),
            jax.ShapeDtypeStruct(weights_block, F32),
            jax.ShapeDtypeStruct(weights_block, F32),
        ),
        compiler_params=pltpu.CompilerParams(vmem_limit_bytes=32 << 20),
        cost_estimate=pl.CostEstimate(
            flops=flops, bytes_accessed=5 << 20, transcendentals=pieces * 8 * BLOCK * 3 * BLOCK
        ),
        name=f"attention_{chunk}",
    )(tab, *operands)


def exchanged(value, axis, bit):
    count = lax.axis_size(axis)
    return lax.ppermute(value, axis, [(place, place ^ bit) for place in range(count)])


def summed_over(value, axis, bit):
    while bit < lax.axis_size(axis):
        low = value.astype(BF16)
        value = low.astype(F32) + exchanged(low, axis, bit).astype(F32)
        bit *= 2
    return value


def sum_gradients(total):
    half = total.shape[0] // 2
    low = total.astype(BF16)
    first = lax.rem(lax.axis_index("day"), 2) == 0
    kept = jnp.where(first, low[:half], low[half:])
    given = jnp.where(first, low[half:], low[:half])
    part = kept.astype(F32) + exchanged(given, "day", 1).astype(F32)
    part = summed_over(part, "day", 2)
    part = summed_over(part, "reach", 1).astype(BF16)
    other = exchanged(part, "day", 1)
    upper = jnp.where(first, part, other).astype(F32)
    lower = jnp.where(first, other, part).astype(F32)
    return upper, lower


def on_device(
    inputs, upstream, query_weight, key_weight, value_weight, output_weight, partner, counts
):
    days_dev, rows_dev, width = inputs.shape
    assert days_dev == 1 and width == 2 * GROUP
    blocks_dev = rows_dev // BLOCK
    reach_total = lax.axis_size("reach")
    day_total = lax.axis_size("day")
    assert lax.axis_size("head") == CORES
    lay = Layout(blocks_dev, reach_total)
    half = width // 2
    in_blocks = inputs.reshape(blocks_dev, BLOCK, width)
    up_blocks = upstream.reshape(blocks_dev, BLOCK, width)
    where = jnp.stack(
        [
            lax.axis_index("reach"),
            lax.axis_index("head"),
            (lax.axis_index("day") > 0).astype(jnp.int32),
        ]
    )
    pack = jnp.concatenate([key_weight.T, value_weight.T, query_weight.T, output_weight], axis=0)
    pack_other = exchanged(pack, "head", 1)

    smem = pl.BlockSpec(memory_space=pltpu.SMEM)
    in_vmem = pl.BlockSpec(memory_space=pltpu.VMEM)
    sent_shape = jax.ShapeDtypeStruct((lay.places, BLOCK, width), BF16)
    sent_a, sent_b, prior, tab = pl.pallas_call(
        lambda *refs: prepare_kernel(lay, *refs),
        out_shape=(
            sent_shape,
            sent_shape,
            jax.ShapeDtypeStruct((lay.items, BLOCK, width), BF16),
            jax.ShapeDtypeStruct((lay.size,), jnp.int32),
        ),
        in_specs=[smem, smem, smem, in_vmem],
        out_specs=(in_vmem, in_vmem, in_vmem, smem),
        scratch_shapes=[
            pltpu.SMEM((lay.reach,), jnp.int32),
            pltpu.SMEM((lay.reach,), jnp.int32),
            pltpu.SMEM((CHUNKS * lay.places,), jnp.int32),
        ],
        compiler_params=pltpu.CompilerParams(vmem_limit_bytes=16 << 20),
        name="prepare",
    )(partner, counts, where, in_blocks)

    def outward(sent):
        return lax.all_to_all(
            sent.reshape(lay.reach, lay.slots * BLOCK, width), "reach", 0, 0, tiled=True
        ).reshape(lay.places, BLOCK, width)

    def homeward(home):
        return lax.all_to_all(
            home.reshape(lay.reach * CORES, lay.slots * BLOCK, half),
            ("reach", "head"),
            0,
            0,
            tiled=True,
        ).reshape(lay.reach * CORES * lay.slots, BLOCK, half)

    received_a = outward(sent_a)
    prior_inputs = lax.ppermute(prior, "day", [(d, d + 1) for d in range(day_total - 1)])
    received_b = outward(sent_b)
    shared = (prior_inputs, pack, pack_other)
    first = attend(lay, 0, tab, in_blocks, up_blocks, received_a, *shared, None)
    home_a = homeward(first[4])
    keep, swap, same, cross, home, grad_mine, grad_other = attend(
        lay, 1, tab, in_blocks, up_blocks, received_b, *shared, first
    )
    home_a, home, grad_other = lax.optimization_barrier((home_a, home, grad_other))
    keep, swap, same, cross = (
        term.reshape(lay.items, BLOCK, half) for term in (keep, swap, same, cross)
    )
    home_b = homeward(home)
    grad_swapped = exchanged(grad_other, "head", 1)
    swapped = exchanged(swap, "head", 1)
    same_came = lax.ppermute(same, "day", [(d + 1, d) for d in range(day_total - 1)])
    cross_came = lax.ppermute(
        cross,
        ("day", "head"),
        [
            ((d + 1) * CORES + c, d * CORES + 1 - c)
            for d in range(day_total - 1)
            for c in range(CORES)
        ],
    )
    upper, lower = sum_gradients(grad_mine + grad_swapped)

    back_blocks = pl.pallas_call(
        lambda *refs: gather_kernel(lay, *refs),
        out_shape=jax.ShapeDtypeStruct((blocks_dev, BLOCK, half), BF16),
        in_specs=[smem] + [in_vmem] * 6,
        out_specs=in_vmem,
        compiler_params=pltpu.CompilerParams(vmem_limit_bytes=16 << 20),
        name="assemble",
    )(tab, keep, swapped, same_came, cross_came, home_a, home_b)
    return (
        back_blocks.reshape(1, rows_dev, half),
        lower[:GROUP].T,
        upper[:, :GROUP],
        upper[:, GROUP:],
        lower[GROUP:],
    )


def solution(mesh):
    placed = (
        P(("groups", "day"), "reach", None),
        P(("groups", "day"), "reach", None),
        P(None, "head"),
        P(None, "head"),
        P(None, "head"),
        P("head", None),
        P("groups"),
        P("groups"),
    )
    return jax.shard_map(
        on_device,
        mesh=mesh,
        in_specs=placed,
        out_specs=(
            P(("groups", "day"), "reach", "head"),
            P("groups", "head"),
            P("groups", "head"),
            P("groups", "head"),
            P(("groups", "head"), None),
        ),
        check_vma=False,
    )
```

```python
import jax
import jax.numpy as jnp
from jax import lax
from jax.experimental import pallas as pl
from jax.experimental.pallas import tpu as pltpu
from jax.sharding import PartitionSpec as P

HD = 32
BLOCK = 128
GROUP = 128
CORES = 2
CHUNKS = 2
WORKERS = CORES * CHUNKS
F32 = jnp.float32
BF16 = jnp.bfloat16
LOG2E = 1.4426950408889634


class Layout:
    def __init__(self, blocks_dev, reach_total):
        self.blocks = blocks_dev
        self.items = blocks_dev // CORES
        self.chunk_items = self.items // CHUNKS
        self.reach = reach_total
        self.slots = max(1, 2 * blocks_dev // reach_total // WORKERS)
        self.places = reach_total * self.slots
        self.block_of = 0
        self.recv_of = self.items
        self.count_own = 2 * self.items
        self.count_partner = 3 * self.items
        self.owner_of = 4 * self.items
        self.item_of = self.owner_of + blocks_dev
        self.home_of = self.item_of + blocks_dev
        self.chunk_of = self.home_of + blocks_dev
        self.core = self.chunk_of + blocks_dev
        self.later_day = self.core + 1
        self.size = -(-(self.core + 2) // 128) * 128


def prepare_kernel(lay, partner, counts, where, inputs, sent_a, sent_b, prior, tab, start, used, picks):
    bd, slots = lay.blocks, lay.slots
    reach_pos, core = where[0], where[1]

    def clear(index, carry):
        used[index] = 0
        start[index] = 0
        return carry

    lax.fori_loop(0, lay.reach, clear, 0, unroll=True)

    def count(index, carry):
        source = lax.div(partner[reach_pos * bd + index], bd)
        start[source] = start[source] + 1
        return carry

    lax.fori_loop(0, bd, count, 0)

    def prefix(index, total):
        here = start[index]
        start[index] = total
        return total + here

    lax.fori_loop(0, lay.reach, prefix, jnp.int32(0))

    def assign(index, carry):
        wanted = partner[reach_pos * bd + index]
        source = lax.div(wanted, bd)
        rank = used[source]
        used[source] = rank + 1
        place = start[source] + rank
        owner = lax.rem(place, CORES)
        chunk = lax.rem(lax.div(place, CORES), CHUNKS)
        item = chunk * lay.chunk_items + lax.div(place, WORKERS)
        slot = jnp.minimum(lax.div(rank, WORKERS), slots - 1)
        tab[lay.owner_of + index] = owner
        tab[lay.item_of + index] = lax.div(place, WORKERS) * CHUNKS + chunk

        @pl.when(owner == core)
        def _():
            tab[lay.block_of + item] = index
            tab[lay.recv_of + item] = source * slots + slot
            tab[lay.count_own + item] = counts[reach_pos * bd + index]
            tab[lay.count_partner + item] = counts[wanted]

        return carry

    lax.fori_loop(0, bd, assign, 0)
    tab[lay.core] = core
    tab[lay.later_day] = where[2]

    def clear_picks(index, carry):
        picks[index] = 0
        return carry

    lax.fori_loop(0, CHUNKS * lay.places, clear_picks, 0)

    def one_reach(peer, carry):
        def before(index, total):
            source = lax.div(partner[peer * bd + index], bd)
            return total + jnp.where(source < reach_pos, 1, 0)

        base = lax.fori_loop(0, bd, before, jnp.int32(0), unroll=True)

        def serve(index, rank):
            wanted = partner[peer * bd + index]
            hit = lax.div(wanted, bd) == reach_pos

            @pl.when(hit)
            def _():
                place = base + rank
                owner = lax.rem(place, CORES)
                chunk = lax.rem(lax.div(place, CORES), CHUNKS)
                slot = jnp.minimum(lax.div(rank, WORKERS), slots - 1)
                local = lax.rem(wanted, bd)
                tab[lay.home_of + local] = (peer * CORES + owner) * slots + slot
                tab[lay.chunk_of + local] = chunk

                @pl.when(owner == core)
                def _():
                    picks[chunk * lay.places + peer * slots + slot] = local

            return rank + jnp.where(hit, 1, 0)

        lax.fori_loop(0, bd, serve, jnp.int32(0))
        return carry

    lax.fori_loop(0, lay.reach, one_reach, 0)

    def pick_a(place, carry):
        sent_a[place] = inputs[picks[place]]
        return carry

    def pick_b(place, carry):
        sent_b[place] = inputs[picks[lay.places + place]]
        return carry

    def pick_prior(item, carry):
        prior[item] = inputs[tab[lay.block_of + item]]
        return carry

    lax.fori_loop(0, lay.places, pick_a, 0)
    lax.fori_loop(0, lay.places, pick_b, 0)
    lax.fori_loop(0, lay.items, pick_prior, 0)


def dot(left, right):
    return lax.dot_general(left, right, (((1,), (0,)), ((), ())), preferred_element_type=F32)


def dot_t(left, right):
    return lax.dot_general(left, right, (((1,), (1,)), ((), ())), preferred_element_type=F32)


def attention_kernel(
    lay,
    chunk,
    tab,
    own_ref,
    up_ref,
    partner_ref,
    prior_ref,
    mine_ref,
    other_ref,
    *refs,
):
    if chunk:
        start_mine_ref, start_other_ref = refs[0], refs[1]
        carried_refs = refs[2:6]
        refs = refs[6:]
    keep_ref, swap_ref, same_ref, cross_ref, home_ref, grad_mine_ref, grad_other_ref = refs
    step = pl.program_id(0)
    item = step + chunk * lay.chunk_items
    core = tab[lay.core]
    factor = HD ** (-0.5)
    own, up = own_ref[0], up_ref[0]
    key_inputs = jnp.concatenate([own, partner_ref[0], prior_ref[0]], axis=0)
    width = own.shape[1]

    @pl.when(step == 0)
    def _():
        if chunk:
            grad_mine_ref[...] = start_mine_ref[...]
            grad_other_ref[...] = start_other_ref[...]
        else:
            grad_mine_ref[...] = jnp.zeros_like(grad_mine_ref)
            grad_other_ref[...] = jnp.zeros_like(grad_other_ref)

    def eye(size):
        rows = lax.broadcasted_iota(jnp.int32, (size, size), 0)
        cols = lax.broadcasted_iota(jnp.int32, (size, size), 1)
        return jnp.where(rows == cols, 1.0, 0.0).astype(BF16)

    query_t = jnp.concatenate([mine_ref[256:384, :], other_ref[256:384, :]], axis=0)
    output_w = jnp.concatenate([mine_ref[384:512, :], other_ref[384:512, :]], axis=0)
    queries = dot_t(own, query_t)
    back_out = dot_t(up, output_w)
    key_inputs_t = dot_t(eye(width), key_inputs).astype(BF16)

    count_own = tab[lay.count_own + item]
    count_partner = tab[lay.count_partner + item]
    count_prior = count_own * tab[lay.later_day]
    rows = lax.broadcasted_iota(jnp.int32, (BLOCK, 2 * BLOCK), 0)
    valid = jnp.concatenate([rows < count_own, rows < count_partner, rows < count_prior], axis=0)
    lane_head = lax.broadcasted_iota(jnp.int32, (BLOCK, GROUP), 1) // HD

    back_inputs = None
    outputs_t, back_query_t = [], []
    for group, (weights_ref, grad_ref) in enumerate(
        ((mine_ref, grad_mine_ref), (other_ref, grad_other_ref))
    ):
        kv_t = weights_ref[0:256, :]
        kv = dot_t(key_inputs, kv_t).astype(BF16)
        kv_cols = dot_t(kv_t, key_inputs).astype(BF16)
        keys, values = kv[:, :GROUP], kv[:, GROUP:]
        group_queries = queries[:, group * GROUP : (group + 1) * GROUP]
        group_back = back_out[:, group * GROUP : (group + 1) * GROUP]
        back_keys = back_values = None
        for pair in range(GROUP // HD // 2):
            heads = (2 * pair, 2 * pair + 1)
            query_pair = jnp.concatenate(
                [jnp.where(lane_head == h, group_queries, 0.0) for h in heads], axis=0
            ).astype(BF16)
            back_pair = jnp.concatenate(
                [jnp.where(lane_head == h, group_back, 0.0) for h in heads], axis=0
            ).astype(BF16)
            logits = jnp.where(valid, dot_t(keys, query_pair), -1e30)
            highest = jnp.max(logits, axis=0, keepdims=True)
            raised = jnp.exp2((logits - highest) * (factor * LOG2E))
            scale = 1.0 / jnp.sum(raised, axis=0, keepdims=True)
            weights = raised * scale
            weights_low = weights.astype(BF16)
            back_weights = dot_t(values, back_pair)
            center = jnp.sum(weights * back_weights, axis=0, keepdims=True)
            back_logits = (weights * ((back_weights - center) * factor)).astype(BF16)
            pair_values = dot(weights_low, back_pair)
            pair_keys = dot(back_logits, query_pair)
            back_values = pair_values if back_values is None else back_values + pair_values
            back_keys = pair_keys if back_keys is None else back_keys + pair_keys
            first = 2 * pair * HD
            out_t = dot(kv_cols[GROUP + first : GROUP + first + 2 * HD, :], weights_low)
            query_grad_t = dot(kv_cols[first : first + 2 * HD, :], back_logits)
            for h in range(2):
                lanes = slice(h * BLOCK, (h + 1) * BLOCK)
                outputs_t.append(out_t[h * HD : (h + 1) * HD, lanes])
                back_query_t.append(query_grad_t[h * HD : (h + 1) * HD, lanes])
        back_kv = jnp.concatenate([back_keys, back_values], axis=1).astype(BF16)
        term = dot(back_kv, kv_t)
        back_inputs = term if back_inputs is None else back_inputs + term
        grad_ref[0:256, :] += dot(key_inputs_t, back_kv)

    outputs_t = jnp.concatenate(outputs_t, axis=0).astype(BF16)
    back_query_t = jnp.concatenate(back_query_t, axis=0).astype(BF16)
    query_grad = dot(back_query_t, own)
    output_grad = dot(outputs_t, up)
    grad_mine_ref[256:384, :] += query_grad[:GROUP]
    grad_other_ref[256:384, :] += query_grad[GROUP:]
    grad_mine_ref[384:512, :] += output_grad[:GROUP]
    grad_other_ref[384:512, :] += output_grad[GROUP:]
    back_query = dot_t(eye(BLOCK), back_query_t).astype(BF16)
    own_term = back_inputs[:BLOCK] + dot(back_query, query_t)
    partner_term = back_inputs[BLOCK : 2 * BLOCK].astype(BF16)
    prior_term = back_inputs[2 * BLOCK :]
    half = width // 2
    first_core = core == 0
    terms = (
        jnp.where(first_core, own_term[:, :half], own_term[:, half:]),
        jnp.where(first_core, own_term[:, half:], own_term[:, :half]),
        jnp.where(first_core, prior_term[:, :half], prior_term[:, half:]).astype(BF16),
        jnp.where(first_core, prior_term[:, half:], prior_term[:, :half]).astype(BF16),
    )
    for place, (term_ref, term) in enumerate(zip((keep_ref, swap_ref, same_ref, cross_ref), terms)):
        if chunk:
            term_ref[0, 0] = carried_refs[place][0]
            term_ref[0, 1] = term
        else:
            term_ref[0] = term
    home_ref[0, 0, 0] = partner_term[:, :half]
    home_ref[0, 1, 0] = partner_term[:, half:]


def gather_kernel(lay, tab, keep, swapped, same, cross, home_a, home_b, out):
    core = tab[lay.core]

    def one(block, carry):
        item = tab[lay.item_of + block]
        mine = tab[lay.owner_of + block] == core
        place = tab[lay.home_of + block]
        first = tab[lay.chunk_of + block] == 0
        total = jnp.where(mine, keep[item], swapped[item])
        total += jnp.where(mine, same[item].astype(F32), cross[item].astype(F32))
        total += jnp.where(first, home_a[place].astype(F32), home_b[place].astype(F32))
        out[block] = total.astype(BF16)
        return carry

    lax.fori_loop(0, lay.blocks, one, 0)


def attend(lay, chunk, tab, in_blocks, up_blocks, received, prior_inputs, pack, pack_other, carried):
    width = in_blocks.shape[-1]
    half = width // 2
    offset = chunk * lay.chunk_items

    def at_item(step, tab):
        return (offset + step, 0, 0)

    def at_block(step, tab):
        return (tab[lay.block_of + offset + step], 0, 0)

    def at_recv(step, tab):
        return (tab[lay.recv_of + offset + step], 0, 0)

    def at_home(step, tab):
        place = tab[lay.recv_of + offset + step]
        return (lax.div(place, lay.slots), 0, lax.rem(place, lay.slots), 0, 0)

    def fixed(step, tab):
        return (0, 0)

    full_block = (1, BLOCK, width)
    half_block = (1, BLOCK, half)
    weights_block = (4 * GROUP, width)
    in_specs = [
        pl.BlockSpec(full_block, at_block),
        pl.BlockSpec(full_block, at_block),
        pl.BlockSpec(full_block, at_recv),
        pl.BlockSpec(full_block, at_item),
        pl.BlockSpec(weights_block, fixed),
        pl.BlockSpec(weights_block, fixed),
    ]
    operands = [in_blocks, up_blocks, received, prior_inputs, pack, pack_other]
    term_shape = (lay.chunk_items, BLOCK, half)
    term_spec = pl.BlockSpec(half_block, lambda step, tab: (step, 0, 0))
    if chunk:
        in_specs += [pl.BlockSpec(weights_block, fixed)] * 2 + [term_spec] * 4
        operands += [carried[5], carried[6]] + list(carried[:4])
        term_shape = (lay.chunk_items, CHUNKS, BLOCK, half)
        term_spec = pl.BlockSpec((1, CHUNKS, BLOCK, half), lambda step, tab: (step, 0, 0, 0))
    pieces = lay.chunk_items
    flops = 2 * pieces * (23 * BLOCK * width * width + 24 * BLOCK * 3 * BLOCK * 512)
    return pl.pallas_call(
        lambda *refs: attention_kernel(lay, chunk, *refs),
        grid_spec=pltpu.PrefetchScalarGridSpec(
            num_scalar_prefetch=1,
            grid=(pieces,),
            in_specs=in_specs,
            out_specs=(
                *[term_spec] * 4,
                pl.BlockSpec((1, CORES, 1, BLOCK, half), at_home),
                pl.BlockSpec(weights_block, fixed),
                pl.BlockSpec(weights_block, fixed),
            ),
        ),
        out_shape=(
            pltpu.HBM(term_shape, F32),
            pltpu.HBM(term_shape, F32),
            pltpu.HBM(term_shape, BF16),
            pltpu.HBM(term_shape, BF16),
            pltpu.HBM((lay.reach, CORES, lay.slots, BLOCK, half), BF16),
            pltpu.HBM(weights_block, F32),
            pltpu.HBM(weights_block, F32),
        ),
        compiler_params=pltpu.CompilerParams(vmem_limit_bytes=32 << 20),
        cost_estimate=pl.CostEstimate(
            flops=flops, bytes_accessed=5 << 20, transcendentals=pieces * 8 * BLOCK * 3 * BLOCK
        ),
        name=f"attention_{chunk}",
    )(
        tab,
        *[
            value
            if place == 2
            else pltpu.with_memory_space_constraint(value, pltpu.HBM)
            for place, value in enumerate(operands)
        ],
    )


def exchanged(value, axis, bit):
    count = lax.axis_size(axis)
    return lax.ppermute(value, axis, [(place, place ^ bit) for place in range(count)])


def summed_over(value, axis, bit):
    while bit < lax.axis_size(axis):
        low = value.astype(BF16)
        value = low.astype(F32) + exchanged(low, axis, bit).astype(F32)
        bit *= 2
    return value


def sum_gradients(total, settled):
    half = total.shape[0] // 2
    first = lax.rem(lax.axis_index("day"), 2) == 0
    kept = jnp.where(first, total[:half], total[half:])
    given = jnp.where(first, total[half:], total[:half])
    part = kept + exchanged(given, "day", 1)
    part = summed_over(part, "day", 2)
    part, *settled = lax.optimization_barrier((part, *settled))
    part = summed_over(part, "reach", 1)
    other = exchanged(part, "day", 1)
    upper = jnp.where(first, part, other)
    lower = jnp.where(first, other, part)
    return upper, lower, settled


def on_device(
    inputs, upstream, query_weight, key_weight, value_weight, output_weight, partner, counts
):
    days_dev, rows_dev, width = inputs.shape
    assert days_dev == 1 and width == 2 * GROUP
    blocks_dev = rows_dev // BLOCK
    reach_total = lax.axis_size("reach")
    day_total = lax.axis_size("day")
    assert lax.axis_size("head") == CORES
    lay = Layout(blocks_dev, reach_total)
    half = width // 2
    in_blocks = inputs.reshape(blocks_dev, BLOCK, width)
    up_blocks = upstream.reshape(blocks_dev, BLOCK, width)
    where = jnp.stack(
        [
            lax.axis_index("reach"),
            lax.axis_index("head"),
            (lax.axis_index("day") > 0).astype(jnp.int32),
        ]
    )
    pack = jnp.concatenate([key_weight.T, value_weight.T, query_weight.T, output_weight], axis=0)
    pack_other = exchanged(pack, "head", 1)

    smem = pl.BlockSpec(memory_space=pltpu.SMEM)
    in_vmem = pl.BlockSpec(memory_space=pltpu.VMEM)
    sent_shape = jax.ShapeDtypeStruct((lay.places, BLOCK, width), BF16)
    sent_a, sent_b, prior, tab = pl.pallas_call(
        lambda *refs: prepare_kernel(lay, *refs),
        out_shape=(
            sent_shape,
            sent_shape,
            jax.ShapeDtypeStruct((lay.items, BLOCK, width), BF16),
            jax.ShapeDtypeStruct((lay.size,), jnp.int32),
        ),
        in_specs=[smem, smem, smem, in_vmem],
        out_specs=(in_vmem, in_vmem, in_vmem, smem),
        scratch_shapes=[
            pltpu.SMEM((lay.reach,), jnp.int32),
            pltpu.SMEM((lay.reach,), jnp.int32),
            pltpu.SMEM((CHUNKS * lay.places,), jnp.int32),
        ],
        compiler_params=pltpu.CompilerParams(vmem_limit_bytes=16 << 20),
        name="prepare",
    )(partner, counts, where, in_blocks)

    def outward(sent):
        return lax.all_to_all(
            sent.reshape(lay.reach, lay.slots * BLOCK, width), "reach", 0, 0, tiled=True
        ).reshape(lay.places, BLOCK, width)

    def homeward(home):
        return lax.all_to_all(
            home.reshape(lay.reach * CORES, lay.slots * BLOCK, half),
            ("reach", "head"),
            0,
            0,
            tiled=True,
        ).reshape(lay.reach * CORES * lay.slots, BLOCK, half)

    received_a = outward(sent_a)
    prior_inputs = lax.ppermute(prior, "day", [(d, d + 1) for d in range(day_total - 1)])
    received_b = outward(sent_b)
    shared = (prior_inputs, pack, pack_other)
    first = attend(lay, 0, tab, in_blocks, up_blocks, received_a, *shared, None)
    home_a = homeward(first[4])
    keep, swap, same, cross, home, grad_mine, grad_other = attend(
        lay, 1, tab, in_blocks, up_blocks, received_b, *shared, first
    )
    home_a, home, grad_other = lax.optimization_barrier((home_a, home, grad_other))
    keep, swap, same, cross = (
        term.reshape(lay.items, BLOCK, half) for term in (keep, swap, same, cross)
    )
    home_b = homeward(home)
    grad_swapped = exchanged(grad_other, "head", 1)
    swapped = exchanged(swap, "head", 1)
    same_came = lax.ppermute(same, "day", [(d + 1, d) for d in range(day_total - 1)])
    cross_came = lax.ppermute(
        cross,
        ("day", "head"),
        [
            ((d + 1) * CORES + c, d * CORES + 1 - c)
            for d in range(day_total - 1)
            for c in range(CORES)
        ],
    )
    upper, lower, (swapped, same_came, cross_came) = sum_gradients(
        grad_mine + grad_swapped, (swapped, same_came, cross_came)
    )

    back_blocks = pl.pallas_call(
        lambda *refs: gather_kernel(lay, *refs),
        out_shape=jax.ShapeDtypeStruct((blocks_dev, BLOCK, half), BF16),
        in_specs=[smem] + [in_vmem] * 6,
        out_specs=in_vmem,
        compiler_params=pltpu.CompilerParams(vmem_limit_bytes=16 << 20),
        name="assemble",
    )(tab, keep, swapped, same_came, cross_came, home_a, home_b)
    return (
        back_blocks.reshape(1, rows_dev, half),
        lower[:GROUP].T,
        upper[:, :GROUP],
        upper[:, GROUP:],
        lower[GROUP:],
    )


def solution(mesh):
    placed = (
        P(("groups", "day"), "reach", None),
        P(("groups", "day"), "reach", None),
        P(None, "head"),
        P(None, "head"),
        P(None, "head"),
        P("head", None),
        P("groups"),
        P("groups"),
    )
    return jax.shard_map(
        on_device,
        mesh=mesh,
        in_specs=placed,
        out_specs=(
            P(("groups", "day"), "reach", "head"),
            P("groups", "head"),
            P("groups", "head"),
            P("groups", "head"),
            P(("groups", "head"), None),
        ),
        check_vma=False,
    )
```

```python
import jax
import jax.numpy as jnp
from jax import lax
from jax.experimental import pallas as pl
from jax.experimental.pallas import tpu as pltpu
from jax.sharding import PartitionSpec as P

HD = 32
BLOCK = 128
GROUP = 128
CORES = 2
CHUNKS = 2
WORKERS = CORES * CHUNKS
F32 = jnp.float32
BF16 = jnp.bfloat16
LOG2E = 1.4426950408889634


class Layout:
    def __init__(self, blocks_dev, reach_total):
        self.blocks = blocks_dev
        self.items = blocks_dev // CORES
        self.chunk_items = self.items // CHUNKS
        self.reach = reach_total
        self.slots = max(1, 2 * blocks_dev // reach_total // WORKERS)
        self.places = reach_total * self.slots
        self.block_of = 0
        self.recv_of = self.items
        self.count_own = 2 * self.items
        self.count_partner = 3 * self.items
        self.owner_of = 4 * self.items
        self.item_of = self.owner_of + blocks_dev
        self.home_of = self.item_of + blocks_dev
        self.chunk_of = self.home_of + blocks_dev
        self.core = self.chunk_of + blocks_dev
        self.later_day = self.core + 1
        self.size = -(-(self.core + 2) // 128) * 128


def prepare_kernel(lay, partner, counts, where, inputs, sent_a, sent_b, prior, tab, start, used, picks):
    bd, slots = lay.blocks, lay.slots
    reach_pos, core = where[0], where[1]

    def clear(index, carry):
        used[index] = 0
        start[index] = 0
        return carry

    lax.fori_loop(0, lay.reach, clear, 0, unroll=True)

    def count(index, carry):
        source = lax.div(partner[reach_pos * bd + index], bd)
        start[source] = start[source] + 1
        return carry

    lax.fori_loop(0, bd, count, 0)

    def prefix(index, total):
        here = start[index]
        start[index] = total
        return total + here

    lax.fori_loop(0, lay.reach, prefix, jnp.int32(0))

    def assign(index, carry):
        wanted = partner[reach_pos * bd + index]
        source = lax.div(wanted, bd)
        rank = used[source]
        used[source] = rank + 1
        place = start[source] + rank
        owner = lax.rem(place, CORES)
        chunk = lax.rem(lax.div(place, CORES), CHUNKS)
        item = chunk * lay.chunk_items + lax.div(place, WORKERS)
        slot = jnp.minimum(lax.div(rank, WORKERS), slots - 1)
        tab[lay.owner_of + index] = owner
        tab[lay.item_of + index] = lax.div(place, WORKERS) * CHUNKS + chunk

        @pl.when(owner == core)
        def _():
            tab[lay.block_of + item] = index
            tab[lay.recv_of + item] = source * slots + slot
            tab[lay.count_own + item] = counts[reach_pos * bd + index]
            tab[lay.count_partner + item] = counts[wanted]

        return carry

    lax.fori_loop(0, bd, assign, 0)
    tab[lay.core] = core
    tab[lay.later_day] = where[2]

    def clear_picks(index, carry):
        picks[index] = 0
        return carry

    lax.fori_loop(0, CHUNKS * lay.places, clear_picks, 0)

    def one_reach(peer, carry):
        def before(index, total):
            source = lax.div(partner[peer * bd + index], bd)
            return total + jnp.where(source < reach_pos, 1, 0)

        base = lax.fori_loop(0, bd, before, jnp.int32(0), unroll=True)

        def serve(index, rank):
            wanted = partner[peer * bd + index]
            hit = lax.div(wanted, bd) == reach_pos

            @pl.when(hit)
            def _():
                place = base + rank
                owner = lax.rem(place, CORES)
                chunk = lax.rem(lax.div(place, CORES), CHUNKS)
                slot = jnp.minimum(lax.div(rank, WORKERS), slots - 1)
                local = lax.rem(wanted, bd)
                tab[lay.home_of + local] = (peer * CORES + owner) * slots + slot
                tab[lay.chunk_of + local] = chunk

                @pl.when(owner == core)
                def _():
                    picks[chunk * lay.places + peer * slots + slot] = local

            return rank + jnp.where(hit, 1, 0)

        lax.fori_loop(0, bd, serve, jnp.int32(0))
        return carry

    lax.fori_loop(0, lay.reach, one_reach, 0)

    def pick_a(place, carry):
        sent_a[place] = inputs[picks[place]]
        return carry

    def pick_b(place, carry):
        sent_b[place] = inputs[picks[lay.places + place]]
        return carry

    def pick_prior(item, carry):
        prior[item] = inputs[tab[lay.block_of + item]]
        return carry

    lax.fori_loop(0, lay.places, pick_a, 0)
    lax.fori_loop(0, lay.places, pick_b, 0)
    lax.fori_loop(0, lay.items, pick_prior, 0)


def dot(left, right):
    return lax.dot_general(left, right, (((1,), (0,)), ((), ())), preferred_element_type=F32)


def dot_t(left, right):
    return lax.dot_general(left, right, (((1,), (1,)), ((), ())), preferred_element_type=F32)


def attention_kernel(
    lay,
    chunk,
    tab,
    own_ref,
    up_ref,
    partner_ref,
    prior_ref,
    mine_ref,
    other_ref,
    *refs,
):
    if chunk:
        start_mine_ref, start_other_ref = refs[0], refs[1]
        carried_refs = refs[2:6]
        refs = refs[6:]
    keep_ref, swap_ref, same_ref, cross_ref, home_ref, grad_mine_ref, grad_other_ref = refs
    step = pl.program_id(0)
    item = step + chunk * lay.chunk_items
    core = tab[lay.core]
    factor = HD ** (-0.5)
    own, up = own_ref[0], up_ref[0]
    key_inputs = jnp.concatenate([own, partner_ref[0], prior_ref[0]], axis=0)
    width = own.shape[1]

    @pl.when(step == 0)
    def _():
        if chunk:
            grad_mine_ref[...] = start_mine_ref[...]
            grad_other_ref[...] = start_other_ref[...]
        else:
            grad_mine_ref[...] = jnp.zeros_like(grad_mine_ref)
            grad_other_ref[...] = jnp.zeros_like(grad_other_ref)

    def eye(size):
        rows = lax.broadcasted_iota(jnp.int32, (size, size), 0)
        cols = lax.broadcasted_iota(jnp.int32, (size, size), 1)
        return jnp.where(rows == cols, 1.0, 0.0).astype(BF16)

    query_t = jnp.concatenate([mine_ref[256:384, :], other_ref[256:384, :]], axis=0)
    output_w = jnp.concatenate([mine_ref[384:512, :], other_ref[384:512, :]], axis=0)
    queries = dot_t(own, query_t)
    back_out = dot_t(up, output_w)
    key_inputs_t = dot_t(eye(width), key_inputs).astype(BF16)

    count_own = tab[lay.count_own + item]
    count_partner = tab[lay.count_partner + item]
    count_prior = count_own * tab[lay.later_day]
    rows = lax.broadcasted_iota(jnp.int32, (BLOCK, 2 * BLOCK), 0)
    valid = jnp.concatenate([rows < count_own, rows < count_partner, rows < count_prior], axis=0)
    lane_head = lax.broadcasted_iota(jnp.int32, (BLOCK, GROUP), 1) // HD

    back_inputs = None
    outputs_t, back_query_t = [], []
    for group, (weights_ref, grad_ref) in enumerate(
        ((mine_ref, grad_mine_ref), (other_ref, grad_other_ref))
    ):
        kv_t = weights_ref[0:256, :]
        kv = dot_t(key_inputs, kv_t).astype(BF16)
        kv_cols = dot_t(kv_t, key_inputs).astype(BF16)
        keys, values = kv[:, :GROUP], kv[:, GROUP:]
        group_queries = queries[:, group * GROUP : (group + 1) * GROUP]
        group_back = back_out[:, group * GROUP : (group + 1) * GROUP]
        back_keys = back_values = None
        for pair in range(GROUP // HD // 2):
            heads = (2 * pair, 2 * pair + 1)
            query_pair = jnp.concatenate(
                [jnp.where(lane_head == h, group_queries, 0.0) for h in heads], axis=0
            ).astype(BF16)
            back_pair = jnp.concatenate(
                [jnp.where(lane_head == h, group_back, 0.0) for h in heads], axis=0
            ).astype(BF16)
            logits = jnp.where(valid, dot_t(keys, query_pair), -1e30)
            highest = jnp.max(logits, axis=0, keepdims=True)
            raised = jnp.exp2((logits - highest) * (factor * LOG2E))
            scale = 1.0 / jnp.sum(raised, axis=0, keepdims=True)
            weights = raised * scale
            weights_low = weights.astype(BF16)
            back_weights = dot_t(values, back_pair)
            center = jnp.sum(weights * back_weights, axis=0, keepdims=True)
            back_logits = (weights * ((back_weights - center) * factor)).astype(BF16)
            pair_values = dot(weights_low, back_pair)
            pair_keys = dot(back_logits, query_pair)
            back_values = pair_values if back_values is None else back_values + pair_values
            back_keys = pair_keys if back_keys is None else back_keys + pair_keys
            first = 2 * pair * HD
            out_t = dot(kv_cols[GROUP + first : GROUP + first + 2 * HD, :], weights_low)
            query_grad_t = dot(kv_cols[first : first + 2 * HD, :], back_logits)
            for h in range(2):
                lanes = slice(h * BLOCK, (h + 1) * BLOCK)
                outputs_t.append(out_t[h * HD : (h + 1) * HD, lanes])
                back_query_t.append(query_grad_t[h * HD : (h + 1) * HD, lanes])
        back_kv = jnp.concatenate([back_keys, back_values], axis=1).astype(BF16)
        term = dot(back_kv, kv_t)
        back_inputs = term if back_inputs is None else back_inputs + term
        grad_ref[0:256, :] += dot(key_inputs_t, back_kv)

    outputs_t = jnp.concatenate(outputs_t, axis=0).astype(BF16)
    back_query_t = jnp.concatenate(back_query_t, axis=0).astype(BF16)
    query_grad = dot(back_query_t, own)
    output_grad = dot(outputs_t, up)
    grad_mine_ref[256:384, :] += query_grad[:GROUP]
    grad_other_ref[256:384, :] += query_grad[GROUP:]
    grad_mine_ref[384:512, :] += output_grad[:GROUP]
    grad_other_ref[384:512, :] += output_grad[GROUP:]
    back_query = dot_t(eye(BLOCK), back_query_t).astype(BF16)
    own_term = back_inputs[:BLOCK] + dot(back_query, query_t)
    partner_term = back_inputs[BLOCK : 2 * BLOCK].astype(BF16)
    prior_term = back_inputs[2 * BLOCK :]
    half = width // 2
    first_core = core == 0
    terms = (
        jnp.where(first_core, own_term[:, :half], own_term[:, half:]),
        jnp.where(first_core, own_term[:, half:], own_term[:, :half]),
        jnp.where(first_core, prior_term[:, :half], prior_term[:, half:]).astype(BF16),
        jnp.where(first_core, prior_term[:, half:], prior_term[:, :half]).astype(BF16),
    )
    for place, (term_ref, term) in enumerate(zip((keep_ref, swap_ref, same_ref, cross_ref), terms)):
        if chunk:
            term_ref[0, 0] = carried_refs[place][0]
            term_ref[0, 1] = term
        else:
            term_ref[0] = term
    home_ref[0, 0, 0] = partner_term[:, :half]
    home_ref[0, 1, 0] = partner_term[:, half:]


def gather_kernel(lay, tab, keep, swapped, same, cross, home_a, home_b, out):
    core = tab[lay.core]

    def one(block, carry):
        item = tab[lay.item_of + block]
        mine = tab[lay.owner_of + block] == core
        place = tab[lay.home_of + block]
        first = tab[lay.chunk_of + block] == 0
        total = jnp.where(mine, keep[item], swapped[item])
        total += jnp.where(mine, same[item].astype(F32), cross[item].astype(F32))
        total += jnp.where(first, home_a[place].astype(F32), home_b[place].astype(F32))
        out[block] = total.astype(BF16)
        return carry

    lax.fori_loop(0, lay.blocks, one, 0)


def attend(lay, chunk, tab, in_blocks, up_blocks, received, prior_inputs, pack, pack_other, carried):
    width = in_blocks.shape[-1]
    half = width // 2
    offset = chunk * lay.chunk_items

    def at_item(step, tab):
        return (offset + step, 0, 0)

    def at_block(step, tab):
        return (tab[lay.block_of + offset + step], 0, 0)

    def at_recv(step, tab):
        return (tab[lay.recv_of + offset + step], 0, 0)

    def at_home(step, tab):
        place = tab[lay.recv_of + offset + step]
        return (lax.div(place, lay.slots), 0, lax.rem(place, lay.slots), 0, 0)

    def fixed(step, tab):
        return (0, 0)

    full_block = (1, BLOCK, width)
    half_block = (1, BLOCK, half)
    weights_block = (4 * GROUP, width)
    in_specs = [
        pl.BlockSpec(full_block, at_block),
        pl.BlockSpec(full_block, at_block),
        pl.BlockSpec(full_block, at_recv),
        pl.BlockSpec(full_block, at_item),
        pl.BlockSpec(weights_block, fixed),
        pl.BlockSpec(weights_block, fixed),
    ]
    operands = [in_blocks, up_blocks, received, prior_inputs, pack, pack_other]
    term_shape = (lay.chunk_items, BLOCK, half)
    term_spec = pl.BlockSpec(half_block, lambda step, tab: (step, 0, 0))
    if chunk:
        in_specs += [pl.BlockSpec(weights_block, fixed)] * 2 + [term_spec] * 4
        operands += [carried[5], carried[6]] + list(carried[:4])
        term_shape = (lay.chunk_items, CHUNKS, BLOCK, half)
        term_spec = pl.BlockSpec((1, CHUNKS, BLOCK, half), lambda step, tab: (step, 0, 0, 0))
    pieces = lay.chunk_items
    flops = 2 * pieces * (23 * BLOCK * width * width + 24 * BLOCK * 3 * BLOCK * 512)
    return pl.pallas_call(
        lambda *refs: attention_kernel(lay, chunk, *refs),
        grid_spec=pltpu.PrefetchScalarGridSpec(
            num_scalar_prefetch=1,
            grid=(pieces,),
            in_specs=in_specs,
            out_specs=(
                *[term_spec] * 4,
                pl.BlockSpec((1, CORES, 1, BLOCK, half), at_home),
                pl.BlockSpec(weights_block, fixed),
                pl.BlockSpec(weights_block, fixed),
            ),
        ),
        out_shape=(
            pltpu.HBM(term_shape, F32),
            pltpu.HBM(term_shape, F32),
            pltpu.HBM(term_shape, BF16),
            pltpu.HBM(term_shape, BF16),
            pltpu.HBM((lay.reach, CORES, lay.slots, BLOCK, half), BF16),
            pltpu.HBM(weights_block, F32),
            pltpu.HBM(weights_block, F32),
        ),
        compiler_params=pltpu.CompilerParams(vmem_limit_bytes=32 << 20),
        cost_estimate=pl.CostEstimate(
            flops=flops, bytes_accessed=5 << 20, transcendentals=pieces * 8 * BLOCK * 3 * BLOCK
        ),
        name=f"attention_{chunk}",
    )(
        tab,
        *[
            value
            if place == 2
            else pltpu.with_memory_space_constraint(value, pltpu.HBM)
            for place, value in enumerate(operands)
        ],
    )


def exchanged(value, axis, bit):
    count = lax.axis_size(axis)
    return lax.ppermute(value, axis, [(place, place ^ bit) for place in range(count)])


def summed_over(value, axis, bit):
    low = value.astype(BF16)
    return low.astype(F32) + exchanged(low, axis, bit).astype(F32)


def sum_gradients(total, early, late):
    half = total.shape[0] // 2
    first = lax.rem(lax.axis_index("day"), 2) == 0
    kept = jnp.where(first, total[:half], total[half:])
    given = jnp.where(first, total[half:], total[:half])
    part = kept + exchanged(given, "day", 1)
    bit = 2
    while bit < lax.axis_size("day"):
        part = summed_over(part, "day", bit)
        bit *= 2
    part, *early = lax.optimization_barrier((part, *early))
    bit = 1
    while bit < lax.axis_size("reach"):
        part = summed_over(part, "reach", bit)
        if bit == 1:
            part, *late = lax.optimization_barrier((part, *late))
        bit *= 2
    return part, exchanged(part, "day", 1), (*early, *late)


def split_kernel(where, part, other, query_out, key_out, value_out, output_out):
    first = lax.rem(where[3], 2) == 0
    upper = jnp.where(first, part[...], other[...])
    lower = jnp.where(first, other[...], part[...])
    key_out[...] = upper[:, :GROUP]
    value_out[...] = upper[:, GROUP:]
    query_out[...] = lower[:GROUP].T
    output_out[...] = lower[GROUP:]


def on_device(
    inputs, upstream, query_weight, key_weight, value_weight, output_weight, partner, counts
):
    days_dev, rows_dev, width = inputs.shape
    assert days_dev == 1 and width == 2 * GROUP
    blocks_dev = rows_dev // BLOCK
    reach_total = lax.axis_size("reach")
    day_total = lax.axis_size("day")
    assert lax.axis_size("head") == CORES
    lay = Layout(blocks_dev, reach_total)
    half = width // 2
    in_blocks = inputs.reshape(blocks_dev, BLOCK, width)
    up_blocks = upstream.reshape(blocks_dev, BLOCK, width)
    where = jnp.stack(
        [
            lax.axis_index("reach"),
            lax.axis_index("head"),
            (lax.axis_index("day") > 0).astype(jnp.int32),
            lax.axis_index("day"),
        ]
    )
    pack = jnp.concatenate([key_weight.T, value_weight.T, query_weight.T, output_weight], axis=0)
    pack_other = exchanged(pack, "head", 1)

    smem = pl.BlockSpec(memory_space=pltpu.SMEM)
    in_vmem = pl.BlockSpec(memory_space=pltpu.VMEM)
    sent_shape = jax.ShapeDtypeStruct((lay.places, BLOCK, width), BF16)
    sent_a, sent_b, prior, tab = pl.pallas_call(
        lambda *refs: prepare_kernel(lay, *refs),
        out_shape=(
            sent_shape,
            sent_shape,
            jax.ShapeDtypeStruct((lay.items, BLOCK, width), BF16),
            jax.ShapeDtypeStruct((lay.size,), jnp.int32),
        ),
        in_specs=[smem, smem, smem, in_vmem],
        out_specs=(in_vmem, in_vmem, in_vmem, smem),
        scratch_shapes=[
            pltpu.SMEM((lay.reach,), jnp.int32),
            pltpu.SMEM((lay.reach,), jnp.int32),
            pltpu.SMEM((CHUNKS * lay.places,), jnp.int32),
        ],
        compiler_params=pltpu.CompilerParams(vmem_limit_bytes=16 << 20),
        name="prepare",
    )(partner, counts, where, in_blocks)

    def outward(sent):
        return lax.all_to_all(
            sent.reshape(lay.reach, lay.slots * BLOCK, width), "reach", 0, 0, tiled=True
        ).reshape(lay.places, BLOCK, width)

    def homeward(home):
        return lax.all_to_all(
            home.reshape(lay.reach * CORES, lay.slots * BLOCK, half),
            ("reach", "head"),
            0,
            0,
            tiled=True,
        ).reshape(lay.reach * CORES * lay.slots, BLOCK, half)

    received_a = outward(sent_a)
    prior_inputs = lax.ppermute(prior, "day", [(d, d + 1) for d in range(day_total - 1)])
    received_b = outward(sent_b)
    shared = (prior_inputs, pack, pack_other)
    first = attend(lay, 0, tab, in_blocks, up_blocks, received_a, *shared, None)
    home_a = homeward(first[4])
    keep, swap, same, cross, home, grad_mine, grad_other = attend(
        lay, 1, tab, in_blocks, up_blocks, received_b, *shared, first
    )
    home_a, home, grad_other = lax.optimization_barrier((home_a, home, grad_other))
    keep, swap, same, cross = (
        term.reshape(lay.items, BLOCK, half) for term in (keep, swap, same, cross)
    )
    home_b = homeward(home)
    grad_swapped = exchanged(grad_other, "head", 1)
    swapped = exchanged(swap, "head", 1)
    same_came = lax.ppermute(same, "day", [(d + 1, d) for d in range(day_total - 1)])
    cross_came = lax.ppermute(
        cross,
        ("day", "head"),
        [
            ((d + 1) * CORES + c, d * CORES + 1 - c)
            for d in range(day_total - 1)
            for c in range(CORES)
        ],
    )
    part, other, (home_b, swapped, same_came, cross_came) = sum_gradients(
        grad_mine + grad_swapped, (home_b, swapped, same_came), (cross_came,)
    )
    weight_grads = pl.pallas_call(
        split_kernel,
        out_shape=(
            jax.ShapeDtypeStruct((width, half), F32),
            jax.ShapeDtypeStruct((width, half), F32),
            jax.ShapeDtypeStruct((width, half), F32),
            jax.ShapeDtypeStruct((half, width), F32),
        ),
        in_specs=[smem] + [in_vmem] * 2,
        out_specs=[in_vmem] * 4,
        name="split",
    )(where, part, other)

    back_blocks = pl.pallas_call(
        lambda *refs: gather_kernel(lay, *refs),
        out_shape=jax.ShapeDtypeStruct((blocks_dev, BLOCK, half), BF16),
        in_specs=[smem] + [in_vmem] * 6,
        out_specs=in_vmem,
        compiler_params=pltpu.CompilerParams(vmem_limit_bytes=16 << 20),
        name="assemble",
    )(tab, keep, swapped, same_came, cross_came, home_a, home_b)
    return (back_blocks.reshape(1, rows_dev, half), *weight_grads)


def solution(mesh):
    placed = (
        P(("groups", "day"), "reach", None),
        P(("groups", "day"), "reach", None),
        P(None, "head"),
        P(None, "head"),
        P(None, "head"),
        P("head", None),
        P("groups"),
        P("groups"),
    )
    return jax.shard_map(
        on_device,
        mesh=mesh,
        in_specs=placed,
        out_specs=(
            P(("groups", "day"), "reach", "head"),
            P("groups", "head"),
            P("groups", "head"),
            P("groups", "head"),
            P(("groups", "head"), None),
        ),
        check_vma=False,
    )
```

```python
import jax
import jax.numpy as jnp
from jax import lax
from jax.experimental import pallas as pl
from jax.experimental.pallas import tpu as pltpu
from jax.sharding import PartitionSpec as P

HD = 32
BLOCK = 128
GROUP = 128
CORES = 2
CHUNKS = 2
WORKERS = CORES * CHUNKS
F32 = jnp.float32
BF16 = jnp.bfloat16
LOG2E = 1.4426950408889634


class Layout:
    def __init__(self, blocks_dev, reach_total):
        self.blocks = blocks_dev
        self.items = blocks_dev // CORES
        self.chunk_items = self.items // CHUNKS
        self.reach = reach_total
        self.slots = max(1, 2 * blocks_dev // reach_total // WORKERS)
        self.places = reach_total * self.slots
        self.cyclic = reach_total <= 4
        self.block_of = 0
        self.recv_of = self.items
        self.count_own = 2 * self.items
        self.count_partner = 3 * self.items
        self.owner_of = 4 * self.items
        self.item_of = self.owner_of + blocks_dev
        self.home_of = self.item_of + blocks_dev
        self.chunk_of = self.home_of + blocks_dev
        self.asker_of = self.chunk_of + blocks_dev
        self.core = self.asker_of + blocks_dev
        self.later_day = self.core + 1
        self.size = -(-(self.core + 2) // 128) * 128


    def offset(self, high, low):
        return lax.rem(high - low + self.reach, self.reach)


def prepare_kernel(lay, partner, counts, where, inputs, sent_a, sent_b, prior, tab, start, used, picks):
    bd, slots = lay.blocks, lay.slots
    reach_pos, core = where[0], where[1]

    def clear(index, carry):
        used[index] = 0
        start[index] = 0
        return carry

    lax.fori_loop(0, lay.reach, clear, 0, unroll=True)

    def count(index, carry):
        source = lax.div(partner[reach_pos * bd + index], bd)
        start[source] = start[source] + 1
        return carry

    lax.fori_loop(0, bd, count, 0)

    def prefix(index, total):
        here = start[index]
        start[index] = total
        return total + here

    lax.fori_loop(0, lay.reach, prefix, jnp.int32(0))

    def assign(index, carry):
        wanted = partner[reach_pos * bd + index]
        source = lax.div(wanted, bd)
        rank = used[source]
        used[source] = rank + 1
        place = start[source] + rank
        owner = lax.rem(place, CORES)
        chunk = lax.rem(lax.div(place, CORES), CHUNKS)
        item = chunk * lay.chunk_items + lax.div(place, WORKERS)
        slot = jnp.minimum(lax.div(rank, WORKERS), slots - 1)
        tab[lay.owner_of + index] = owner
        tab[lay.item_of + index] = item

        @pl.when(owner == core)
        def _():
            tab[lay.block_of + item] = index
            peer = lay.offset(reach_pos, source) if lay.cyclic else source
            tab[lay.recv_of + item] = peer * slots + slot
            tab[lay.count_own + item] = counts[reach_pos * bd + index]
            tab[lay.count_partner + item] = counts[wanted]

        return carry

    lax.fori_loop(0, bd, assign, 0)
    tab[lay.core] = core
    tab[lay.later_day] = where[2]

    def clear_picks(index, carry):
        picks[index] = 0
        return carry

    lax.fori_loop(0, CHUNKS * lay.places, clear_picks, 0)

    def one_reach(peer, carry):
        def before(index, total):
            source = lax.div(partner[peer * bd + index], bd)
            return total + jnp.where(source < reach_pos, 1, 0)

        base = lax.fori_loop(0, bd, before, jnp.int32(0), unroll=True)
        target = lay.offset(peer, reach_pos) if lay.cyclic else peer

        def serve(index, rank):
            wanted = partner[peer * bd + index]
            hit = lax.div(wanted, bd) == reach_pos

            @pl.when(hit)
            def _():
                place = base + rank
                owner = lax.rem(place, CORES)
                chunk = lax.rem(lax.div(place, CORES), CHUNKS)
                slot = jnp.minimum(lax.div(rank, WORKERS), slots - 1)
                local = lax.rem(wanted, bd)
                tab[lay.home_of + local] = target * slots + slot
                tab[lay.chunk_of + local] = chunk
                tab[lay.asker_of + local] = owner

                @pl.when(owner == core)
                def _():
                    picks[chunk * lay.places + target * slots + slot] = local

            return rank + jnp.where(hit, 1, 0)

        lax.fori_loop(0, bd, serve, jnp.int32(0))
        return carry

    lax.fori_loop(0, lay.reach, one_reach, 0)

    def pick_a(place, carry):
        sent_a[place] = inputs[picks[place]]
        return carry

    def pick_b(place, carry):
        sent_b[place] = inputs[picks[lay.places + place]]
        return carry

    def pick_prior(item, carry):
        prior[item] = inputs[tab[lay.block_of + item]]
        return carry

    lax.fori_loop(0, lay.places, pick_a, 0)
    lax.fori_loop(0, lay.places, pick_b, 0)
    lax.fori_loop(0, lay.items, pick_prior, 0)


def dot(left, right):
    return lax.dot_general(left, right, (((1,), (0,)), ((), ())), preferred_element_type=F32)


def dot_t(left, right):
    return lax.dot_general(left, right, (((1,), (1,)), ((), ())), preferred_element_type=F32)


def attention_kernel(
    lay,
    chunk,
    tab,
    own_ref,
    up_ref,
    partner_ref,
    prior_ref,
    mine_ref,
    other_ref,
    *refs,
):
    if chunk:
        start_mine_ref, start_other_ref = refs[:2]
        refs = refs[2:]
    own_out_ref, day_ref, home_ref, grad_mine_ref, grad_other_ref = refs
    step = pl.program_id(0)
    item = step + chunk * lay.chunk_items
    factor = HD ** (-0.5)
    own, up = own_ref[0], up_ref[0]
    key_inputs = jnp.concatenate([own, partner_ref[0], prior_ref[0]], axis=0)
    width = own.shape[1]

    @pl.when(step == 0)
    def _():
        if chunk:
            grad_mine_ref[...] = start_mine_ref[...]
            grad_other_ref[...] = start_other_ref[...]
        else:
            grad_mine_ref[...] = jnp.zeros_like(grad_mine_ref)
            grad_other_ref[...] = jnp.zeros_like(grad_other_ref)

    def eye(size):
        rows = lax.broadcasted_iota(jnp.int32, (size, size), 0)
        cols = lax.broadcasted_iota(jnp.int32, (size, size), 1)
        return jnp.where(rows == cols, 1.0, 0.0).astype(BF16)

    query_t = jnp.concatenate([mine_ref[256:384, :], other_ref[256:384, :]], axis=0)
    output_w = jnp.concatenate([mine_ref[384:512, :], other_ref[384:512, :]], axis=0)
    queries = dot_t(own, query_t)
    back_out = dot_t(up, output_w)
    key_inputs_t = dot_t(eye(width), key_inputs).astype(BF16)

    count_own = tab[lay.count_own + item]
    count_partner = tab[lay.count_partner + item]
    count_prior = count_own * tab[lay.later_day]
    rows = lax.broadcasted_iota(jnp.int32, (BLOCK, 2 * BLOCK), 0)
    valid = jnp.concatenate([rows < count_own, rows < count_partner, rows < count_prior], axis=0)
    lane_head = lax.broadcasted_iota(jnp.int32, (BLOCK, GROUP), 1) // HD

    back_inputs = None
    outputs_t, back_query_t = [], []
    for group, (weights_ref, grad_ref) in enumerate(
        ((mine_ref, grad_mine_ref), (other_ref, grad_other_ref))
    ):
        kv_t = weights_ref[0:256, :]
        kv = dot_t(key_inputs, kv_t).astype(BF16)
        kv_cols = dot_t(kv_t, key_inputs).astype(BF16)
        keys, values = kv[:, :GROUP], kv[:, GROUP:]
        group_queries = queries[:, group * GROUP : (group + 1) * GROUP]
        group_back = back_out[:, group * GROUP : (group + 1) * GROUP]
        back_keys = back_values = None
        for pair in range(GROUP // HD // 2):
            heads = (2 * pair, 2 * pair + 1)
            query_pair = jnp.concatenate(
                [jnp.where(lane_head == h, group_queries, 0.0) for h in heads], axis=0
            ).astype(BF16)
            back_pair = jnp.concatenate(
                [jnp.where(lane_head == h, group_back, 0.0) for h in heads], axis=0
            ).astype(BF16)
            logits = jnp.where(valid, dot_t(keys, query_pair), -1e30)
            highest = jnp.max(logits, axis=0, keepdims=True)
            raised = jnp.exp2((logits - highest) * (factor * LOG2E))
            scale = 1.0 / jnp.sum(raised, axis=0, keepdims=True)
            weights = raised * scale
            weights_low = weights.astype(BF16)
            back_weights = dot_t(values, back_pair)
            center = jnp.sum(weights * back_weights, axis=0, keepdims=True)
            back_logits = (weights * ((back_weights - center) * factor)).astype(BF16)
            pair_values = dot(weights_low, back_pair)
            pair_keys = dot(back_logits, query_pair)
            back_values = pair_values if back_values is None else back_values + pair_values
            back_keys = pair_keys if back_keys is None else back_keys + pair_keys
            first = 2 * pair * HD
            out_t = dot(kv_cols[GROUP + first : GROUP + first + 2 * HD, :], weights_low)
            query_grad_t = dot(kv_cols[first : first + 2 * HD, :], back_logits)
            for h in range(2):
                lanes = slice(h * BLOCK, (h + 1) * BLOCK)
                outputs_t.append(out_t[h * HD : (h + 1) * HD, lanes])
                back_query_t.append(query_grad_t[h * HD : (h + 1) * HD, lanes])
        back_kv = jnp.concatenate([back_keys, back_values], axis=1).astype(BF16)
        term = dot(back_kv, kv_t)
        back_inputs = term if back_inputs is None else back_inputs + term
        grad_ref[0:256, :] += dot(key_inputs_t, back_kv)

    outputs_t = jnp.concatenate(outputs_t, axis=0).astype(BF16)
    back_query_t = jnp.concatenate(back_query_t, axis=0).astype(BF16)
    query_grad = dot(back_query_t, own)
    output_grad = dot(outputs_t, up)
    grad_mine_ref[256:384, :] += query_grad[:GROUP]
    grad_other_ref[256:384, :] += query_grad[GROUP:]
    grad_mine_ref[384:512, :] += output_grad[:GROUP]
    grad_other_ref[384:512, :] += output_grad[GROUP:]
    back_query = dot_t(eye(BLOCK), back_query_t).astype(BF16)
    own_out_ref[0] = back_inputs[:BLOCK] + dot(back_query, query_t)
    home_ref[0] = back_inputs[BLOCK : 2 * BLOCK].astype(BF16)
    day_ref[0] = back_inputs[2 * BLOCK :].astype(BF16)


def fold_kernel(lay, tab, own_a, own_b, day_a, day_b, home_a, home_b, keep, give):
    core = tab[lay.core]
    half = keep.shape[2]

    def one(block, carry):
        item = tab[lay.item_of + block]
        mine = tab[lay.owner_of + block] == core
        place = tab[lay.home_of + block]
        asked = tab[lay.asker_of + block] == core
        early = tab[lay.chunk_of + block] == 0
        in_a = item < lay.chunk_items
        item_a = jnp.minimum(item, lay.chunk_items - 1)
        item_b = jnp.maximum(item - lay.chunk_items, 0)
        own = jnp.where(in_a, own_a[item_a], own_b[item_b])
        own += jnp.where(in_a, day_a[item_a].astype(F32), day_b[item_b].astype(F32))
        home = jnp.where(early, home_a[place].astype(F32), home_b[place].astype(F32))
        total = jnp.where(mine, own, 0.0) + jnp.where(asked, home, 0.0)
        low, high = total[:, :half], total[:, half:]
        keep[block] = jnp.where(core == 0, low, high)
        give[block] = jnp.where(core == 0, high, low)
        return carry

    lax.fori_loop(0, lay.blocks, one, 0)


def add_kernel(kept, got, out):
    out[...] = (kept[...] + got[...]).astype(BF16)


def attend(lay, chunk, tab, in_blocks, up_blocks, received, prior_inputs, pack, pack_other, carried):
    width = in_blocks.shape[-1]
    offset = chunk * lay.chunk_items

    def at_item(step, tab):
        return (offset + step, 0, 0)

    def at_block(step, tab):
        return (tab[lay.block_of + offset + step], 0, 0)

    def at_recv(step, tab):
        return (tab[lay.recv_of + offset + step], 0, 0)

    def at_step(step, tab):
        return (step, 0, 0)

    def fixed(step, tab):
        return (0, 0)

    full_block = (1, BLOCK, width)
    weights_block = (4 * GROUP, width)
    in_specs = [
        pl.BlockSpec(full_block, at_block),
        pl.BlockSpec(full_block, at_block),
        pl.BlockSpec(full_block, at_recv),
        pl.BlockSpec(full_block, at_item),
        pl.BlockSpec(weights_block, fixed),
        pl.BlockSpec(weights_block, fixed),
    ]
    operands = [in_blocks, up_blocks, received, prior_inputs, pack, pack_other]
    if chunk:
        in_specs += [pl.BlockSpec(weights_block, fixed)] * 2
        operands += carried
    pieces = lay.chunk_items
    flops = 2 * pieces * (23 * BLOCK * width * width + 24 * BLOCK * 3 * BLOCK * 512)
    return pl.pallas_call(
        lambda *refs: attention_kernel(lay, chunk, *refs),
        grid_spec=pltpu.PrefetchScalarGridSpec(
            num_scalar_prefetch=1,
            grid=(pieces,),
            in_specs=in_specs,
            out_specs=(
                pl.BlockSpec(full_block, at_step),
                pl.BlockSpec(full_block, at_step),
                pl.BlockSpec(full_block, at_recv),
                pl.BlockSpec(weights_block, fixed),
                pl.BlockSpec(weights_block, fixed),
            ),
        ),
        out_shape=(
            pltpu.HBM((pieces, BLOCK, width), F32),
            pltpu.HBM((pieces, BLOCK, width), BF16),
            pltpu.HBM((lay.places, BLOCK, width), BF16),
            pltpu.HBM(weights_block, F32),
            pltpu.HBM(weights_block, F32),
        ),
        compiler_params=pltpu.CompilerParams(vmem_limit_bytes=32 << 20),
        cost_estimate=pl.CostEstimate(
            flops=flops, bytes_accessed=5 << 20, transcendentals=pieces * 8 * BLOCK * 3 * BLOCK
        ),
        name=f"attention_{chunk}",
    )(
        tab,
        *[
            value
            if place == 2
            else pltpu.with_memory_space_constraint(value, pltpu.HBM)
            for place, value in enumerate(operands)
        ],
    )


def exchanged(value, axis, bit):
    count = lax.axis_size(axis)
    return lax.ppermute(value, axis, [(place, place ^ bit) for place in range(count)])


def summed_over(value, axis, bit):
    low = value.astype(BF16)
    return low.astype(F32) + exchanged(low, axis, bit).astype(F32)


def sum_gradients(total, settled):
    half = total.shape[0] // 2
    first = lax.rem(lax.axis_index("day"), 2) == 0
    kept = jnp.where(first, total[:half], total[half:])
    given = jnp.where(first, total[half:], total[:half])
    part = kept + exchanged(given, "day", 1)
    bit = 2
    while bit < lax.axis_size("day"):
        part = summed_over(part, "day", bit)
        bit *= 2
    part, *settled = lax.optimization_barrier((part, *settled))
    bit = 1
    while bit < lax.axis_size("reach"):
        part = summed_over(part, "reach", bit)
        bit *= 2
    return part, exchanged(part, "day", 1), settled


def split_kernel(where, part, other, query_out, key_out, value_out, output_out):
    first = lax.rem(where[3], 2) == 0
    upper = jnp.where(first, part[...], other[...])
    lower = jnp.where(first, other[...], part[...])
    key_out[...] = upper[:, :GROUP]
    value_out[...] = upper[:, GROUP:]
    query_out[...] = lower[:GROUP].T
    output_out[...] = lower[GROUP:]


def on_device(
    inputs, upstream, query_weight, key_weight, value_weight, output_weight, partner, counts
):
    days_dev, rows_dev, width = inputs.shape
    assert days_dev == 1 and width == 2 * GROUP
    blocks_dev = rows_dev // BLOCK
    reach_total = lax.axis_size("reach")
    day_total = lax.axis_size("day")
    assert lax.axis_size("head") == CORES
    lay = Layout(blocks_dev, reach_total)
    half = width // 2
    in_blocks = inputs.reshape(blocks_dev, BLOCK, width)
    up_blocks = upstream.reshape(blocks_dev, BLOCK, width)
    where = jnp.stack(
        [
            lax.axis_index("reach"),
            lax.axis_index("head"),
            (lax.axis_index("day") > 0).astype(jnp.int32),
            lax.axis_index("day"),
        ]
    )
    pack = jnp.concatenate([key_weight.T, value_weight.T, query_weight.T, output_weight], axis=0)
    pack_other = exchanged(pack, "head", 1)

    smem = pl.BlockSpec(memory_space=pltpu.SMEM)
    in_vmem = pl.BlockSpec(memory_space=pltpu.VMEM)
    sent_shape = jax.ShapeDtypeStruct((lay.places, BLOCK, width), BF16)
    sent_a, sent_b, prior, tab = pl.pallas_call(
        lambda *refs: prepare_kernel(lay, *refs),
        out_shape=(
            sent_shape,
            sent_shape,
            jax.ShapeDtypeStruct((lay.items, BLOCK, width), BF16),
            jax.ShapeDtypeStruct((lay.size,), jnp.int32),
        ),
        in_specs=[smem, smem, smem, in_vmem],
        out_specs=(in_vmem, in_vmem, in_vmem, smem),
        scratch_shapes=[
            pltpu.SMEM((lay.reach,), jnp.int32),
            pltpu.SMEM((lay.reach,), jnp.int32),
            pltpu.SMEM((CHUNKS * lay.places,), jnp.int32),
        ],
        compiler_params=pltpu.CompilerParams(vmem_limit_bytes=16 << 20),
        name="prepare",
    )(partner, counts, where, in_blocks)

    def ring(value, back):
        shape = value.shape
        if not lay.cyclic:
            value = value.reshape(lay.reach, lay.slots * BLOCK, width)
            return [lax.all_to_all(value, "reach", 0, 0, tiled=True).reshape(shape)]
        pieces = [value[: lay.slots]]
        for shift in range(1, lay.reach):
            step = -shift if back else shift
            pieces.append(
                lax.ppermute(
                    value[shift * lay.slots : (shift + 1) * lay.slots],
                    "reach",
                    [(place, (place + step) % lay.reach) for place in range(lay.reach)],
                )
            )
        return pieces

    next_day = [(d, d + 1) for d in range(day_total - 1)]
    last_day = [(d + 1, d) for d in range(day_total - 1)]
    received_a = jnp.concatenate(ring(sent_a, False), axis=0)
    prior_inputs = lax.ppermute(prior, "day", next_day)
    received_b = ring(sent_b, False)
    shared = (prior_inputs, pack, pack_other)
    own_a, day_a, home_a, *grads = attend(
        lay, 0, tab, in_blocks, up_blocks, received_a, *shared, None
    )
    received_b, grads = lax.optimization_barrier((received_b, grads))
    received_b = jnp.concatenate(received_b, axis=0)
    home_a = ring(home_a, True)
    day_a = lax.ppermute(day_a, "day", last_day)
    own_b, day_b, home_b, grad_mine, grad_other = attend(
        lay, 1, tab, in_blocks, up_blocks, received_b, *shared, grads
    )
    home_a, day_a, home_b, day_b, grad_other = lax.optimization_barrier(
        (home_a, day_a, home_b, day_b, grad_other)
    )
    grad_swapped = exchanged(grad_other, "head", 1)
    home_b = ring(home_b, True)
    day_b = lax.ppermute(day_b, "day", last_day)
    part, other, (home_b, day_b) = sum_gradients(grad_mine + grad_swapped, (home_b, day_b))
    home_a, home_b = jnp.concatenate(home_a, axis=0), jnp.concatenate(home_b, axis=0)
    half_shape = jax.ShapeDtypeStruct((blocks_dev, BLOCK, half), F32)
    keep, give = pl.pallas_call(
        lambda *refs: fold_kernel(lay, *refs),
        out_shape=(half_shape, half_shape),
        in_specs=[smem] + [in_vmem] * 6,
        out_specs=[in_vmem] * 2,
        compiler_params=pltpu.CompilerParams(vmem_limit_bytes=16 << 20),
        name="fold",
    )(tab, own_a, own_b, day_a, day_b, home_a, home_b)
    got = exchanged(give, "head", 1)
    back_blocks = pl.pallas_call(
        add_kernel,
        out_shape=jax.ShapeDtypeStruct((blocks_dev, BLOCK, half), BF16),
        in_specs=[in_vmem] * 2,
        out_specs=in_vmem,
        compiler_params=pltpu.CompilerParams(vmem_limit_bytes=16 << 20),
        name="add",
    )(keep, got)
    weight_grads = pl.pallas_call(
        split_kernel,
        out_shape=(
            jax.ShapeDtypeStruct((width, half), F32),
            jax.ShapeDtypeStruct((width, half), F32),
            jax.ShapeDtypeStruct((width, half), F32),
            jax.ShapeDtypeStruct((half, width), F32),
        ),
        in_specs=[smem] + [in_vmem] * 2,
        out_specs=[in_vmem] * 4,
        name="split",
    )(where, part, other)

    return (back_blocks.reshape(1, rows_dev, half), *weight_grads)


def solution(mesh):
    placed = (
        P(("groups", "day"), "reach", None),
        P(("groups", "day"), "reach", None),
        P(None, "head"),
        P(None, "head"),
        P(None, "head"),
        P("head", None),
        P("groups"),
        P("groups"),
    )
    return jax.shard_map(
        on_device,
        mesh=mesh,
        in_specs=placed,
        out_specs=(
            P(("groups", "day"), "reach", "head"),
            P("groups", "head"),
            P("groups", "head"),
            P("groups", "head"),
            P(("groups", "head"), None),
        ),
        check_vma=False,
    )
```

```python
import jax
import jax.numpy as jnp
from jax import lax
from jax.experimental import pallas as pl
from jax.experimental.pallas import tpu as pltpu
from jax.sharding import PartitionSpec as P

HD = 32
BLOCK = 128
GROUP = 128
CORES = 2
CHUNKS = 2
WORKERS = CORES * CHUNKS
F32 = jnp.float32
BF16 = jnp.bfloat16
PACK = 4
LOG2E = 1.4426950408889634


class Layout:
    def __init__(self, blocks_dev, reach_total):
        self.blocks = blocks_dev
        self.items = blocks_dev // CORES
        self.chunk_items = self.items // CHUNKS
        self.reach = reach_total
        self.slots = max(1, 2 * blocks_dev // reach_total // WORKERS)
        self.places = reach_total * self.slots
        self.block_of = 0
        self.recv_of = self.items
        self.count_own = 2 * self.items
        self.count_partner = 3 * self.items
        self.owner_of = 4 * self.items
        self.item_of = self.owner_of + blocks_dev
        self.core = self.item_of + blocks_dev
        self.later_day = self.core + 1
        self.size = -(-(self.core + 2) // 128) * 128
        self.home_of = 0
        self.chunk_of = blocks_dev
        self.asker_of = 2 * blocks_dev
        self.picks = 3 * blocks_dev
        self.homes_size = -(-(self.picks + CHUNKS * self.places) // 128) * 128


def pick_kernel(lay, partner, where, inputs, sent, homes, held, sem):
    bd, slots = lay.blocks, lay.slots
    reach_pos, core = where[0], where[1]
    copy = pltpu.make_async_copy(inputs, held, sem)
    copy.start()

    def clear_picks(index, carry):
        homes[lay.picks + index] = 0
        return carry

    lax.fori_loop(0, CHUNKS * lay.places, clear_picks, 0, unroll=True)

    def one_reach(peer, carry):
        def before(index, total):
            source = lax.div(partner[peer * bd + index], bd)
            return total + jnp.where(source < reach_pos, 1, 0)

        base = lax.fori_loop(0, bd, before, jnp.int32(0), unroll=True)

        def serve(index, rank):
            wanted = partner[peer * bd + index]
            hit = lax.div(wanted, bd) == reach_pos

            @pl.when(hit)
            def _():
                place = base + rank
                owner = lax.rem(place, CORES)
                chunk = lax.rem(lax.div(place, CORES), CHUNKS)
                slot = peer * slots + jnp.minimum(lax.div(rank, WORKERS), slots - 1)
                local = lax.rem(wanted, bd)
                homes[lay.home_of + local] = slot
                homes[lay.chunk_of + local] = chunk
                homes[lay.asker_of + local] = owner

                @pl.when(owner == core)
                def _():
                    homes[lay.picks + chunk * lay.places + slot] = local

            return rank + jnp.where(hit, 1, 0)

        lax.fori_loop(0, bd, serve, jnp.int32(0))
        return carry

    lax.fori_loop(0, lay.reach, one_reach, 0)
    copy.wait()

    def pick(place, carry):
        sent[place] = held[homes[lay.picks + place]]
        return carry

    lax.fori_loop(0, lay.places, pick, 0)


def deal_kernel(lay, partner, counts, where, homes, inputs, sent, prior, tab, start, used):
    bd, slots = lay.blocks, lay.slots
    reach_pos, core = where[0], where[1]

    def clear(index, carry):
        used[index] = 0
        start[index] = 0
        return carry

    lax.fori_loop(0, lay.reach, clear, 0, unroll=True)

    def count(index, carry):
        source = lax.div(partner[reach_pos * bd + index], bd)
        start[source] = start[source] + 1
        return carry

    lax.fori_loop(0, bd, count, 0)

    def prefix(index, total):
        here = start[index]
        start[index] = total
        return total + here

    lax.fori_loop(0, lay.reach, prefix, jnp.int32(0))

    def assign(index, carry):
        wanted = partner[reach_pos * bd + index]
        source = lax.div(wanted, bd)
        rank = used[source]
        used[source] = rank + 1
        place = start[source] + rank
        owner = lax.rem(place, CORES)
        chunk = lax.rem(lax.div(place, CORES), CHUNKS)
        item = chunk * lay.chunk_items + lax.div(place, WORKERS)
        slot = jnp.minimum(lax.div(rank, WORKERS), slots - 1)
        tab[lay.owner_of + index] = owner
        tab[lay.item_of + index] = item

        @pl.when(owner == core)
        def _():
            tab[lay.block_of + item] = index
            tab[lay.recv_of + item] = source * slots + slot
            tab[lay.count_own + item] = counts[reach_pos * bd + index]
            tab[lay.count_partner + item] = counts[wanted]

        return carry

    lax.fori_loop(0, bd, assign, 0)
    tab[lay.core] = core
    tab[lay.later_day] = where[2]

    def pick(place, carry):
        sent[place] = inputs[homes[lay.picks + lay.places + place]]
        return carry

    def pick_prior(item, carry):
        prior[item] = inputs[tab[lay.block_of + item]]
        return carry

    lax.fori_loop(0, lay.places, pick, 0)
    lax.fori_loop(0, lay.items, pick_prior, 0)


def dot(left, right):
    return lax.dot_general(left, right, (((1,), (0,)), ((), ())), preferred_element_type=F32)


def dot_t(left, right):
    return lax.dot_general(left, right, (((1,), (1,)), ((), ())), preferred_element_type=F32)


def attention_kernel(
    lay,
    chunk,
    tab,
    own_ref,
    up_ref,
    partner_ref,
    prior_ref,
    mine_ref,
    other_ref,
    *refs,
):
    if chunk:
        start_mine_ref, start_other_ref = refs[:2]
        refs = refs[2:]
    own_out_ref, day_ref, home_ref, grad_mine_ref, grad_other_ref = refs
    step = pl.program_id(0)
    item = step + chunk * lay.chunk_items
    factor = HD ** (-0.5)
    own, up = own_ref[0], up_ref[0]
    key_inputs = jnp.concatenate([own, partner_ref[0], prior_ref[0]], axis=0)
    width = own.shape[1]

    @pl.when(step == 0)
    def _():
        if chunk:
            grad_mine_ref[...] = start_mine_ref[...]
            grad_other_ref[...] = start_other_ref[...]
        else:
            grad_mine_ref[...] = jnp.zeros_like(grad_mine_ref)
            grad_other_ref[...] = jnp.zeros_like(grad_other_ref)

    def eye(size):
        rows = lax.broadcasted_iota(jnp.int32, (size, size), 0)
        cols = lax.broadcasted_iota(jnp.int32, (size, size), 1)
        return jnp.where(rows == cols, 1.0, 0.0).astype(BF16)

    query_t = jnp.concatenate([mine_ref[256:384, :], other_ref[256:384, :]], axis=0)
    output_w = jnp.concatenate([mine_ref[384:512, :], other_ref[384:512, :]], axis=0)
    queries = dot_t(own, query_t)
    back_out = dot_t(up, output_w)
    key_inputs_t = key_inputs.T

    count_own = tab[lay.count_own + item]
    count_partner = tab[lay.count_partner + item]
    count_prior = count_own * tab[lay.later_day]
    rows = lax.broadcasted_iota(jnp.int32, (BLOCK, PACK * BLOCK), 0)
    valid = jnp.concatenate([rows < count_own, rows < count_partner, rows < count_prior], axis=0)
    lane_head = lax.broadcasted_iota(jnp.int32, (BLOCK, GROUP), 1) // HD

    per_group = GROUP // HD // PACK
    groups = []
    for group, (weights_ref, grad_ref) in enumerate(
        ((mine_ref, grad_mine_ref), (other_ref, grad_other_ref))
    ):
        kv_t = weights_ref[0:256, :]
        kv = dot_t(key_inputs, kv_t).astype(BF16)
        kv_cols = kv.T
        lanes = slice(group * GROUP, (group + 1) * GROUP)
        groups.append((kv_t, kv, kv_cols, queries[:, lanes], back_out[:, lanes], grad_ref))

    def start(step):
        kv_t, kv, kv_cols, group_queries, group_back, grad_ref = groups[step // per_group]
        heads = [step % per_group * PACK + h for h in range(PACK)]
        query_pack, back_pack = (
            jnp.concatenate([jnp.where(lane_head == h, rows_of, 0.0) for h in heads], axis=0).astype(BF16)
            for rows_of in (group_queries, group_back)
        )
        return query_pack, back_pack, dot_t(kv[:, :GROUP], query_pack), dot_t(kv[:, GROUP:], back_pack)

    def middle(logits, back_weights):
        logits = jnp.where(valid, logits, -1e30)
        highest = jnp.max(logits, axis=0, keepdims=True)
        raised = jnp.exp2((logits - highest) * (factor * LOG2E))
        scale = 1.0 / jnp.sum(raised, axis=0, keepdims=True)
        weights = raised * scale
        center = jnp.sum(weights * back_weights, axis=0, keepdims=True)
        back_logits = (weights * ((back_weights - center) * factor)).astype(BF16)
        return weights.astype(BF16), back_logits

    outputs_t, back_query_t = [], []
    pair_keys, pair_values = {}, {}

    def finish(step, query_pack, back_pack, weights_low, back_logits):
        group = step // per_group
        kv_cols = groups[group][2]
        pair_values.setdefault(group, []).append(dot(weights_low, back_pack))
        pair_keys.setdefault(group, []).append(dot(back_logits, query_pack))
        first = step % per_group * PACK * HD
        size = PACK * HD
        out_t = dot(kv_cols[GROUP + first : GROUP + first + size, :], weights_low)
        query_grad_t = dot(kv_cols[first : first + size, :], back_logits)
        for h in range(PACK):
            lanes = slice(h * BLOCK, (h + 1) * BLOCK)
            outputs_t.append(out_t[h * HD : (h + 1) * HD, lanes])
            back_query_t.append(query_grad_t[h * HD : (h + 1) * HD, lanes])

    total_steps = 2 * per_group
    started = start(0)
    waiting = None
    for step in range(total_steps):
        following = start(step + 1) if step + 1 < total_steps else None
        query_pack, back_pack, logits, back_weights = started
        if waiting is not None:
            finish(*waiting)
        made = middle(logits, back_weights)
        waiting = (step, query_pack, back_pack, *made)
        started = following
    finish(*waiting)

    back_inputs = None
    for group, (kv_t, _, _, _, _, grad_ref) in enumerate(groups):
        back_kv = jnp.concatenate([sum(pair_keys[group][1:], pair_keys[group][0]), sum(pair_values[group][1:], pair_values[group][0])], axis=1).astype(BF16)
        term = dot(back_kv, kv_t)
        back_inputs = term if back_inputs is None else back_inputs + term
        grad_ref[0:256, :] += dot(key_inputs_t, back_kv)

    outputs_t = jnp.concatenate(outputs_t, axis=0).astype(BF16)
    back_query_t = jnp.concatenate(back_query_t, axis=0).astype(BF16)
    query_grad = dot(back_query_t, own)
    output_grad = dot(outputs_t, up)
    grad_mine_ref[256:384, :] += query_grad[:GROUP]
    grad_other_ref[256:384, :] += query_grad[GROUP:]
    grad_mine_ref[384:512, :] += output_grad[:GROUP]
    grad_other_ref[384:512, :] += output_grad[GROUP:]
    back_query = back_query_t.T
    own_out_ref[0] = back_inputs[:BLOCK] + dot(back_query, query_t)
    home_ref[0] = back_inputs[BLOCK : 2 * BLOCK].astype(BF16)
    day_ref[0] = back_inputs[2 * BLOCK :].astype(BF16)


def fold_kernel(lay, tab, homes, own_a, own_b, day_a, day_b, home_a, home_b, keep, give):
    core = tab[lay.core]
    half = keep.shape[2]

    def one(block, carry):
        item = tab[lay.item_of + block]
        mine = tab[lay.owner_of + block] == core
        place = homes[lay.home_of + block]
        asked = homes[lay.asker_of + block] == core
        early = homes[lay.chunk_of + block] == 0
        in_a = item < lay.chunk_items
        item_a = jnp.minimum(item, lay.chunk_items - 1)
        item_b = jnp.maximum(item - lay.chunk_items, 0)
        own = jnp.where(in_a, own_a[item_a], own_b[item_b])
        own += jnp.where(in_a, day_a[item_a].astype(F32), day_b[item_b].astype(F32))
        home = jnp.where(early, home_a[place].astype(F32), home_b[place].astype(F32))
        total = jnp.where(mine, own, 0.0) + jnp.where(asked, home, 0.0)
        low, high = total[:, :half], total[:, half:]
        keep[block] = jnp.where(core == 0, low, high)
        give[block] = jnp.where(core == 0, high, low)
        return carry

    lax.fori_loop(0, lay.blocks, one, 0)


def add_kernel(kept, got, out):
    out[...] = (kept[...] + got[...]).astype(BF16)


def attend(lay, chunk, tab, in_blocks, up_blocks, received, prior_inputs, pack, pack_other, carried):
    width = in_blocks.shape[-1]
    offset = chunk * lay.chunk_items

    def at_item(step, tab):
        return (offset + step, 0, 0)

    def at_block(step, tab):
        return (tab[lay.block_of + offset + step], 0, 0)

    def at_recv(step, tab):
        return (tab[lay.recv_of + offset + step], 0, 0)

    def at_step(step, tab):
        return (step, 0, 0)

    def fixed(step, tab):
        return (0, 0)

    full_block = (1, BLOCK, width)
    weights_block = (4 * GROUP, width)
    in_specs = [
        pl.BlockSpec(full_block, at_block),
        pl.BlockSpec(full_block, at_block),
        pl.BlockSpec(full_block, at_recv),
        pl.BlockSpec(full_block, at_item),
        pl.BlockSpec(weights_block, fixed),
        pl.BlockSpec(weights_block, fixed),
    ]
    operands = [in_blocks, up_blocks, received, prior_inputs, pack, pack_other]
    if chunk:
        in_specs += [pl.BlockSpec(weights_block, fixed)] * 2
        operands += carried
    pieces = lay.chunk_items
    flops = 2 * pieces * (23 * BLOCK * width * width + 24 * BLOCK * 3 * BLOCK * 512)
    return pl.pallas_call(
        lambda *refs: attention_kernel(lay, chunk, *refs),
        grid_spec=pltpu.PrefetchScalarGridSpec(
            num_scalar_prefetch=1,
            grid=(pieces,),
            in_specs=in_specs,
            out_specs=(
                pl.BlockSpec(full_block, at_step),
                pl.BlockSpec(full_block, at_step),
                pl.BlockSpec(full_block, at_recv),
                pl.BlockSpec(weights_block, fixed),
                pl.BlockSpec(weights_block, fixed),
            ),
        ),
        out_shape=(
            pltpu.HBM((pieces, BLOCK, width), F32),
            pltpu.HBM((pieces, BLOCK, width), BF16),
            pltpu.HBM((lay.places, BLOCK, width), BF16),
            pltpu.HBM(weights_block, F32),
            pltpu.HBM(weights_block, F32),
        ),
        compiler_params=pltpu.CompilerParams(vmem_limit_bytes=32 << 20),
        cost_estimate=pl.CostEstimate(
            flops=flops, bytes_accessed=5 << 20, transcendentals=pieces * 8 * BLOCK * 3 * BLOCK
        ),
        name=f"attention_{chunk}",
    )(
        tab,
        *[
            value
            if place == 2
            else pltpu.with_memory_space_constraint(value, pltpu.HBM)
            for place, value in enumerate(operands)
        ],
    )


def exchanged(value, axis, bit):
    count = lax.axis_size(axis)
    return lax.ppermute(value, axis, [(place, place ^ bit) for place in range(count)])


def summed_over(value, axis, bit):
    low = value.astype(BF16)
    return low.astype(F32) + exchanged(low, axis, bit).astype(F32)


def sum_gradients(total, settled):
    half = total.shape[0] // 2
    first = lax.rem(lax.axis_index("day"), 2) == 0
    kept = jnp.where(first, total[:half], total[half:])
    given = jnp.where(first, total[half:], total[:half])
    part = kept.astype(BF16).astype(F32) + exchanged(given.astype(BF16), "day", 1).astype(F32)
    bit = 2
    while bit < lax.axis_size("day"):
        part = summed_over(part, "day", bit)
        bit *= 2
    bit = 1
    while bit < lax.axis_size("reach"):
        part = summed_over(part, "reach", bit)
        if bit == 1:
            part, *settled = lax.optimization_barrier((part, *settled))
        bit *= 2
    return part, exchanged(part, "day", 1), settled


def split_kernel(where, part, other, query_out, key_out, value_out, output_out):
    first = lax.rem(where[3], 2) == 0
    upper = jnp.where(first, part[...], other[...])
    lower = jnp.where(first, other[...], part[...])
    key_out[...] = upper[:, :GROUP]
    value_out[...] = upper[:, GROUP:]
    query_out[...] = lower[:GROUP].T
    output_out[...] = lower[GROUP:]


def on_device(
    inputs, upstream, query_weight, key_weight, value_weight, output_weight, partner, counts
):
    days_dev, rows_dev, width = inputs.shape
    assert days_dev == 1 and width == 2 * GROUP
    blocks_dev = rows_dev // BLOCK
    reach_total = lax.axis_size("reach")
    day_total = lax.axis_size("day")
    assert lax.axis_size("head") == CORES
    lay = Layout(blocks_dev, reach_total)
    half = width // 2
    in_blocks = inputs.reshape(blocks_dev, BLOCK, width)
    up_blocks = upstream.reshape(blocks_dev, BLOCK, width)
    where = jnp.stack(
        [
            lax.axis_index("reach"),
            lax.axis_index("head"),
            (lax.axis_index("day") > 0).astype(jnp.int32),
            lax.axis_index("day"),
        ]
    )
    pack = jnp.concatenate([key_weight.T, value_weight.T, query_weight.T, output_weight], axis=0)
    pack_other = exchanged(pack, "head", 1)

    smem = pl.BlockSpec(memory_space=pltpu.SMEM)
    in_vmem = pl.BlockSpec(memory_space=pltpu.VMEM)
    anywhere = pl.BlockSpec(memory_space=pl.ANY)
    sent_shape = jax.ShapeDtypeStruct((lay.places, BLOCK, width), BF16)
    sent_a, homes = pl.pallas_call(
        lambda *refs: pick_kernel(lay, *refs),
        out_shape=(sent_shape, jax.ShapeDtypeStruct((lay.homes_size,), jnp.int32)),
        in_specs=[smem, smem, anywhere],
        out_specs=(in_vmem, smem),
        scratch_shapes=[
            pltpu.VMEM((blocks_dev, BLOCK, width), BF16),
            pltpu.SemaphoreType.DMA,
        ],
        compiler_params=pltpu.CompilerParams(vmem_limit_bytes=16 << 20),
        name="pick",
    )(partner, where, pltpu.with_memory_space_constraint(in_blocks, pltpu.HBM))
    sent_b, prior, tab = pl.pallas_call(
        lambda *refs: deal_kernel(lay, *refs),
        out_shape=(
            sent_shape,
            jax.ShapeDtypeStruct((lay.items, BLOCK, width), BF16),
            jax.ShapeDtypeStruct((lay.size,), jnp.int32),
        ),
        in_specs=[smem, smem, smem, smem, in_vmem],
        out_specs=(in_vmem, in_vmem, smem),
        scratch_shapes=[
            pltpu.SMEM((lay.reach,), jnp.int32),
            pltpu.SMEM((lay.reach,), jnp.int32),
        ],
        compiler_params=pltpu.CompilerParams(vmem_limit_bytes=16 << 20),
        name="deal",
    )(partner, counts, where, homes, in_blocks)

    def ring(value):
        shape = value.shape
        value = value.reshape(lay.reach, lay.slots * BLOCK, width)
        return lax.all_to_all(value, "reach", 0, 0, tiled=True).reshape(shape)

    next_day = [(d, d + 1) for d in range(day_total - 1)]
    last_day = [(d + 1, d) for d in range(day_total - 1)]
    received_a = ring(sent_a)
    prior_inputs = lax.ppermute(prior, "day", next_day)
    received_b = ring(sent_b)
    shared = (prior_inputs, pack, pack_other)
    own_a, day_a, home_a, *grads = attend(
        lay, 0, tab, in_blocks, up_blocks, received_a, *shared, None
    )
    home_a = ring(home_a)
    day_a = lax.ppermute(day_a, "day", last_day)
    own_b, day_b, home_b, grad_mine, grad_other = attend(
        lay, 1, tab, in_blocks, up_blocks, received_b, *shared, grads
    )
    home_a, day_a, home_b, day_b, grad_other = lax.optimization_barrier(
        (home_a, day_a, home_b, day_b, grad_other)
    )
    grad_swapped = exchanged(grad_other, "head", 1)
    home_b = ring(home_b)
    day_b = lax.ppermute(day_b, "day", last_day)
    part, other, (home_b, day_b) = sum_gradients(grad_mine + grad_swapped, (home_b, day_b))
    half_shape = jax.ShapeDtypeStruct((blocks_dev, BLOCK, half), F32)
    keep, give = pl.pallas_call(
        lambda *refs: fold_kernel(lay, *refs),
        out_shape=(half_shape, half_shape),
        in_specs=[smem] * 2 + [in_vmem] * 6,
        out_specs=[in_vmem] * 2,
        compiler_params=pltpu.CompilerParams(vmem_limit_bytes=16 << 20),
        name="fold",
    )(tab, homes, own_a, own_b, day_a, day_b, home_a, home_b)
    got = exchanged(give, "head", 1)
    back_blocks = pl.pallas_call(
        add_kernel,
        out_shape=jax.ShapeDtypeStruct((blocks_dev, BLOCK, half), BF16),
        in_specs=[in_vmem] * 2,
        out_specs=in_vmem,
        compiler_params=pltpu.CompilerParams(vmem_limit_bytes=16 << 20),
        name="add",
    )(keep, got)
    weight_grads = pl.pallas_call(
        split_kernel,
        out_shape=(
            jax.ShapeDtypeStruct((width, half), F32),
            jax.ShapeDtypeStruct((width, half), F32),
            jax.ShapeDtypeStruct((width, half), F32),
            jax.ShapeDtypeStruct((half, width), F32),
        ),
        in_specs=[smem] + [in_vmem] * 2,
        out_specs=[in_vmem] * 4,
        name="split",
    )(where, part, other)

    return (back_blocks.reshape(1, rows_dev, half), *weight_grads)


def solution(mesh):
    placed = (
        P(("groups", "day"), "reach", None),
        P(("groups", "day"), "reach", None),
        P(None, "head"),
        P(None, "head"),
        P(None, "head"),
        P("head", None),
        P("groups"),
        P("groups"),
    )
    return jax.shard_map(
        on_device,
        mesh=mesh,
        in_specs=placed,
        out_specs=(
            P(("groups", "day"), "reach", "head"),
            P("groups", "head"),
            P("groups", "head"),
            P("groups", "head"),
            P(("groups", "head"), None),
        ),
        check_vma=False,
    )
```

```python
import jax
import jax.numpy as jnp
from jax import lax
from jax.experimental import pallas as pl
from jax.experimental.pallas import tpu as pltpu
from jax.sharding import PartitionSpec as P

HD = 32
BLOCK = 128
GROUP = 128
CORES = 2
CHUNKS = 2
WORKERS = CORES * CHUNKS
F32 = jnp.float32
BF16 = jnp.bfloat16
PACK = 4
LOG2E = 1.4426950408889634


class Layout:
    def __init__(self, blocks_dev, reach_total):
        self.blocks = blocks_dev
        self.items = blocks_dev // CORES
        self.chunk_items = self.items // CHUNKS
        self.reach = reach_total
        self.slots = max(1, 2 * blocks_dev // reach_total // WORKERS)
        self.places = reach_total * self.slots
        self.block_of = 0
        self.recv_of = self.items
        self.count_own = 2 * self.items
        self.count_partner = 3 * self.items
        self.owner_of = 4 * self.items
        self.item_of = self.owner_of + blocks_dev
        self.core = self.item_of + blocks_dev
        self.later_day = self.core + 1
        self.size = -(-(self.core + 2) // 128) * 128
        self.home_of = 0
        self.chunk_of = blocks_dev
        self.asker_of = 2 * blocks_dev
        self.picks = 3 * blocks_dev
        self.homes_size = -(-(self.picks + CHUNKS * self.places) // 128) * 128


def pick_kernel(lay, partner, where, inputs, sent, homes, held, sem):
    bd, slots = lay.blocks, lay.slots
    reach_pos, core = where[0], where[1]
    copy = pltpu.make_async_copy(inputs, held, sem)
    copy.start()

    def clear_picks(index, carry):
        homes[lay.picks + index] = 0
        return carry

    lax.fori_loop(0, CHUNKS * lay.places, clear_picks, 0, unroll=True)

    def one_reach(peer, carry):
        def before(index, total):
            source = lax.div(partner[peer * bd + index], bd)
            return total + jnp.where(source < reach_pos, 1, 0)

        base = lax.fori_loop(0, bd, before, jnp.int32(0), unroll=True)

        def serve(index, rank):
            wanted = partner[peer * bd + index]
            hit = lax.div(wanted, bd) == reach_pos

            @pl.when(hit)
            def _():
                place = base + rank
                owner = lax.rem(place, CORES)
                chunk = lax.rem(lax.div(place, CORES), CHUNKS)
                slot = peer * slots + jnp.minimum(lax.div(rank, WORKERS), slots - 1)
                local = lax.rem(wanted, bd)
                homes[lay.home_of + local] = slot
                homes[lay.chunk_of + local] = chunk
                homes[lay.asker_of + local] = owner

                @pl.when(owner == core)
                def _():
                    homes[lay.picks + chunk * lay.places + slot] = local

            return rank + jnp.where(hit, 1, 0)

        lax.fori_loop(0, bd, serve, jnp.int32(0))
        return carry

    lax.fori_loop(0, lay.reach, one_reach, 0)
    copy.wait()

    def pick(place, carry):
        sent[place] = held[homes[lay.picks + place]]
        return carry

    lax.fori_loop(0, lay.places, pick, 0)


def deal_kernel(lay, partner, counts, where, homes, inputs, sent, prior, tab, start, used):
    bd, slots = lay.blocks, lay.slots
    reach_pos, core = where[0], where[1]

    def clear(index, carry):
        used[index] = 0
        start[index] = 0
        return carry

    lax.fori_loop(0, lay.reach, clear, 0, unroll=True)

    def count(index, carry):
        source = lax.div(partner[reach_pos * bd + index], bd)
        start[source] = start[source] + 1
        return carry

    lax.fori_loop(0, bd, count, 0)

    def prefix(index, total):
        here = start[index]
        start[index] = total
        return total + here

    lax.fori_loop(0, lay.reach, prefix, jnp.int32(0))

    def assign(index, carry):
        wanted = partner[reach_pos * bd + index]
        source = lax.div(wanted, bd)
        rank = used[source]
        used[source] = rank + 1
        place = start[source] + rank
        owner = lax.rem(place, CORES)
        chunk = lax.rem(lax.div(place, CORES), CHUNKS)
        item = chunk * lay.chunk_items + lax.div(place, WORKERS)
        slot = jnp.minimum(lax.div(rank, WORKERS), slots - 1)
        tab[lay.owner_of + index] = owner
        tab[lay.item_of + index] = item

        @pl.when(owner == core)
        def _():
            tab[lay.block_of + item] = index
            tab[lay.recv_of + item] = source * slots + slot
            tab[lay.count_own + item] = counts[reach_pos * bd + index]
            tab[lay.count_partner + item] = counts[wanted]

        return carry

    lax.fori_loop(0, bd, assign, 0)
    tab[lay.core] = core
    tab[lay.later_day] = where[2]

    def pick(place, carry):
        sent[place] = inputs[homes[lay.picks + lay.places + place]]
        return carry

    def pick_prior(item, carry):
        prior[item] = inputs[tab[lay.block_of + item]]
        return carry

    lax.fori_loop(0, lay.places, pick, 0)
    lax.fori_loop(0, lay.items, pick_prior, 0)


def dot(left, right):
    return lax.dot_general(left, right, (((1,), (0,)), ((), ())), preferred_element_type=F32)


def dot_t(left, right):
    return lax.dot_general(left, right, (((1,), (1,)), ((), ())), preferred_element_type=F32)


def attention_kernel(
    lay,
    chunk,
    tab,
    own_ref,
    up_ref,
    partner_ref,
    prior_ref,
    mine_ref,
    other_ref,
    *refs,
):
    if chunk:
        start_mine_ref, start_other_ref = refs[:2]
        refs = refs[2:]
    own_out_ref, day_ref, home_ref, grad_mine_ref, grad_other_ref = refs
    step = pl.program_id(0)
    item = step + chunk * lay.chunk_items
    factor = HD ** (-0.5)
    own, up = own_ref[0], up_ref[0]
    key_inputs = jnp.concatenate([own, partner_ref[0], prior_ref[0]], axis=0)
    width = own.shape[1]

    @pl.when(step == 0)
    def _():
        if chunk:
            grad_mine_ref[...] = start_mine_ref[...]
            grad_other_ref[...] = start_other_ref[...]
        else:
            grad_mine_ref[...] = jnp.zeros_like(grad_mine_ref)
            grad_other_ref[...] = jnp.zeros_like(grad_other_ref)

    def eye(size):
        rows = lax.broadcasted_iota(jnp.int32, (size, size), 0)
        cols = lax.broadcasted_iota(jnp.int32, (size, size), 1)
        return jnp.where(rows == cols, 1.0, 0.0).astype(BF16)

    query_t = jnp.concatenate([mine_ref[256:384, :], other_ref[256:384, :]], axis=0)
    output_w = jnp.concatenate([mine_ref[384:512, :], other_ref[384:512, :]], axis=0)
    queries = dot_t(own, query_t)
    back_out = dot_t(up, output_w)
    key_inputs_t = key_inputs.T

    count_own = tab[lay.count_own + item]
    count_partner = tab[lay.count_partner + item]
    count_prior = count_own * tab[lay.later_day]
    rows = lax.broadcasted_iota(jnp.int32, (BLOCK, PACK * BLOCK), 0)
    valid = jnp.concatenate([rows < count_own, rows < count_partner, rows < count_prior], axis=0)
    lane_head = lax.broadcasted_iota(jnp.int32, (BLOCK, GROUP), 1) // HD

    per_group = GROUP // HD // PACK
    groups = []
    for group, (weights_ref, grad_ref) in enumerate(
        ((mine_ref, grad_mine_ref), (other_ref, grad_other_ref))
    ):
        kv_t = weights_ref[0:256, :]
        kv = dot_t(key_inputs, kv_t).astype(BF16)
        kv_cols = kv.T
        lanes = slice(group * GROUP, (group + 1) * GROUP)
        groups.append((kv_t, kv, kv_cols, queries[:, lanes], back_out[:, lanes], grad_ref))

    def start(step):
        kv_t, kv, kv_cols, group_queries, group_back, grad_ref = groups[step // per_group]
        heads = [step % per_group * PACK + h for h in range(PACK)]
        query_pack, back_pack = (
            jnp.concatenate([jnp.where(lane_head == h, rows_of, 0.0) for h in heads], axis=0).astype(BF16)
            for rows_of in (group_queries, group_back)
        )
        return query_pack, back_pack, dot_t(kv[:, :GROUP], query_pack), dot_t(kv[:, GROUP:], back_pack)

    def middle(logits, back_weights):
        logits = jnp.where(valid, logits, -1e30)
        highest = jnp.max(logits, axis=0, keepdims=True)
        raised = jnp.exp2((logits - highest) * (factor * LOG2E))
        scale = 1.0 / jnp.sum(raised, axis=0, keepdims=True)
        weights = raised * scale
        center = jnp.sum(weights * back_weights, axis=0, keepdims=True)
        back_logits = (weights * ((back_weights - center) * factor)).astype(BF16)
        return weights.astype(BF16), back_logits

    outputs_t, back_query_t = [], []
    pair_keys, pair_values = {}, {}

    def finish(step, query_pack, back_pack, weights_low, back_logits):
        group = step // per_group
        kv_cols = groups[group][2]
        pair_values.setdefault(group, []).append(dot(weights_low, back_pack))
        pair_keys.setdefault(group, []).append(dot(back_logits, query_pack))
        first = step % per_group * PACK * HD
        size = PACK * HD
        out_t = dot(kv_cols[GROUP + first : GROUP + first + size, :], weights_low)
        query_grad_t = dot(kv_cols[first : first + size, :], back_logits)
        for h in range(PACK):
            lanes = slice(h * BLOCK, (h + 1) * BLOCK)
            outputs_t.append(out_t[h * HD : (h + 1) * HD, lanes])
            back_query_t.append(query_grad_t[h * HD : (h + 1) * HD, lanes])

    total_steps = 2 * per_group
    started = start(0)
    waiting = None
    for step in range(total_steps):
        following = start(step + 1) if step + 1 < total_steps else None
        query_pack, back_pack, logits, back_weights = started
        if waiting is not None:
            finish(*waiting)
        made = middle(logits, back_weights)
        waiting = (step, query_pack, back_pack, *made)
        started = following
    finish(*waiting)

    back_inputs = None
    for group, (kv_t, _, _, _, _, grad_ref) in enumerate(groups):
        back_kv = jnp.concatenate([sum(pair_keys[group][1:], pair_keys[group][0]), sum(pair_values[group][1:], pair_values[group][0])], axis=1).astype(BF16)
        term = dot(back_kv, kv_t)
        back_inputs = term if back_inputs is None else back_inputs + term
        grad_ref[0:256, :] += dot(key_inputs_t, back_kv)

    outputs_t = jnp.concatenate(outputs_t, axis=0).astype(BF16)
    back_query_t = jnp.concatenate(back_query_t, axis=0).astype(BF16)
    query_grad = dot(back_query_t, own)
    output_grad = dot(outputs_t, up)
    grad_mine_ref[256:384, :] += query_grad[:GROUP]
    grad_other_ref[256:384, :] += query_grad[GROUP:]
    grad_mine_ref[384:512, :] += output_grad[:GROUP]
    grad_other_ref[384:512, :] += output_grad[GROUP:]
    back_query = back_query_t.T
    own_out_ref[0] = back_inputs[:BLOCK] + dot(back_query, query_t)
    home_ref[0] = back_inputs[BLOCK : 2 * BLOCK].astype(BF16)
    day_ref[0] = back_inputs[2 * BLOCK :].astype(BF16)


def fold_kernel(lay, tab, homes, own_a, own_b, day_a, day_b, home_a, home_b, keep, give):
    core = tab[lay.core]
    half = keep.shape[2]

    def one(block, carry):
        item = tab[lay.item_of + block]
        mine = tab[lay.owner_of + block] == core
        place = homes[lay.home_of + block]
        asked = homes[lay.asker_of + block] == core
        early = homes[lay.chunk_of + block] == 0
        in_a = item < lay.chunk_items
        item_a = jnp.minimum(item, lay.chunk_items - 1)
        item_b = jnp.maximum(item - lay.chunk_items, 0)
        own = jnp.where(in_a, own_a[item_a], own_b[item_b])
        own += jnp.where(in_a, day_a[item_a].astype(F32), day_b[item_b].astype(F32))
        home = jnp.where(early, home_a[place].astype(F32), home_b[place].astype(F32))
        total = jnp.where(mine, own, 0.0) + jnp.where(asked, home, 0.0)
        low, high = total[:, :half], total[:, half:]
        keep[block] = jnp.where(core == 0, low, high)
        give[block] = jnp.where(core == 0, high, low)
        return carry

    lax.fori_loop(0, lay.blocks, one, 0)


def add_kernel(kept, got, out):
    out[...] = (kept[...] + got[...]).astype(BF16)


def attend(lay, chunk, tab, in_blocks, up_blocks, received, prior_inputs, pack, pack_other, carried):
    width = in_blocks.shape[-1]
    offset = chunk * lay.chunk_items

    def at_item(step, tab):
        return (offset + step, 0, 0)

    def at_block(step, tab):
        return (tab[lay.block_of + offset + step], 0, 0)

    def at_recv(step, tab):
        return (tab[lay.recv_of + offset + step], 0, 0)

    def at_step(step, tab):
        return (step, 0, 0)

    def fixed(step, tab):
        return (0, 0)

    full_block = (1, BLOCK, width)
    weights_block = (4 * GROUP, width)
    in_specs = [
        pl.BlockSpec(full_block, at_block),
        pl.BlockSpec(full_block, at_block),
        pl.BlockSpec(full_block, at_recv),
        pl.BlockSpec(full_block, at_item),
        pl.BlockSpec(weights_block, fixed),
        pl.BlockSpec(weights_block, fixed),
    ]
    operands = [in_blocks, up_blocks, received, prior_inputs, pack, pack_other]
    if chunk:
        in_specs += [pl.BlockSpec(weights_block, fixed)] * 2
        operands += carried
    pieces = lay.chunk_items
    flops = 2 * pieces * (23 * BLOCK * width * width + 24 * BLOCK * 3 * BLOCK * 512)
    return pl.pallas_call(
        lambda *refs: attention_kernel(lay, chunk, *refs),
        grid_spec=pltpu.PrefetchScalarGridSpec(
            num_scalar_prefetch=1,
            grid=(pieces,),
            in_specs=in_specs,
            out_specs=(
                pl.BlockSpec(full_block, at_step),
                pl.BlockSpec(full_block, at_step),
                pl.BlockSpec(full_block, at_recv),
                pl.BlockSpec(weights_block, fixed),
                pl.BlockSpec(weights_block, fixed),
            ),
        ),
        out_shape=(
            pltpu.HBM((pieces, BLOCK, width), F32),
            pltpu.HBM((pieces, BLOCK, width), BF16),
            pltpu.HBM((lay.places, BLOCK, width), BF16),
            pltpu.HBM(weights_block, F32),
            pltpu.HBM(weights_block, F32),
        ),
        compiler_params=pltpu.CompilerParams(vmem_limit_bytes=32 << 20),
        cost_estimate=pl.CostEstimate(
            flops=flops, bytes_accessed=5 << 20, transcendentals=pieces * 8 * BLOCK * 3 * BLOCK
        ),
        name=f"attention_{chunk}",
    )(
        tab,
        *[
            value
            if place == 2
            else pltpu.with_memory_space_constraint(value, pltpu.HBM)
            for place, value in enumerate(operands)
        ],
    )


def exchanged(value, axis, bit):
    count = lax.axis_size(axis)
    return lax.ppermute(value, axis, [(place, place ^ bit) for place in range(count)])


def summed_over(value, axis, bit):
    low = value.astype(BF16)
    return low.astype(F32) + exchanged(low, axis, bit).astype(F32)


def sum_gradients(total, home_b, fold):
    half = total.shape[0] // 2
    first = lax.rem(lax.axis_index("day"), 2) == 0
    kept = jnp.where(first, total[:half], total[half:])
    given = jnp.where(first, total[half:], total[:half])
    part = kept.astype(BF16).astype(F32) + exchanged(given.astype(BF16), "day", 1).astype(F32)
    bit = 2
    while bit < lax.axis_size("day"):
        part = summed_over(part, "day", bit)
        bit *= 2
    bit = 1
    while bit < lax.axis_size("reach"):
        part = summed_over(part, "reach", bit)
        if bit == 1:
            part, home_b = lax.optimization_barrier((part, home_b))
        bit *= 2
    part, folded = lax.optimization_barrier((part.astype(BF16), fold(home_b)))
    return part, exchanged(part, "day", 1), folded


def split_kernel(where, part, other, query_out, key_out, value_out, output_out):
    first = lax.rem(where[3], 2) == 0
    mine, theirs = part[...].astype(F32), other[...].astype(F32)
    upper = jnp.where(first, mine, theirs)
    lower = jnp.where(first, theirs, mine)
    key_out[...] = upper[:, :GROUP]
    value_out[...] = upper[:, GROUP:]
    query_out[...] = lower[:GROUP].T
    output_out[...] = lower[GROUP:]


def on_device(
    inputs, upstream, query_weight, key_weight, value_weight, output_weight, partner, counts
):
    days_dev, rows_dev, width = inputs.shape
    assert days_dev == 1 and width == 2 * GROUP
    blocks_dev = rows_dev // BLOCK
    reach_total = lax.axis_size("reach")
    day_total = lax.axis_size("day")
    assert lax.axis_size("head") == CORES
    lay = Layout(blocks_dev, reach_total)
    half = width // 2
    in_blocks = inputs.reshape(blocks_dev, BLOCK, width)
    up_blocks = upstream.reshape(blocks_dev, BLOCK, width)
    where = jnp.stack(
        [
            lax.axis_index("reach"),
            lax.axis_index("head"),
            (lax.axis_index("day") > 0).astype(jnp.int32),
            lax.axis_index("day"),
        ]
    )
    pack = jnp.concatenate([key_weight.T, value_weight.T, query_weight.T, output_weight], axis=0)
    pack_other = exchanged(pack, "head", 1)

    smem = pl.BlockSpec(memory_space=pltpu.SMEM)
    in_vmem = pl.BlockSpec(memory_space=pltpu.VMEM)
    anywhere = pl.BlockSpec(memory_space=pl.ANY)
    sent_shape = jax.ShapeDtypeStruct((lay.places, BLOCK, width), BF16)
    sent_a, homes = pl.pallas_call(
        lambda *refs: pick_kernel(lay, *refs),
        out_shape=(sent_shape, jax.ShapeDtypeStruct((lay.homes_size,), jnp.int32)),
        in_specs=[smem, smem, anywhere],
        out_specs=(in_vmem, smem),
        scratch_shapes=[
            pltpu.VMEM((blocks_dev, BLOCK, width), BF16),
            pltpu.SemaphoreType.DMA,
        ],
        compiler_params=pltpu.CompilerParams(vmem_limit_bytes=16 << 20),
        name="pick",
    )(partner, where, pltpu.with_memory_space_constraint(in_blocks, pltpu.HBM))
    sent_b, prior, tab = pl.pallas_call(
        lambda *refs: deal_kernel(lay, *refs),
        out_shape=(
            sent_shape,
            jax.ShapeDtypeStruct((lay.items, BLOCK, width), BF16),
            jax.ShapeDtypeStruct((lay.size,), jnp.int32),
        ),
        in_specs=[smem, smem, smem, smem, in_vmem],
        out_specs=(in_vmem, in_vmem, smem),
        scratch_shapes=[
            pltpu.SMEM((lay.reach,), jnp.int32),
            pltpu.SMEM((lay.reach,), jnp.int32),
        ],
        compiler_params=pltpu.CompilerParams(vmem_limit_bytes=16 << 20),
        name="deal",
    )(partner, counts, where, homes, in_blocks)

    def ring(value):
        shape = value.shape
        value = value.reshape(lay.reach, lay.slots * BLOCK, width)
        return lax.all_to_all(value, "reach", 0, 0, tiled=True).reshape(shape)

    next_day = [(d, d + 1) for d in range(day_total - 1)]
    last_day = [(d + 1, d) for d in range(day_total - 1)]
    received_a = ring(sent_a)
    prior_inputs = lax.ppermute(prior, "day", next_day)
    received_b = ring(sent_b)
    shared = (prior_inputs, pack, pack_other)
    own_a, day_a, home_a, *grads = attend(
        lay, 0, tab, in_blocks, up_blocks, received_a, *shared, None
    )
    home_a = ring(home_a)
    day_a = lax.ppermute(day_a, "day", last_day)
    own_b, day_b, home_b, grad_mine, grad_other = attend(
        lay, 1, tab, in_blocks, up_blocks, received_b, *shared, grads
    )
    home_a, day_a, home_b, day_b, grad_other = lax.optimization_barrier(
        (home_a, day_a, home_b, day_b, grad_other)
    )
    grad_swapped = exchanged(grad_other, "head", 1)
    home_b = ring(home_b)
    day_b = lax.ppermute(day_b, "day", last_day)
    half_shape = jax.ShapeDtypeStruct((blocks_dev, BLOCK, half), F32)

    def fold(home_b):
        return pl.pallas_call(
            lambda *refs: fold_kernel(lay, *refs),
            out_shape=(half_shape, half_shape),
            in_specs=[smem] * 2 + [in_vmem] * 6,
            out_specs=[in_vmem] * 2,
            compiler_params=pltpu.CompilerParams(vmem_limit_bytes=16 << 20),
            name="fold",
        )(tab, homes, own_a, own_b, day_a, day_b, home_a, home_b)

    part, other, (keep, give) = sum_gradients(grad_mine + grad_swapped, home_b, fold)
    got = exchanged(give, "head", 1)
    back_blocks = pl.pallas_call(
        add_kernel,
        out_shape=jax.ShapeDtypeStruct((blocks_dev, BLOCK, half), BF16),
        in_specs=[in_vmem] * 2,
        out_specs=in_vmem,
        compiler_params=pltpu.CompilerParams(vmem_limit_bytes=16 << 20),
        name="add",
    )(keep, got)
    weight_grads = pl.pallas_call(
        split_kernel,
        out_shape=(
            jax.ShapeDtypeStruct((width, half), F32),
            jax.ShapeDtypeStruct((width, half), F32),
            jax.ShapeDtypeStruct((width, half), F32),
            jax.ShapeDtypeStruct((half, width), F32),
        ),
        in_specs=[smem] + [in_vmem] * 2,
        out_specs=[in_vmem] * 4,
        name="split",
    )(where, part, other)

    return (back_blocks.reshape(1, rows_dev, half), *weight_grads)


def solution(mesh):
    placed = (
        P(("groups", "day"), "reach", None),
        P(("groups", "day"), "reach", None),
        P(None, "head"),
        P(None, "head"),
        P(None, "head"),
        P("head", None),
        P("groups"),
        P("groups"),
    )
    return jax.shard_map(
        on_device,
        mesh=mesh,
        in_specs=placed,
        out_specs=(
            P(("groups", "day"), "reach", "head"),
            P("groups", "head"),
            P("groups", "head"),
            P("groups", "head"),
            P(("groups", "head"), None),
        ),
        check_vma=False,
    )
```

```python
import jax
import jax.numpy as jnp
from jax import lax
from jax.experimental import pallas as pl
from jax.experimental.pallas import tpu as pltpu
from jax.sharding import PartitionSpec as P

HD = 32
BLOCK = 128
GROUP = 128
CORES = 2
CHUNKS = 2
WORKERS = CORES * CHUNKS
F32 = jnp.float32
BF16 = jnp.bfloat16
PACK = 4
LOG2E = 1.4426950408889634


class Layout:
    def __init__(self, blocks_dev, reach_total):
        self.blocks = blocks_dev
        self.items = blocks_dev // CORES
        self.chunk_items = self.items // CHUNKS
        self.reach = reach_total
        self.slots = max(1, 2 * blocks_dev // reach_total // WORKERS)
        self.places = reach_total * self.slots
        self.block_of = 0
        self.recv_of = self.items
        self.count_own = 2 * self.items
        self.count_partner = 3 * self.items
        self.owner_of = 4 * self.items
        self.item_of = self.owner_of + blocks_dev
        self.core = self.item_of + blocks_dev
        self.later_day = self.core + 1
        self.size = -(-(self.core + 2) // 128) * 128
        self.home_of = 0
        self.chunk_of = blocks_dev
        self.asker_of = 2 * blocks_dev
        self.picks = 3 * blocks_dev
        self.homes_size = -(-(self.picks + CHUNKS * self.places) // 128) * 128


def pick_kernel(lay, partner, where, inputs, sent, homes, held, sem):
    bd, slots = lay.blocks, lay.slots
    reach_pos, core = where[0], where[1]
    copy = pltpu.make_async_copy(inputs, held, sem)
    copy.start()

    def clear_picks(index, carry):
        homes[lay.picks + index] = 0
        return carry

    lax.fori_loop(0, CHUNKS * lay.places, clear_picks, 0, unroll=True)

    def one_reach(peer, carry):
        def before(index, total):
            source = lax.div(partner[peer * bd + index], bd)
            return total + jnp.where(source < reach_pos, 1, 0)

        base = lax.fori_loop(0, bd, before, jnp.int32(0), unroll=True)

        def serve(index, rank):
            wanted = partner[peer * bd + index]
            hit = lax.div(wanted, bd) == reach_pos

            @pl.when(hit)
            def _():
                place = base + rank
                owner = lax.rem(place, CORES)
                chunk = lax.rem(lax.div(place, CORES), CHUNKS)
                slot = peer * slots + jnp.minimum(lax.div(rank, WORKERS), slots - 1)
                local = lax.rem(wanted, bd)
                homes[lay.home_of + local] = slot
                homes[lay.chunk_of + local] = chunk
                homes[lay.asker_of + local] = owner

                @pl.when(owner == core)
                def _():
                    homes[lay.picks + chunk * lay.places + slot] = local

            return rank + jnp.where(hit, 1, 0)

        lax.fori_loop(0, bd, serve, jnp.int32(0))
        return carry

    lax.fori_loop(0, lay.reach, one_reach, 0)
    copy.wait()

    def pick(place, carry):
        sent[place] = held[homes[lay.picks + place]]
        return carry

    lax.fori_loop(0, lay.places, pick, 0)


def deal_kernel(lay, partner, counts, where, homes, inputs, sent, prior, tab, start, used):
    bd, slots = lay.blocks, lay.slots
    reach_pos, core = where[0], where[1]

    def clear(index, carry):
        used[index] = 0
        start[index] = 0
        return carry

    lax.fori_loop(0, lay.reach, clear, 0, unroll=True)

    def count(index, carry):
        source = lax.div(partner[reach_pos * bd + index], bd)
        start[source] = start[source] + 1
        return carry

    lax.fori_loop(0, bd, count, 0)

    def prefix(index, total):
        here = start[index]
        start[index] = total
        return total + here

    lax.fori_loop(0, lay.reach, prefix, jnp.int32(0))

    def assign(index, carry):
        wanted = partner[reach_pos * bd + index]
        source = lax.div(wanted, bd)
        rank = used[source]
        used[source] = rank + 1
        place = start[source] + rank
        owner = lax.rem(place, CORES)
        chunk = lax.rem(lax.div(place, CORES), CHUNKS)
        item = chunk * lay.chunk_items + lax.div(place, WORKERS)
        slot = jnp.minimum(lax.div(rank, WORKERS), slots - 1)
        tab[lay.owner_of + index] = owner
        tab[lay.item_of + index] = item

        @pl.when(owner == core)
        def _():
            tab[lay.block_of + item] = index
            tab[lay.recv_of + item] = source * slots + slot
            tab[lay.count_own + item] = counts[reach_pos * bd + index]
            tab[lay.count_partner + item] = counts[wanted]

        return carry

    lax.fori_loop(0, bd, assign, 0)
    tab[lay.core] = core
    tab[lay.later_day] = where[2]

    def pick(place, carry):
        sent[place] = inputs[homes[lay.picks + lay.places + place]]
        return carry

    def pick_prior(item, carry):
        prior[item] = inputs[tab[lay.block_of + item]]
        return carry

    lax.fori_loop(0, lay.places, pick, 0)
    lax.fori_loop(0, lay.items, pick_prior, 0)


def dot(left, right):
    return lax.dot_general(left, right, (((1,), (0,)), ((), ())), preferred_element_type=F32)


def dot_t(left, right):
    return lax.dot_general(left, right, (((1,), (1,)), ((), ())), preferred_element_type=F32)


def attention_kernel(
    lay,
    chunk,
    tab,
    own_ref,
    up_ref,
    partner_ref,
    prior_ref,
    mine_ref,
    other_ref,
    *refs,
):
    if chunk:
        start_mine_ref, start_other_ref = refs[:2]
        refs = refs[2:]
    own_out_ref, day_ref, home_ref, grad_mine_ref, grad_other_ref = refs
    step = pl.program_id(0)
    item = step + chunk * lay.chunk_items
    factor = HD ** (-0.5)
    own, up = own_ref[0], up_ref[0]
    key_inputs = jnp.concatenate([own, partner_ref[0], prior_ref[0]], axis=0)
    width = own.shape[1]

    @pl.when(step == 0)
    def _():
        if chunk:
            grad_mine_ref[...] = start_mine_ref[...]
            grad_other_ref[...] = start_other_ref[...]
        else:
            grad_mine_ref[...] = jnp.zeros_like(grad_mine_ref)
            grad_other_ref[...] = jnp.zeros_like(grad_other_ref)

    def eye(size):
        rows = lax.broadcasted_iota(jnp.int32, (size, size), 0)
        cols = lax.broadcasted_iota(jnp.int32, (size, size), 1)
        return jnp.where(rows == cols, 1.0, 0.0).astype(BF16)

    query_t = jnp.concatenate([mine_ref[256:384, :], other_ref[256:384, :]], axis=0)
    output_w = jnp.concatenate([mine_ref[384:512, :], other_ref[384:512, :]], axis=0)
    queries = dot_t(own, query_t)
    back_out = dot_t(up, output_w)
    key_inputs_t = key_inputs.T

    count_own = tab[lay.count_own + item]
    count_partner = tab[lay.count_partner + item]
    count_prior = count_own * tab[lay.later_day]
    rows = lax.broadcasted_iota(jnp.int32, (BLOCK, PACK * BLOCK), 0)
    valid = jnp.concatenate([rows < count_own, rows < count_partner, rows < count_prior], axis=0)
    lane_head = lax.broadcasted_iota(jnp.int32, (BLOCK, GROUP), 1) // HD

    per_group = GROUP // HD // PACK
    groups = []
    for group, (weights_ref, grad_ref) in enumerate(
        ((mine_ref, grad_mine_ref), (other_ref, grad_other_ref))
    ):
        kv_t = weights_ref[0:256, :]
        kv = dot_t(key_inputs, kv_t).astype(BF16)
        kv_cols = kv.T
        lanes = slice(group * GROUP, (group + 1) * GROUP)
        groups.append((kv_t, kv, kv_cols, queries[:, lanes], back_out[:, lanes], grad_ref))

    def start(step):
        kv_t, kv, kv_cols, group_queries, group_back, grad_ref = groups[step // per_group]
        heads = [step % per_group * PACK + h for h in range(PACK)]
        query_pack, back_pack = (
            jnp.concatenate([jnp.where(lane_head == h, rows_of, 0.0) for h in heads], axis=0).astype(BF16)
            for rows_of in (group_queries, group_back)
        )
        return query_pack, back_pack, dot_t(kv[:, :GROUP], query_pack), dot_t(kv[:, GROUP:], back_pack)

    def middle(logits, back_weights):
        logits = jnp.where(valid, logits, -1e30)
        highest = jnp.max(logits, axis=0, keepdims=True)
        raised = jnp.exp2((logits - highest) * (factor * LOG2E))
        scale = 1.0 / jnp.sum(raised, axis=0, keepdims=True)
        weights = raised * scale
        center = jnp.sum(weights * back_weights, axis=0, keepdims=True)
        back_logits = (weights * ((back_weights - center) * factor)).astype(BF16)
        return weights.astype(BF16), back_logits

    outputs_t, back_query_t = [], []
    pair_keys, pair_values = {}, {}

    def finish(step, query_pack, back_pack, weights_low, back_logits):
        group = step // per_group
        kv_cols = groups[group][2]
        pair_values.setdefault(group, []).append(dot(weights_low, back_pack))
        pair_keys.setdefault(group, []).append(dot(back_logits, query_pack))
        first = step % per_group * PACK * HD
        size = PACK * HD
        out_t = dot(kv_cols[GROUP + first : GROUP + first + size, :], weights_low)
        query_grad_t = dot(kv_cols[first : first + size, :], back_logits)
        for h in range(PACK):
            lanes = slice(h * BLOCK, (h + 1) * BLOCK)
            outputs_t.append(out_t[h * HD : (h + 1) * HD, lanes])
            back_query_t.append(query_grad_t[h * HD : (h + 1) * HD, lanes])

    total_steps = 2 * per_group
    started = start(0)
    waiting = None
    for step in range(total_steps):
        following = start(step + 1) if step + 1 < total_steps else None
        query_pack, back_pack, logits, back_weights = started
        if waiting is not None:
            finish(*waiting)
        made = middle(logits, back_weights)
        waiting = (step, query_pack, back_pack, *made)
        started = following
    finish(*waiting)

    back_inputs = None
    for group, (kv_t, _, _, _, _, grad_ref) in enumerate(groups):
        back_kv = jnp.concatenate([sum(pair_keys[group][1:], pair_keys[group][0]), sum(pair_values[group][1:], pair_values[group][0])], axis=1).astype(BF16)
        term = dot(back_kv, kv_t)
        back_inputs = term if back_inputs is None else back_inputs + term
        grad_ref[0:256, :] += dot(key_inputs_t, back_kv)

    outputs_t = jnp.concatenate(outputs_t, axis=0).astype(BF16)
    back_query_t = jnp.concatenate(back_query_t, axis=0).astype(BF16)
    query_grad = dot(back_query_t, own)
    output_grad = dot(outputs_t, up)
    grad_mine_ref[256:384, :] += query_grad[:GROUP]
    grad_other_ref[256:384, :] += query_grad[GROUP:]
    grad_mine_ref[384:512, :] += output_grad[:GROUP]
    grad_other_ref[384:512, :] += output_grad[GROUP:]
    back_query = back_query_t.T
    own_out_ref[0] = back_inputs[:BLOCK] + dot(back_query, query_t)
    home_ref[0] = back_inputs[BLOCK : 2 * BLOCK].astype(BF16)
    day_ref[0] = back_inputs[2 * BLOCK :].astype(BF16)


def fold_kernel(lay, tab, homes, own_a, own_b, day_a, day_b, home_a, home_b, keep, give):
    core = tab[lay.core]
    half = keep.shape[2]

    def one(block, carry):
        item = tab[lay.item_of + block]
        mine = tab[lay.owner_of + block] == core
        place = homes[lay.home_of + block]
        asked = homes[lay.asker_of + block] == core
        early = homes[lay.chunk_of + block] == 0
        in_a = item < lay.chunk_items
        item_a = jnp.minimum(item, lay.chunk_items - 1)
        item_b = jnp.maximum(item - lay.chunk_items, 0)
        own = jnp.where(in_a, own_a[item_a], own_b[item_b])
        own += jnp.where(in_a, day_a[item_a].astype(F32), day_b[item_b].astype(F32))
        home = jnp.where(early, home_a[place].astype(F32), home_b[place].astype(F32))
        total = jnp.where(mine, own, 0.0) + jnp.where(asked, home, 0.0)
        low, high = total[:, :half], total[:, half:]
        keep[block] = jnp.where(core == 0, low, high)
        give[block] = jnp.where(core == 0, high, low)
        return carry

    lax.fori_loop(0, lay.blocks, one, 0)


def add_kernel(kept, got, out):
    out[...] = (kept[...] + got[...]).astype(BF16)


def attend(lay, chunk, tab, in_blocks, up_blocks, received, prior_inputs, pack, pack_other, carried):
    width = in_blocks.shape[-1]
    offset = chunk * lay.chunk_items

    def at_item(step, tab):
        return (offset + step, 0, 0)

    def at_block(step, tab):
        return (tab[lay.block_of + offset + step], 0, 0)

    def at_recv(step, tab):
        return (tab[lay.recv_of + offset + step], 0, 0)

    def at_step(step, tab):
        return (step, 0, 0)

    def fixed(step, tab):
        return (0, 0)

    full_block = (1, BLOCK, width)
    weights_block = (4 * GROUP, width)
    in_specs = [
        pl.BlockSpec(full_block, at_block),
        pl.BlockSpec(full_block, at_block),
        pl.BlockSpec(full_block, at_recv),
        pl.BlockSpec(full_block, at_item),
        pl.BlockSpec(weights_block, fixed),
        pl.BlockSpec(weights_block, fixed),
    ]
    operands = [in_blocks, up_blocks, received, prior_inputs, pack, pack_other]
    if chunk:
        in_specs += [pl.BlockSpec(weights_block, fixed)] * 2
        operands += carried
    pieces = lay.chunk_items
    flops = 2 * pieces * (23 * BLOCK * width * width + 24 * BLOCK * 3 * BLOCK * 512)
    return pl.pallas_call(
        lambda *refs: attention_kernel(lay, chunk, *refs),
        grid_spec=pltpu.PrefetchScalarGridSpec(
            num_scalar_prefetch=1,
            grid=(pieces,),
            in_specs=in_specs,
            out_specs=(
                pl.BlockSpec(full_block, at_step),
                pl.BlockSpec(full_block, at_step),
                pl.BlockSpec(full_block, at_recv),
                pl.BlockSpec(weights_block, fixed),
                pl.BlockSpec(weights_block, fixed),
            ),
        ),
        out_shape=(
            pltpu.HBM((pieces, BLOCK, width), F32),
            pltpu.HBM((pieces, BLOCK, width), BF16),
            pltpu.HBM((lay.places, BLOCK, width), BF16),
            pltpu.HBM(weights_block, F32),
            pltpu.HBM(weights_block, F32),
        ),
        compiler_params=pltpu.CompilerParams(vmem_limit_bytes=32 << 20),
        cost_estimate=pl.CostEstimate(
            flops=flops, bytes_accessed=5 << 20, transcendentals=pieces * 8 * BLOCK * 3 * BLOCK
        ),
        name=f"attention_{chunk}",
    )(
        tab,
        *[
            value
            if place == 2
            else pltpu.with_memory_space_constraint(value, pltpu.HBM)
            for place, value in enumerate(operands)
        ],
    )


def exchanged(value, axis, bit):
    count = lax.axis_size(axis)
    return lax.ppermute(value, axis, [(place, place ^ bit) for place in range(count)])


def summed_over(value, axis, bit):
    low = value.astype(BF16)
    return low.astype(F32) + exchanged(low, axis, bit).astype(F32)


def sum_gradients(total, home_b, ring, fold):
    half = total.shape[0] // 2
    first = lax.rem(lax.axis_index("day"), 2) == 0
    kept = jnp.where(first, total[:half], total[half:])
    given = jnp.where(first, total[half:], total[:half])
    given, home_b = lax.optimization_barrier((given.astype(BF16), home_b))
    home_b = ring(home_b)
    part = kept.astype(BF16).astype(F32) + exchanged(given, "day", 1).astype(F32)
    bit = 2
    while bit < lax.axis_size("day"):
        part = summed_over(part, "day", bit)
        bit *= 2
    bit = 1
    while bit < lax.axis_size("reach"):
        part = summed_over(part, "reach", bit)
        bit *= 2
    part = part.astype(BF16)
    keep, give = fold(home_b)
    other, give = lax.optimization_barrier((exchanged(part, "day", 1), give))
    return part, other, keep, give


def split_kernel(where, part, other, query_out, key_out, value_out, output_out):
    first = lax.rem(where[3], 2) == 0
    mine, theirs = part[...].astype(F32), other[...].astype(F32)
    upper = jnp.where(first, mine, theirs)
    lower = jnp.where(first, theirs, mine)
    key_out[...] = upper[:, :GROUP]
    value_out[...] = upper[:, GROUP:]
    query_out[...] = lower[:GROUP].T
    output_out[...] = lower[GROUP:]


def on_device(
    inputs, upstream, query_weight, key_weight, value_weight, output_weight, partner, counts
):
    days_dev, rows_dev, width = inputs.shape
    assert days_dev == 1 and width == 2 * GROUP
    blocks_dev = rows_dev // BLOCK
    reach_total = lax.axis_size("reach")
    day_total = lax.axis_size("day")
    assert lax.axis_size("head") == CORES
    lay = Layout(blocks_dev, reach_total)
    half = width // 2
    in_blocks = inputs.reshape(blocks_dev, BLOCK, width)
    up_blocks = upstream.reshape(blocks_dev, BLOCK, width)
    where = jnp.stack(
        [
            lax.axis_index("reach"),
            lax.axis_index("head"),
            (lax.axis_index("day") > 0).astype(jnp.int32),
            lax.axis_index("day"),
        ]
    )
    pack = jnp.concatenate([key_weight.T, value_weight.T, query_weight.T, output_weight], axis=0)
    pack_other = exchanged(pack, "head", 1)

    smem = pl.BlockSpec(memory_space=pltpu.SMEM)
    in_vmem = pl.BlockSpec(memory_space=pltpu.VMEM)
    anywhere = pl.BlockSpec(memory_space=pl.ANY)
    sent_shape = jax.ShapeDtypeStruct((lay.places, BLOCK, width), BF16)
    sent_a, homes = pl.pallas_call(
        lambda *refs: pick_kernel(lay, *refs),
        out_shape=(sent_shape, jax.ShapeDtypeStruct((lay.homes_size,), jnp.int32)),
        in_specs=[smem, smem, anywhere],
        out_specs=(in_vmem, smem),
        scratch_shapes=[
            pltpu.VMEM((blocks_dev, BLOCK, width), BF16),
            pltpu.SemaphoreType.DMA,
        ],
        compiler_params=pltpu.CompilerParams(vmem_limit_bytes=16 << 20),
        name="pick",
    )(partner, where, pltpu.with_memory_space_constraint(in_blocks, pltpu.HBM))
    sent_b, prior, tab = pl.pallas_call(
        lambda *refs: deal_kernel(lay, *refs),
        out_shape=(
            sent_shape,
            jax.ShapeDtypeStruct((lay.items, BLOCK, width), BF16),
            jax.ShapeDtypeStruct((lay.size,), jnp.int32),
        ),
        in_specs=[smem, smem, smem, smem, in_vmem],
        out_specs=(in_vmem, in_vmem, smem),
        scratch_shapes=[
            pltpu.SMEM((lay.reach,), jnp.int32),
            pltpu.SMEM((lay.reach,), jnp.int32),
        ],
        compiler_params=pltpu.CompilerParams(vmem_limit_bytes=16 << 20),
        name="deal",
    )(partner, counts, where, homes, in_blocks)

    def ring(value):
        shape = value.shape
        value = value.reshape(lay.reach, lay.slots * BLOCK, width)
        return lax.all_to_all(value, "reach", 0, 0, tiled=True).reshape(shape)

    next_day = [(d, d + 1) for d in range(day_total - 1)]
    last_day = [(d + 1, d) for d in range(day_total - 1)]
    received_a = ring(sent_a)
    prior_inputs = lax.ppermute(prior, "day", next_day)
    received_b = ring(sent_b)
    shared = (prior_inputs, pack, pack_other)
    own_a, day_a, home_a, *grads = attend(
        lay, 0, tab, in_blocks, up_blocks, received_a, *shared, None
    )
    home_a = ring(home_a)
    day_a = lax.ppermute(day_a, "day", last_day)
    own_b, day_b, home_b, grad_mine, grad_other = attend(
        lay, 1, tab, in_blocks, up_blocks, received_b, *shared, grads
    )
    home_a, day_a, home_b, day_b, grad_other = lax.optimization_barrier(
        (home_a, day_a, home_b, day_b, grad_other)
    )
    grad_swapped = exchanged(grad_other, "head", 1)
    day_b = lax.ppermute(day_b, "day", last_day)
    half_shape = jax.ShapeDtypeStruct((blocks_dev, BLOCK, half), F32)

    def fold(home_b):
        return pl.pallas_call(
            lambda *refs: fold_kernel(lay, *refs),
            out_shape=(half_shape, half_shape),
            in_specs=[smem] * 2 + [in_vmem] * 6,
            out_specs=[in_vmem] * 2,
            compiler_params=pltpu.CompilerParams(vmem_limit_bytes=16 << 20),
            name="fold",
        )(tab, homes, own_a, own_b, day_a, day_b, home_a, home_b)

    part, other, keep, give = sum_gradients(
        grad_mine + grad_swapped, home_b, ring, fold
    )
    got = exchanged(give, "head", 1)
    back_blocks = pl.pallas_call(
        add_kernel,
        out_shape=jax.ShapeDtypeStruct((blocks_dev, BLOCK, half), BF16),
        in_specs=[in_vmem] * 2,
        out_specs=in_vmem,
        compiler_params=pltpu.CompilerParams(vmem_limit_bytes=16 << 20),
        name="add",
    )(keep, got)
    weight_grads = pl.pallas_call(
        split_kernel,
        out_shape=(
            jax.ShapeDtypeStruct((width, half), F32),
            jax.ShapeDtypeStruct((width, half), F32),
            jax.ShapeDtypeStruct((width, half), F32),
            jax.ShapeDtypeStruct((half, width), F32),
        ),
        in_specs=[smem] + [in_vmem] * 2,
        out_specs=[in_vmem] * 4,
        name="split",
    )(where, part, other)

    return (back_blocks.reshape(1, rows_dev, half), *weight_grads)


def solution(mesh):
    placed = (
        P(("groups", "day"), "reach", None),
        P(("groups", "day"), "reach", None),
        P(None, "head"),
        P(None, "head"),
        P(None, "head"),
        P("head", None),
        P("groups"),
        P("groups"),
    )
    return jax.shard_map(
        on_device,
        mesh=mesh,
        in_specs=placed,
        out_specs=(
            P(("groups", "day"), "reach", "head"),
            P("groups", "head"),
            P("groups", "head"),
            P("groups", "head"),
            P(("groups", "head"), None),
        ),
        check_vma=False,
    )
```

```python
import jax
import jax.numpy as jnp
from jax import lax
from jax.experimental import pallas as pl
from jax.experimental.pallas import tpu as pltpu
from jax.sharding import PartitionSpec as P

HD = 32
BLOCK = 128
GROUP = 128
CORES = 2
CHUNKS = 2
WORKERS = CORES * CHUNKS
F32 = jnp.float32
BF16 = jnp.bfloat16
PACK = 4
LOG2E = 1.4426950408889634


class Layout:
    def __init__(self, blocks_dev, reach_total):
        self.blocks = blocks_dev
        self.items = blocks_dev // CORES
        self.chunk_items = self.items // CHUNKS
        self.reach = reach_total
        self.slots = max(1, 2 * blocks_dev // reach_total // WORKERS)
        self.places = reach_total * self.slots
        self.block_of = 0
        self.recv_of = self.items
        self.count_own = 2 * self.items
        self.count_partner = 3 * self.items
        self.owner_of = 4 * self.items
        self.item_of = self.owner_of + blocks_dev
        self.core = self.item_of + blocks_dev
        self.later_day = self.core + 1
        self.size = -(-(self.core + 2) // 128) * 128
        self.spare = blocks_dev
        self.home_of = 0
        self.chunk_of = blocks_dev + 1
        self.asker_of = 2 * (blocks_dev + 1)
        self.picks = 3 * (blocks_dev + 1)
        self.spare_pick = self.picks + CHUNKS * self.places
        self.homes_size = -(-(self.spare_pick + 1) // 128) * 128


def pick_kernel(lay, partner_hbm, inputs, sent, homes, partner, held, sems):
    bd, slots = lay.blocks, lay.slots
    reach_pos, core = lax.axis_index("reach"), lax.axis_index("head")
    table_copy = pltpu.make_async_copy(partner_hbm, partner, sems.at[0])
    table_copy.start()
    copy = pltpu.make_async_copy(inputs, held, sems.at[1])
    copy.start()
    for place in range(CHUNKS * lay.places):
        homes[lay.picks + place] = 0
    table_copy.wait()

    def one_reach(peer, carry):
        base = jnp.int32(0)
        wanted = []
        for index in range(bd):
            block = partner[peer * bd + index]
            source = lax.div(block, bd)
            base = base + jnp.where(source < reach_pos, 1, 0)
            wanted.append((source == reach_pos, lax.rem(block, bd)))
        rank = jnp.int32(0)
        for hit, local in wanted:
            place = base + rank
            owner = lax.rem(place, CORES)
            chunk = lax.rem(lax.div(place, CORES), CHUNKS)
            slot = peer * slots + jnp.minimum(lax.div(rank, WORKERS), slots - 1)
            target = jnp.where(hit, local, lay.spare)
            homes[lay.home_of + target] = slot
            homes[lay.chunk_of + target] = chunk
            homes[lay.asker_of + target] = owner
            pick = lay.picks + chunk * lay.places + slot
            homes[jnp.where(hit & (owner == core), pick, lay.spare_pick)] = local
            rank = rank + jnp.where(hit, 1, 0)
        return carry

    lax.fori_loop(0, lay.reach, one_reach, 0)
    copy.wait()
    for place in range(lay.places):
        sent[place] = held[homes[lay.picks + place]]


def deal_kernel(lay, partner, counts, homes, inputs, sent, prior, tab, start, used):
    bd, slots = lay.blocks, lay.slots
    reach_pos, core = lax.axis_index("reach"), lax.axis_index("head")

    def clear(index, carry):
        used[index] = 0
        start[index] = 0
        return carry

    lax.fori_loop(0, lay.reach, clear, 0, unroll=True)

    def count(index, carry):
        source = lax.div(partner[reach_pos * bd + index], bd)
        start[source] = start[source] + 1
        return carry

    lax.fori_loop(0, bd, count, 0)

    def prefix(index, total):
        here = start[index]
        start[index] = total
        return total + here

    lax.fori_loop(0, lay.reach, prefix, jnp.int32(0))

    def assign(index, carry):
        wanted = partner[reach_pos * bd + index]
        source = lax.div(wanted, bd)
        rank = used[source]
        used[source] = rank + 1
        place = start[source] + rank
        owner = lax.rem(place, CORES)
        chunk = lax.rem(lax.div(place, CORES), CHUNKS)
        item = chunk * lay.chunk_items + lax.div(place, WORKERS)
        slot = jnp.minimum(lax.div(rank, WORKERS), slots - 1)
        tab[lay.owner_of + index] = owner
        tab[lay.item_of + index] = item

        @pl.when(owner == core)
        def _():
            tab[lay.block_of + item] = index
            tab[lay.recv_of + item] = source * slots + slot
            tab[lay.count_own + item] = counts[reach_pos * bd + index]
            tab[lay.count_partner + item] = counts[wanted]

        return carry

    lax.fori_loop(0, bd, assign, 0)
    tab[lay.core] = core
    tab[lay.later_day] = jnp.where(lax.axis_index("day") > 0, 1, 0)

    def pick(place, carry):
        sent[place] = inputs[homes[lay.picks + lay.places + place]]
        return carry

    def pick_prior(item, carry):
        prior[item] = inputs[tab[lay.block_of + item]]
        return carry

    lax.fori_loop(0, lay.places, pick, 0)
    lax.fori_loop(0, lay.items, pick_prior, 0)


def dot(left, right):
    return lax.dot_general(left, right, (((1,), (0,)), ((), ())), preferred_element_type=F32)


def dot_t(left, right):
    return lax.dot_general(left, right, (((1,), (1,)), ((), ())), preferred_element_type=F32)


def attention_kernel(
    lay,
    chunk,
    tab,
    own_ref,
    up_ref,
    partner_ref,
    prior_ref,
    mine_ref,
    other_ref,
    *refs,
):
    if chunk:
        start_mine_ref, start_other_ref = refs[:2]
        refs = refs[2:]
    own_out_ref, day_ref, home_ref, grad_mine_ref, grad_other_ref = refs
    step = pl.program_id(0)
    item = step + chunk * lay.chunk_items
    factor = HD ** (-0.5)
    own, up = own_ref[0], up_ref[0]
    key_inputs = jnp.concatenate([own, partner_ref[0], prior_ref[0]], axis=0)
    width = own.shape[1]

    @pl.when(step == 0)
    def _():
        if chunk:
            grad_mine_ref[...] = start_mine_ref[...]
            grad_other_ref[...] = start_other_ref[...]
        else:
            grad_mine_ref[...] = jnp.zeros_like(grad_mine_ref)
            grad_other_ref[...] = jnp.zeros_like(grad_other_ref)

    def eye(size):
        rows = lax.broadcasted_iota(jnp.int32, (size, size), 0)
        cols = lax.broadcasted_iota(jnp.int32, (size, size), 1)
        return jnp.where(rows == cols, 1.0, 0.0).astype(BF16)

    query_t = jnp.concatenate([mine_ref[256:384, :], other_ref[256:384, :]], axis=0)
    output_w = jnp.concatenate([mine_ref[384:512, :], other_ref[384:512, :]], axis=0)
    queries = dot_t(own, query_t)
    back_out = dot_t(up, output_w)
    key_inputs_t = key_inputs.T

    count_own = tab[lay.count_own + item]
    count_partner = tab[lay.count_partner + item]
    count_prior = count_own * tab[lay.later_day]
    rows = lax.broadcasted_iota(jnp.int32, (BLOCK, PACK * BLOCK), 0)
    valid = jnp.concatenate([rows < count_own, rows < count_partner, rows < count_prior], axis=0)
    lane_head = lax.broadcasted_iota(jnp.int32, (BLOCK, GROUP), 1) // HD

    per_group = GROUP // HD // PACK
    groups = []
    for group, (weights_ref, grad_ref) in enumerate(
        ((mine_ref, grad_mine_ref), (other_ref, grad_other_ref))
    ):
        kv_t = weights_ref[0:256, :]
        kv = dot_t(key_inputs, kv_t).astype(BF16)
        kv_cols = kv.T
        lanes = slice(group * GROUP, (group + 1) * GROUP)
        groups.append((kv_t, kv, kv_cols, queries[:, lanes], back_out[:, lanes], grad_ref))

    def start(step):
        kv_t, kv, kv_cols, group_queries, group_back, grad_ref = groups[step // per_group]
        heads = [step % per_group * PACK + h for h in range(PACK)]
        query_pack, back_pack = (
            jnp.concatenate([jnp.where(lane_head == h, rows_of, 0.0) for h in heads], axis=0).astype(BF16)
            for rows_of in (group_queries, group_back)
        )
        return query_pack, back_pack, dot_t(kv[:, :GROUP], query_pack), dot_t(kv[:, GROUP:], back_pack)

    def middle(logits, back_weights):
        logits = jnp.where(valid, logits, -1e30)
        highest = jnp.max(logits, axis=0, keepdims=True)
        raised = jnp.exp2((logits - highest) * (factor * LOG2E))
        scale = 1.0 / jnp.sum(raised, axis=0, keepdims=True)
        weights = raised * scale
        center = jnp.sum(weights * back_weights, axis=0, keepdims=True)
        back_logits = (weights * ((back_weights - center) * factor)).astype(BF16)
        return weights.astype(BF16), back_logits

    outputs_t, back_query_t = [], []
    pair_keys, pair_values = {}, {}

    def finish(step, query_pack, back_pack, weights_low, back_logits):
        group = step // per_group
        kv_cols = groups[group][2]
        pair_values.setdefault(group, []).append(dot(weights_low, back_pack))
        pair_keys.setdefault(group, []).append(dot(back_logits, query_pack))
        first = step % per_group * PACK * HD
        size = PACK * HD
        out_t = dot(kv_cols[GROUP + first : GROUP + first + size, :], weights_low)
        query_grad_t = dot(kv_cols[first : first + size, :], back_logits)
        for h in range(PACK):
            lanes = slice(h * BLOCK, (h + 1) * BLOCK)
            outputs_t.append(out_t[h * HD : (h + 1) * HD, lanes])
            back_query_t.append(query_grad_t[h * HD : (h + 1) * HD, lanes])

    total_steps = 2 * per_group
    started = start(0)
    waiting = None
    for step in range(total_steps):
        following = start(step + 1) if step + 1 < total_steps else None
        query_pack, back_pack, logits, back_weights = started
        if waiting is not None:
            finish(*waiting)
        made = middle(logits, back_weights)
        waiting = (step, query_pack, back_pack, *made)
        started = following
    finish(*waiting)

    back_inputs = None
    for group, (kv_t, _, _, _, _, grad_ref) in enumerate(groups):
        back_kv = jnp.concatenate([sum(pair_keys[group][1:], pair_keys[group][0]), sum(pair_values[group][1:], pair_values[group][0])], axis=1).astype(BF16)
        term = dot(back_kv, kv_t)
        back_inputs = term if back_inputs is None else back_inputs + term
        grad_ref[0:256, :] += dot(key_inputs_t, back_kv)

    outputs_t = jnp.concatenate(outputs_t, axis=0).astype(BF16)
    back_query_t = jnp.concatenate(back_query_t, axis=0).astype(BF16)
    query_grad = dot(back_query_t, own)
    output_grad = dot(outputs_t, up)
    grad_mine_ref[256:384, :] += query_grad[:GROUP]
    grad_other_ref[256:384, :] += query_grad[GROUP:]
    grad_mine_ref[384:512, :] += output_grad[:GROUP]
    grad_other_ref[384:512, :] += output_grad[GROUP:]
    back_query = back_query_t.T
    own_out_ref[0] = back_inputs[:BLOCK] + dot(back_query, query_t)
    home_ref[0] = back_inputs[BLOCK : 2 * BLOCK].astype(BF16)
    day_ref[0] = back_inputs[2 * BLOCK :].astype(BF16)


def fold_kernel(lay, tab, homes, own_a, own_b, day_a, day_b, home_a, home_b, keep, give):
    core = tab[lay.core]
    half = keep.shape[2]

    def one(block, carry):
        item = tab[lay.item_of + block]
        mine = tab[lay.owner_of + block] == core
        place = homes[lay.home_of + block]
        asked = homes[lay.asker_of + block] == core
        early = homes[lay.chunk_of + block] == 0
        in_a = item < lay.chunk_items
        item_a = jnp.minimum(item, lay.chunk_items - 1)
        item_b = jnp.maximum(item - lay.chunk_items, 0)
        own = jnp.where(in_a, own_a[item_a], own_b[item_b])
        own += jnp.where(in_a, day_a[item_a].astype(F32), day_b[item_b].astype(F32))
        home = jnp.where(early, home_a[place].astype(F32), home_b[place].astype(F32))
        total = jnp.where(mine, own, 0.0) + jnp.where(asked, home, 0.0)
        low, high = total[:, :half], total[:, half:]
        keep[block] = jnp.where(core == 0, low, high)
        give[block] = jnp.where(core == 0, high, low)
        return carry

    lax.fori_loop(0, lay.blocks, one, 0)


def add_kernel(kept, got, out):
    out[...] = (kept[...] + got[...]).astype(BF16)


def attend(lay, chunk, tab, in_blocks, up_blocks, received, prior_inputs, pack, pack_other, carried):
    width = in_blocks.shape[-1]
    offset = chunk * lay.chunk_items

    def at_item(step, tab):
        return (offset + step, 0, 0)

    def at_block(step, tab):
        return (tab[lay.block_of + offset + step], 0, 0)

    def at_recv(step, tab):
        return (tab[lay.recv_of + offset + step], 0, 0)

    def at_step(step, tab):
        return (step, 0, 0)

    def fixed(step, tab):
        return (0, 0)

    full_block = (1, BLOCK, width)
    weights_block = (4 * GROUP, width)
    in_specs = [
        pl.BlockSpec(full_block, at_block),
        pl.BlockSpec(full_block, at_block),
        pl.BlockSpec(full_block, at_recv),
        pl.BlockSpec(full_block, at_item),
        pl.BlockSpec(weights_block, fixed),
        pl.BlockSpec(weights_block, fixed),
    ]
    operands = [in_blocks, up_blocks, received, prior_inputs, pack, pack_other]
    if chunk:
        in_specs += [pl.BlockSpec(weights_block, fixed)] * 2
        operands += carried
    pieces = lay.chunk_items
    flops = 2 * pieces * (23 * BLOCK * width * width + 24 * BLOCK * 3 * BLOCK * 512)
    return pl.pallas_call(
        lambda *refs: attention_kernel(lay, chunk, *refs),
        grid_spec=pltpu.PrefetchScalarGridSpec(
            num_scalar_prefetch=1,
            grid=(pieces,),
            in_specs=in_specs,
            out_specs=(
                pl.BlockSpec(full_block, at_step),
                pl.BlockSpec(full_block, at_step),
                pl.BlockSpec(full_block, at_recv),
                pl.BlockSpec(weights_block, fixed),
                pl.BlockSpec(weights_block, fixed),
            ),
        ),
        out_shape=(
            pltpu.HBM((pieces, BLOCK, width), F32),
            pltpu.HBM((pieces, BLOCK, width), BF16),
            pltpu.HBM((lay.places, BLOCK, width), BF16),
            pltpu.HBM(weights_block, F32),
            pltpu.HBM(weights_block, F32),
        ),
        compiler_params=pltpu.CompilerParams(vmem_limit_bytes=32 << 20),
        cost_estimate=pl.CostEstimate(
            flops=flops, bytes_accessed=5 << 20, transcendentals=pieces * 8 * BLOCK * 3 * BLOCK
        ),
        name=f"attention_{chunk}",
    )(
        tab,
        *[
            value
            if place == 2
            else pltpu.with_memory_space_constraint(value, pltpu.HBM)
            for place, value in enumerate(operands)
        ],
    )


def exchanged(value, axis, bit):
    count = lax.axis_size(axis)
    return lax.ppermute(value, axis, [(place, place ^ bit) for place in range(count)])


def summed_over(value, axis, bit):
    low = value.astype(BF16)
    return low.astype(F32) + exchanged(low, axis, bit).astype(F32)


def sum_gradients(total, home_b, fold):
    half = total.shape[0] // 2
    first = lax.rem(lax.axis_index("day"), 2) == 0
    kept = jnp.where(first, total[:half], total[half:])
    given = jnp.where(first, total[half:], total[:half])
    part = kept.astype(BF16).astype(F32) + exchanged(given.astype(BF16), "day", 1).astype(F32)
    bit = 2
    while bit < lax.axis_size("day"):
        part = summed_over(part, "day", bit)
        bit *= 2
    bit = 1
    while bit < lax.axis_size("reach"):
        part = summed_over(part, "reach", bit)
        if bit == 1:
            part, home_b = lax.optimization_barrier((part, home_b))
        bit *= 2
    part, folded = lax.optimization_barrier((part.astype(BF16), fold(home_b)))
    return part, exchanged(part, "day", 1), folded


def split_kernel(part, other, query_out, key_out, value_out, output_out):
    first = lax.rem(lax.axis_index("day"), 2) == 0
    mine, theirs = part[...].astype(F32), other[...].astype(F32)
    upper = jnp.where(first, mine, theirs)
    lower = jnp.where(first, theirs, mine)
    key_out[...] = upper[:, :GROUP]
    value_out[...] = upper[:, GROUP:]
    query_out[...] = lower[:GROUP].T
    output_out[...] = lower[GROUP:]


def on_device(
    inputs, upstream, query_weight, key_weight, value_weight, output_weight, partner, counts
):
    days_dev, rows_dev, width = inputs.shape
    assert days_dev == 1 and width == 2 * GROUP
    blocks_dev = rows_dev // BLOCK
    reach_total = lax.axis_size("reach")
    day_total = lax.axis_size("day")
    assert lax.axis_size("head") == CORES
    lay = Layout(blocks_dev, reach_total)
    half = width // 2
    in_blocks = inputs.reshape(blocks_dev, BLOCK, width)
    up_blocks = upstream.reshape(blocks_dev, BLOCK, width)
    pack = jnp.concatenate([key_weight.T, value_weight.T, query_weight.T, output_weight], axis=0)
    pack_other = exchanged(pack, "head", 1)

    smem = pl.BlockSpec(memory_space=pltpu.SMEM)
    in_vmem = pl.BlockSpec(memory_space=pltpu.VMEM)
    anywhere = pl.BlockSpec(memory_space=pl.ANY)
    sent_shape = jax.ShapeDtypeStruct((lay.places, BLOCK, width), BF16)
    sent_a, homes = pl.pallas_call(
        lambda *refs: pick_kernel(lay, *refs),
        out_shape=(sent_shape, jax.ShapeDtypeStruct((lay.homes_size,), jnp.int32)),
        in_specs=[anywhere, anywhere],
        out_specs=(in_vmem, smem),
        scratch_shapes=[
            pltpu.SMEM(partner.shape, jnp.int32),
            pltpu.VMEM((blocks_dev, BLOCK, width), BF16),
            pltpu.SemaphoreType.DMA((2,)),
        ],
        compiler_params=pltpu.CompilerParams(vmem_limit_bytes=16 << 20),
        name="pick",
    )(
        pltpu.with_memory_space_constraint(partner, pltpu.HBM),
        pltpu.with_memory_space_constraint(in_blocks, pltpu.HBM),
    )
    sent_b, prior, tab = pl.pallas_call(
        lambda *refs: deal_kernel(lay, *refs),
        out_shape=(
            sent_shape,
            jax.ShapeDtypeStruct((lay.items, BLOCK, width), BF16),
            jax.ShapeDtypeStruct((lay.size,), jnp.int32),
        ),
        in_specs=[smem, smem, smem, in_vmem],
        out_specs=(in_vmem, in_vmem, smem),
        scratch_shapes=[
            pltpu.SMEM((lay.reach,), jnp.int32),
            pltpu.SMEM((lay.reach,), jnp.int32),
        ],
        compiler_params=pltpu.CompilerParams(vmem_limit_bytes=16 << 20),
        name="deal",
    )(partner, counts, homes, in_blocks)

    def ring(value):
        shape = value.shape
        value = value.reshape(lay.reach, lay.slots * BLOCK, width)
        return lax.all_to_all(value, "reach", 0, 0, tiled=True).reshape(shape)

    next_day = [(d, d + 1) for d in range(day_total - 1)]
    last_day = [(d + 1, d) for d in range(day_total - 1)]
    received_a = ring(sent_a)
    prior_inputs = lax.ppermute(prior, "day", next_day)
    received_b = ring(sent_b)
    shared = (prior_inputs, pack, pack_other)
    own_a, day_a, home_a, *grads = attend(
        lay, 0, tab, in_blocks, up_blocks, received_a, *shared, None
    )
    home_a = ring(home_a)
    day_a = lax.ppermute(day_a, "day", last_day)
    own_b, day_b, home_b, grad_mine, grad_other = attend(
        lay, 1, tab, in_blocks, up_blocks, received_b, *shared, grads
    )
    home_a, home_b, day_b, grad_other = lax.optimization_barrier(
        (home_a, home_b, day_b, grad_other)
    )
    grad_swapped = exchanged(grad_other, "head", 1)
    home_b = ring(home_b)
    day_b = lax.ppermute(day_b, "day", last_day)
    half_shape = jax.ShapeDtypeStruct((blocks_dev, BLOCK, half), F32)

    def fold(home_b):
        return pl.pallas_call(
            lambda *refs: fold_kernel(lay, *refs),
            out_shape=(half_shape, half_shape),
            in_specs=[smem] * 2 + [in_vmem] * 6,
            out_specs=[in_vmem] * 2,
            compiler_params=pltpu.CompilerParams(vmem_limit_bytes=16 << 20),
            name="fold",
        )(tab, homes, own_a, own_b, day_a, day_b, home_a, home_b)

    part, other, (keep, give) = sum_gradients(grad_mine + grad_swapped, home_b, fold)
    got = exchanged(give, "head", 1)
    back_blocks = pl.pallas_call(
        add_kernel,
        out_shape=jax.ShapeDtypeStruct((blocks_dev, BLOCK, half), BF16),
        in_specs=[in_vmem] * 2,
        out_specs=in_vmem,
        compiler_params=pltpu.CompilerParams(vmem_limit_bytes=16 << 20),
        name="add",
    )(keep, got)
    back_blocks, other = lax.optimization_barrier((back_blocks, other))
    weight_grads = pl.pallas_call(
        split_kernel,
        out_shape=(
            jax.ShapeDtypeStruct((width, half), F32),
            jax.ShapeDtypeStruct((width, half), F32),
            jax.ShapeDtypeStruct((width, half), F32),
            jax.ShapeDtypeStruct((half, width), F32),
        ),
        grid=(1,),
        name="split",
    )(part, other)

    return (back_blocks.reshape(1, rows_dev, half), *weight_grads)


def solution(mesh):
    placed = (
        P(("groups", "day"), "reach", None),
        P(("groups", "day"), "reach", None),
        P(None, "head"),
        P(None, "head"),
        P(None, "head"),
        P("head", None),
        P("groups"),
        P("groups"),
    )
    return jax.shard_map(
        on_device,
        mesh=mesh,
        in_specs=placed,
        out_specs=(
            P(("groups", "day"), "reach", "head"),
            P("groups", "head"),
            P("groups", "head"),
            P("groups", "head"),
            P(("groups", "head"), None),
        ),
        check_vma=False,
    )
```

```python
import jax
import jax.numpy as jnp
from jax import lax
from jax.experimental import pallas as pl
from jax.experimental.pallas import tpu as pltpu
from jax.sharding import PartitionSpec as P

HD = 32
BLOCK = 128
GROUP = 128
CORES = 2
F32 = jnp.float32
BF16 = jnp.bfloat16
PACK = 4
STEP_ITEMS = 4
LOG2E = 1.4426950408889634


class Layout:
    def __init__(self, blocks_dev, reach_total):
        self.blocks = blocks_dev
        self.items = blocks_dev // CORES
        self.reach = reach_total
        self.slots = max(1, 2 * blocks_dev // reach_total // CORES)
        self.places = reach_total * self.slots
        self.block_of = 0
        self.recv_of = self.items
        self.count_own = 2 * self.items
        self.count_partner = 3 * self.items
        self.owner_of = 4 * self.items
        self.item_of = self.owner_of + blocks_dev
        self.later_day = self.item_of + blocks_dev
        self.size = -(-(self.later_day + 1) // 128) * 128
        self.spare = blocks_dev
        self.home_of = 0
        self.asker_of = blocks_dev + 1
        self.picks = 2 * (blocks_dev + 1)
        self.spare_pick = self.picks + self.places
        self.homes_size = -(-(self.spare_pick + 1) // 128) * 128


def pick_kernel(lay, partner_hbm, inputs, sent, homes, partner, held, sems):
    bd, slots = lay.blocks, lay.slots
    reach_pos, core = lax.axis_index("reach"), lax.axis_index("head")
    table_copy = pltpu.make_async_copy(partner_hbm, partner, sems.at[0])
    table_copy.start()
    copy = pltpu.make_async_copy(inputs, held, sems.at[1])
    copy.start()
    for place in range(lay.places):
        homes[lay.picks + place] = 0
    table_copy.wait()

    def one_reach(peer, carry):
        base = jnp.int32(0)
        wanted = []
        for index in range(bd):
            block = partner[peer * bd + index]
            source = lax.div(block, bd)
            base = base + jnp.where(source < reach_pos, 1, 0)
            wanted.append((source == reach_pos, lax.rem(block, bd)))
        rank = jnp.int32(0)
        for hit, local in wanted:
            place = base + rank
            owner = lax.rem(place, CORES)
            slot = peer * slots + jnp.minimum(lax.div(rank, CORES), slots - 1)
            target = jnp.where(hit, local, lay.spare)
            homes[lay.home_of + target] = slot
            homes[lay.asker_of + target] = owner
            homes[jnp.where(hit & (owner == core), lay.picks + slot, lay.spare_pick)] = local
            rank = rank + jnp.where(hit, 1, 0)
        return carry

    lax.fori_loop(0, lay.reach, one_reach, 0)
    copy.wait()
    for place in range(lay.places):
        sent[place] = held[homes[lay.picks + place]]


def deal_kernel(lay, partner, counts, inputs, prior, tab, start, used):
    bd, slots = lay.blocks, lay.slots
    reach_pos, core = lax.axis_index("reach"), lax.axis_index("head")

    def clear(index, carry):
        used[index] = 0
        start[index] = 0
        return carry

    lax.fori_loop(0, lay.reach, clear, 0, unroll=True)

    def count(index, carry):
        source = lax.div(partner[reach_pos * bd + index], bd)
        start[source] = start[source] + 1
        return carry

    lax.fori_loop(0, bd, count, 0)

    def prefix(index, total):
        here = start[index]
        start[index] = total
        return total + here

    lax.fori_loop(0, lay.reach, prefix, jnp.int32(0))

    def assign(index, carry):
        wanted = partner[reach_pos * bd + index]
        source = lax.div(wanted, bd)
        rank = used[source]
        used[source] = rank + 1
        place = start[source] + rank
        owner = lax.rem(place, CORES)
        item = lax.div(place, CORES)
        slot = jnp.minimum(lax.div(rank, CORES), slots - 1)
        tab[lay.owner_of + index] = owner
        tab[lay.item_of + index] = item

        @pl.when(owner == core)
        def _():
            tab[lay.block_of + item] = index
            tab[lay.recv_of + item] = source * slots + slot
            tab[lay.count_own + item] = counts[reach_pos * bd + index]
            tab[lay.count_partner + item] = counts[wanted]

        return carry

    lax.fori_loop(0, bd, assign, 0)
    tab[lay.later_day] = jnp.where(lax.axis_index("day") > 0, 1, 0)

    def pick_prior(item, carry):
        prior[item] = inputs[tab[lay.block_of + item]]
        return carry

    lax.fori_loop(0, lay.items, pick_prior, 0)


def dot(left, right):
    return lax.dot_general(left, right, (((1,), (0,)), ((), ())), preferred_element_type=F32)


def dot_t(left, right):
    return lax.dot_general(left, right, (((1,), (1,)), ((), ())), preferred_element_type=F32)


def attention_kernel(lay, tab, *refs):
    step = pl.program_id(0)
    read, refs = refs[: 4 * STEP_ITEMS], refs[4 * STEP_ITEMS :]
    mine_ref, other_ref, *refs = refs
    own_out_ref, day_ref, home_ref, grad_mine_ref, grad_other_ref = refs
    factor = HD ** (-0.5)
    per_group = GROUP // HD // PACK

    @pl.when(step == 0)
    def _():
        grad_mine_ref[...] = jnp.zeros_like(grad_mine_ref)
        grad_other_ref[...] = jnp.zeros_like(grad_other_ref)

    rows = lax.broadcasted_iota(jnp.int32, (BLOCK, PACK * BLOCK), 0)
    lane_head = lax.broadcasted_iota(jnp.int32, (BLOCK, GROUP), 1) // HD
    query_t = jnp.concatenate([mine_ref[256:384, :], other_ref[256:384, :]], axis=0)
    output_w = jnp.concatenate([mine_ref[384:512, :], other_ref[384:512, :]], axis=0)

    class Item:
        pass

    def begin(place):
        it = Item()
        own_ref, up_ref, partner_ref, prior_ref = read[4 * place : 4 * place + 4]
        it.place = place
        item = step * STEP_ITEMS + place
        it.item = item
        it.own, it.up = own_ref[0], up_ref[0]
        it.inputs = jnp.concatenate([it.own, partner_ref[0], prior_ref[0]], axis=0)
        queries = dot_t(it.own, query_t)
        back_out = dot_t(it.up, output_w)
        count_own = tab[lay.count_own + item]
        it.counts = (count_own, tab[lay.count_partner + item], count_own * tab[lay.later_day])
        it.groups = []
        for group, weights_ref in enumerate((mine_ref, other_ref)):
            kv_t = weights_ref[0:256, :]
            kv = dot_t(it.inputs, kv_t).astype(BF16)
            lanes = slice(group * GROUP, (group + 1) * GROUP)
            it.groups.append((kv_t, kv, kv.T, queries[:, lanes], back_out[:, lanes]))
        it.outputs_t, it.back_query_t = [], []
        it.keys, it.values = ([], []), ([], [])
        return it

    def start(it, part):
        _, kv, _, group_queries, group_back = it.groups[part // per_group]
        heads = [part % per_group * PACK + h for h in range(PACK)]
        query_pack, back_pack = (
            jnp.concatenate(
                [jnp.where(lane_head == h, rows_of, 0.0) for h in heads], axis=0
            ).astype(BF16)
            for rows_of in (group_queries, group_back)
        )
        logits = dot_t(kv[:, :GROUP], query_pack)
        return it, part, query_pack, back_pack, logits, dot_t(kv[:, GROUP:], back_pack)

    def middle(it, part, query_pack, back_pack, logits, back_weights):
        logits = jnp.concatenate(
            [
                jnp.where(rows < count, logits[index * BLOCK : (index + 1) * BLOCK], -1e30)
                for index, count in enumerate(it.counts)
            ],
            axis=0,
        )
        highest = jnp.max(logits, axis=0, keepdims=True)
        raised = jnp.exp2((logits - highest) * (factor * LOG2E))
        scale = 1.0 / jnp.sum(raised, axis=0, keepdims=True)
        weights = raised * scale
        center = jnp.sum(weights * back_weights, axis=0, keepdims=True)
        back_logits = (weights * ((back_weights - center) * factor)).astype(BF16)
        return it, part, query_pack, back_pack, weights.astype(BF16), back_logits

    def finish(it, part, query_pack, back_pack, weights_low, back_logits):
        group = part // per_group
        kv_cols = it.groups[group][2]
        it.values[group].append(dot(weights_low, back_pack))
        it.keys[group].append(dot(back_logits, query_pack))
        size = PACK * HD
        first = part % per_group * size
        out_t = dot(kv_cols[GROUP + first : GROUP + first + size, :], weights_low)
        query_grad_t = dot(kv_cols[first : first + size, :], back_logits)
        for h in range(PACK):
            lanes = slice(h * BLOCK, (h + 1) * BLOCK)
            it.outputs_t.append(out_t[h * HD : (h + 1) * HD, lanes])
            it.back_query_t.append(query_grad_t[h * HD : (h + 1) * HD, lanes])

    def end(it):
        inputs_t = it.inputs.T
        back_inputs = None
        for group, grad_ref in enumerate((grad_mine_ref, grad_other_ref)):
            kv_t = it.groups[group][0]
            keys, values = it.keys[group], it.values[group]
            back_kv = jnp.concatenate(
                [sum(keys[1:], keys[0]), sum(values[1:], values[0])], axis=1
            ).astype(BF16)
            term = dot(back_kv, kv_t)
            back_inputs = term if back_inputs is None else back_inputs + term
            grad_ref[0:256, :] += dot(inputs_t, back_kv)
        outputs_t = jnp.concatenate(it.outputs_t, axis=0).astype(BF16)
        back_query_t = jnp.concatenate(it.back_query_t, axis=0).astype(BF16)
        query_grad = dot(back_query_t, it.own)
        output_grad = dot(outputs_t, it.up)
        grad_mine_ref[256:384, :] += query_grad[:GROUP]
        grad_other_ref[256:384, :] += query_grad[GROUP:]
        grad_mine_ref[384:512, :] += output_grad[:GROUP]
        grad_other_ref[384:512, :] += output_grad[GROUP:]
        own_out_ref[it.place] = back_inputs[:BLOCK] + dot(back_query_t.T, query_t)
        home_ref[tab[lay.recv_of + it.item]] = back_inputs[BLOCK : 2 * BLOCK].astype(BF16)
        day_ref[it.place] = back_inputs[2 * BLOCK :].astype(BF16)

    parts = 2 * per_group
    items = [begin(0)]
    started = start(items[0], 0)
    waiting = None
    ended = 0
    for index in range(STEP_ITEMS * parts):
        following = None
        if index + 1 < STEP_ITEMS * parts:
            place, part = divmod(index + 1, parts)
            if part == 0:
                items.append(begin(place))
            following = start(items[place], part)
        if waiting is not None:
            finish(*waiting)
            if waiting[1] == parts - 1:
                end(waiting[0])
        waiting = middle(*started)
        started = following
    finish(*waiting)
    end(waiting[0])


def fold_kernel(lay, tab, homes, own_terms, day_terms, home_terms, keep, give):
    core = lax.axis_index("head")
    half = keep.shape[2]

    def one(block, carry):
        item = tab[lay.item_of + block]
        mine = tab[lay.owner_of + block] == core
        asked = homes[lay.asker_of + block] == core
        own = own_terms[item] + day_terms[item].astype(F32)
        home = home_terms[homes[lay.home_of + block]].astype(F32)
        total = jnp.where(mine, own, 0.0) + jnp.where(asked, home, 0.0)
        low, high = total[:, :half], total[:, half:]
        keep[block] = jnp.where(core == 0, low, high)
        give[block] = jnp.where(core == 0, high, low)
        return carry

    lax.fori_loop(0, lay.blocks, one, 0)


def add_kernel(kept, got, out):
    out[...] = (kept[...] + got[...]).astype(BF16)


def attend(lay, tab, in_blocks, up_blocks, received, prior_inputs, pack, pack_other):
    width = in_blocks.shape[-1]

    def at_item(place):
        return lambda step, tab: (step * STEP_ITEMS + place, 0, 0)

    def at_block(place):
        return lambda step, tab: (tab[lay.block_of + step * STEP_ITEMS + place], 0, 0)

    def at_recv(place):
        return lambda step, tab: (tab[lay.recv_of + step * STEP_ITEMS + place], 0, 0)

    def at_step(step, tab):
        return (step, 0, 0)

    def fixed(step, tab):
        return (0, 0)

    full_block = (1, BLOCK, width)
    weights_block = (4 * GROUP, width)
    in_specs, operands = [], []
    for place in range(STEP_ITEMS):
        in_specs += [
            pl.BlockSpec(full_block, at_block(place)),
            pl.BlockSpec(full_block, at_block(place)),
            pl.BlockSpec(full_block, at_recv(place)),
            pl.BlockSpec(full_block, at_item(place)),
        ]
        operands += [in_blocks, up_blocks, received, prior_inputs]
    in_specs += [pl.BlockSpec(weights_block, fixed)] * 2
    operands += [pack, pack_other]
    pieces = lay.items
    flops = 2 * pieces * (23 * BLOCK * width * width + 24 * BLOCK * 3 * BLOCK * 512)
    return pl.pallas_call(
        lambda *refs: attention_kernel(lay, *refs),
        grid_spec=pltpu.PrefetchScalarGridSpec(
            num_scalar_prefetch=1,
            grid=(pieces // STEP_ITEMS,),
            in_specs=in_specs,
            out_specs=(
                pl.BlockSpec((STEP_ITEMS, BLOCK, width), at_step),
                pl.BlockSpec((STEP_ITEMS, BLOCK, width), at_step),
                pl.BlockSpec((lay.places, BLOCK, width), lambda step, tab: (0, 0, 0)),
                pl.BlockSpec(weights_block, fixed),
                pl.BlockSpec(weights_block, fixed),
            ),
        ),
        out_shape=(
            pltpu.HBM((pieces, BLOCK, width), F32),
            pltpu.HBM((pieces, BLOCK, width), BF16),
            pltpu.HBM((lay.places, BLOCK, width), BF16),
            pltpu.HBM(weights_block, F32),
            pltpu.HBM(weights_block, F32),
        ),
        compiler_params=pltpu.CompilerParams(vmem_limit_bytes=32 << 20),
        cost_estimate=pl.CostEstimate(
            flops=flops, bytes_accessed=9 << 20, transcendentals=pieces * 8 * BLOCK * 3 * BLOCK
        ),
        name="attention",
    )(
        tab,
        *[
            value
            if value is received
            else pltpu.with_memory_space_constraint(value, pltpu.HBM)
            for value in operands
        ],
    )


def exchanged(value, axis, bit):
    count = lax.axis_size(axis)
    return lax.ppermute(value, axis, [(place, place ^ bit) for place in range(count)])


def summed_over(value, axis, bit):
    low = value.astype(BF16)
    return low.astype(F32) + exchanged(low, axis, bit).astype(F32)


def sum_gradients(total):
    half = total.shape[0] // 2
    first = lax.rem(lax.axis_index("day"), 2) == 0
    kept = jnp.where(first, total[:half], total[half:])
    given = jnp.where(first, total[half:], total[:half])
    part = kept.astype(BF16).astype(F32) + exchanged(given.astype(BF16), "day", 1).astype(F32)
    bit = 2
    while bit < lax.axis_size("day"):
        part = summed_over(part, "day", bit)
        bit *= 2
    bit = 1
    while bit < lax.axis_size("reach"):
        part = summed_over(part, "reach", bit)
        bit *= 2
    part = part.astype(BF16)
    return part, exchanged(part, "day", 1)


def split_kernel(part, other, query_out, key_out, value_out, output_out):
    first = lax.rem(lax.axis_index("day"), 2) == 0
    mine, theirs = part[...].astype(F32), other[...].astype(F32)
    upper = jnp.where(first, mine, theirs)
    lower = jnp.where(first, theirs, mine)
    key_out[...] = upper[:, :GROUP]
    value_out[...] = upper[:, GROUP:]
    query_out[...] = lower[:GROUP].T
    output_out[...] = lower[GROUP:]


def on_device(
    inputs, upstream, query_weight, key_weight, value_weight, output_weight, partner, counts
):
    days_dev, rows_dev, width = inputs.shape
    assert days_dev == 1 and width == 2 * GROUP
    blocks_dev = rows_dev // BLOCK
    reach_total = lax.axis_size("reach")
    day_total = lax.axis_size("day")
    assert lax.axis_size("head") == CORES
    lay = Layout(blocks_dev, reach_total)
    half = width // 2
    in_blocks = inputs.reshape(blocks_dev, BLOCK, width)
    up_blocks = upstream.reshape(blocks_dev, BLOCK, width)
    pack = jnp.concatenate([key_weight.T, value_weight.T, query_weight.T, output_weight], axis=0)
    pack_other = exchanged(pack, "head", 1)

    smem = pl.BlockSpec(memory_space=pltpu.SMEM)
    in_vmem = pl.BlockSpec(memory_space=pltpu.VMEM)
    anywhere = pl.BlockSpec(memory_space=pl.ANY)
    sent_shape = jax.ShapeDtypeStruct((lay.places, BLOCK, width), BF16)
    sent, homes = pl.pallas_call(
        lambda *refs: pick_kernel(lay, *refs),
        out_shape=(sent_shape, jax.ShapeDtypeStruct((lay.homes_size,), jnp.int32)),
        in_specs=[anywhere, anywhere],
        out_specs=(in_vmem, smem),
        scratch_shapes=[
            pltpu.SMEM(partner.shape, jnp.int32),
            pltpu.VMEM((blocks_dev, BLOCK, width), BF16),
            pltpu.SemaphoreType.DMA((2,)),
        ],
        compiler_params=pltpu.CompilerParams(vmem_limit_bytes=16 << 20),
        name="pick",
    )(
        pltpu.with_memory_space_constraint(partner, pltpu.HBM),
        pltpu.with_memory_space_constraint(in_blocks, pltpu.HBM),
    )
    prior, tab = pl.pallas_call(
        lambda *refs: deal_kernel(lay, *refs),
        out_shape=(
            jax.ShapeDtypeStruct((lay.items, BLOCK, width), BF16),
            jax.ShapeDtypeStruct((lay.size,), jnp.int32),
        ),
        in_specs=[smem, smem, in_vmem],
        out_specs=(in_vmem, smem),
        scratch_shapes=[
            pltpu.SMEM((lay.reach,), jnp.int32),
            pltpu.SMEM((lay.reach,), jnp.int32),
        ],
        compiler_params=pltpu.CompilerParams(vmem_limit_bytes=16 << 20),
        name="deal",
    )(partner, counts, in_blocks)

    def ring(value):
        shape = value.shape
        value = value.reshape(lay.reach, lay.slots * BLOCK, width)
        return lax.all_to_all(value, "reach", 0, 0, tiled=True).reshape(shape)

    next_day = [(d, d + 1) for d in range(day_total - 1)]
    last_day = [(d + 1, d) for d in range(day_total - 1)]
    received = ring(sent)
    prior_inputs = lax.ppermute(prior, "day", next_day)
    own_terms, day_terms, home_terms, grad_mine, grad_other = attend(
        lay, tab, in_blocks, up_blocks, received, prior_inputs, pack, pack_other
    )
    home_terms = ring(home_terms)
    grad_swapped = exchanged(grad_other, "head", 1)
    day_terms = lax.ppermute(day_terms, "day", last_day)
    half_shape = jax.ShapeDtypeStruct((blocks_dev, BLOCK, half), F32)

    part, other = sum_gradients(grad_mine + grad_swapped)
    _, home_terms = lax.optimization_barrier((part, home_terms))
    keep, give = pl.pallas_call(
        lambda *refs: fold_kernel(lay, *refs),
        out_shape=(half_shape, half_shape),
        in_specs=[smem] * 2 + [in_vmem] * 3,
        out_specs=[in_vmem] * 2,
        compiler_params=pltpu.CompilerParams(vmem_limit_bytes=16 << 20),
        name="fold",
    )(tab, homes, own_terms, day_terms, home_terms)
    other, give = lax.optimization_barrier((other, give))
    got = exchanged(give, "head", 1)
    back_blocks = pl.pallas_call(
        add_kernel,
        out_shape=jax.ShapeDtypeStruct((blocks_dev, BLOCK, half), BF16),
        in_specs=[in_vmem] * 2,
        out_specs=in_vmem,
        compiler_params=pltpu.CompilerParams(vmem_limit_bytes=16 << 20),
        name="add",
    )(keep, got)
    weight_grads = pl.pallas_call(
        split_kernel,
        out_shape=(
            jax.ShapeDtypeStruct((width, half), F32),
            jax.ShapeDtypeStruct((width, half), F32),
            jax.ShapeDtypeStruct((width, half), F32),
            jax.ShapeDtypeStruct((half, width), F32),
        ),
        grid=(1,),
        name="split",
    )(part, other)

    return (back_blocks.reshape(1, rows_dev, half), *weight_grads)


def solution(mesh):
    placed = (
        P(("groups", "day"), "reach", None),
        P(("groups", "day"), "reach", None),
        P(None, "head"),
        P(None, "head"),
        P(None, "head"),
        P("head", None),
        P("groups"),
        P("groups"),
    )
    return jax.shard_map(
        on_device,
        mesh=mesh,
        in_specs=placed,
        out_specs=(
            P(("groups", "day"), "reach", "head"),
            P("groups", "head"),
            P("groups", "head"),
            P("groups", "head"),
            P(("groups", "head"), None),
        ),
        check_vma=False,
    )
```

```python
import jax
import jax.numpy as jnp
from jax import lax
from jax.experimental import pallas as pl
from jax.experimental.pallas import tpu as pltpu
from jax.sharding import PartitionSpec as P

HD = 32
BLOCK = 128
GROUP = 128
CORES = 2
CHUNKS = 2
WORKERS = CORES * CHUNKS
F32 = jnp.float32
BF16 = jnp.bfloat16
PACK = 4
STEP_ITEMS = 4
LOG2E = 1.4426950408889634


class Layout:
    def __init__(self, blocks_dev, reach_total):
        self.blocks = blocks_dev
        self.items = blocks_dev // CORES
        self.chunk_items = self.items // CHUNKS
        self.reach = reach_total
        self.slots = max(1, 2 * blocks_dev // reach_total // WORKERS)
        self.places = reach_total * self.slots
        self.block_of = 0
        self.recv_of = self.items
        self.count_own = 2 * self.items
        self.count_partner = 3 * self.items
        self.owner_of = 4 * self.items
        self.item_of = self.owner_of + blocks_dev
        self.core = self.item_of + blocks_dev
        self.later_day = self.core + 1
        self.size = -(-(self.core + 2) // 128) * 128
        self.spare = blocks_dev
        self.home_of = 0
        self.chunk_of = blocks_dev + 1
        self.asker_of = 2 * (blocks_dev + 1)
        self.picks = 3 * (blocks_dev + 1)
        self.spare_pick = self.picks + CHUNKS * self.places
        self.homes_size = -(-(self.spare_pick + 1) // 128) * 128


def pick_kernel(lay, partner_hbm, inputs, sent, homes, partner, held, sems):
    bd, slots = lay.blocks, lay.slots
    reach_pos, core = lax.axis_index("reach"), lax.axis_index("head")
    table_copy = pltpu.make_async_copy(partner_hbm, partner, sems.at[0])
    table_copy.start()
    copy = pltpu.make_async_copy(inputs, held, sems.at[1])
    copy.start()
    for place in range(CHUNKS * lay.places):
        homes[lay.picks + place] = 0
    table_copy.wait()

    def one_reach(peer, carry):
        base = jnp.int32(0)
        wanted = []
        for index in range(bd):
            block = partner[peer * bd + index]
            source = lax.div(block, bd)
            base = base + jnp.where(source < reach_pos, 1, 0)
            wanted.append((source == reach_pos, lax.rem(block, bd)))
        rank = jnp.int32(0)
        for hit, local in wanted:
            place = base + rank
            owner = lax.rem(place, CORES)
            chunk = lax.rem(lax.div(place, CORES), CHUNKS)
            slot = peer * slots + jnp.minimum(lax.div(rank, WORKERS), slots - 1)
            target = jnp.where(hit, local, lay.spare)
            homes[lay.home_of + target] = slot
            homes[lay.chunk_of + target] = chunk
            homes[lay.asker_of + target] = owner
            pick = lay.picks + chunk * lay.places + slot
            homes[jnp.where(hit & (owner == core), pick, lay.spare_pick)] = local
            rank = rank + jnp.where(hit, 1, 0)
        return carry

    lax.fori_loop(0, lay.reach, one_reach, 0)
    copy.wait()
    for place in range(lay.places):
        sent[place] = held[homes[lay.picks + place]]


def deal_kernel(lay, partner, counts, homes, inputs, sent, prior, tab, start, used):
    bd, slots = lay.blocks, lay.slots
    reach_pos, core = lax.axis_index("reach"), lax.axis_index("head")

    def clear(index, carry):
        used[index] = 0
        start[index] = 0
        return carry

    lax.fori_loop(0, lay.reach, clear, 0, unroll=True)

    def count(index, carry):
        source = lax.div(partner[reach_pos * bd + index], bd)
        start[source] = start[source] + 1
        return carry

    lax.fori_loop(0, bd, count, 0)

    def prefix(index, total):
        here = start[index]
        start[index] = total
        return total + here

    lax.fori_loop(0, lay.reach, prefix, jnp.int32(0))

    def assign(index, carry):
        wanted = partner[reach_pos * bd + index]
        source = lax.div(wanted, bd)
        rank = used[source]
        used[source] = rank + 1
        place = start[source] + rank
        owner = lax.rem(place, CORES)
        chunk = lax.rem(lax.div(place, CORES), CHUNKS)
        item = chunk * lay.chunk_items + lax.div(place, WORKERS)
        slot = jnp.minimum(lax.div(rank, WORKERS), slots - 1)
        tab[lay.owner_of + index] = owner
        tab[lay.item_of + index] = item

        @pl.when(owner == core)
        def _():
            tab[lay.block_of + item] = index
            tab[lay.recv_of + item] = source * slots + slot
            tab[lay.count_own + item] = counts[reach_pos * bd + index]
            tab[lay.count_partner + item] = counts[wanted]

        return carry

    lax.fori_loop(0, bd, assign, 0)
    tab[lay.core] = core
    tab[lay.later_day] = jnp.where(lax.axis_index("day") > 0, 1, 0)

    def pick(place, carry):
        sent[place] = inputs[homes[lay.picks + lay.places + place]]
        return carry

    def pick_prior(item, carry):
        prior[item] = inputs[tab[lay.block_of + item]]
        return carry

    lax.fori_loop(0, lay.places, pick, 0)
    lax.fori_loop(0, lay.items, pick_prior, 0)


def dot(left, right):
    return lax.dot_general(left, right, (((1,), (0,)), ((), ())), preferred_element_type=F32)


def dot_t(left, right):
    return lax.dot_general(left, right, (((1,), (1,)), ((), ())), preferred_element_type=F32)


def attention_kernel(lay, chunk, tab, *refs):
    step = pl.program_id(0)
    read, refs = refs[: 4 * STEP_ITEMS], refs[4 * STEP_ITEMS :]
    mine_ref, other_ref, *refs = refs
    if chunk:
        start_mine_ref, start_other_ref, *refs = refs
    own_out_ref, day_ref, home_ref, grad_mine_ref, grad_other_ref = refs
    factor = HD ** (-0.5)
    per_group = GROUP // HD // PACK

    @pl.when(step == 0)
    def _():
        if chunk:
            grad_mine_ref[...] = start_mine_ref[...]
            grad_other_ref[...] = start_other_ref[...]
        else:
            grad_mine_ref[...] = jnp.zeros_like(grad_mine_ref)
            grad_other_ref[...] = jnp.zeros_like(grad_other_ref)

    rows = lax.broadcasted_iota(jnp.int32, (BLOCK, PACK * BLOCK), 0)
    lane_head = lax.broadcasted_iota(jnp.int32, (BLOCK, GROUP), 1) // HD
    query_t = jnp.concatenate([mine_ref[256:384, :], other_ref[256:384, :]], axis=0)
    output_w = jnp.concatenate([mine_ref[384:512, :], other_ref[384:512, :]], axis=0)

    class Item:
        pass

    def begin(place):
        it = Item()
        own_ref, up_ref, partner_ref, prior_ref = read[4 * place : 4 * place + 4]
        it.place = place
        item = step * STEP_ITEMS + place + chunk * lay.chunk_items
        it.item = item
        it.own, it.up = own_ref[0], up_ref[0]
        it.inputs = jnp.concatenate([it.own, partner_ref[0], prior_ref[0]], axis=0)
        queries = dot_t(it.own, query_t)
        back_out = dot_t(it.up, output_w)
        count_own = tab[lay.count_own + item]
        it.counts = (count_own, tab[lay.count_partner + item], count_own * tab[lay.later_day])
        it.groups = []
        for group, weights_ref in enumerate((mine_ref, other_ref)):
            kv_t = weights_ref[0:256, :]
            kv = dot_t(it.inputs, kv_t).astype(BF16)
            lanes = slice(group * GROUP, (group + 1) * GROUP)
            it.groups.append((kv_t, kv, kv.T, queries[:, lanes], back_out[:, lanes]))
        it.outputs_t, it.back_query_t = [], []
        it.keys, it.values = ([], []), ([], [])
        return it

    def start(it, part):
        _, kv, _, group_queries, group_back = it.groups[part // per_group]
        heads = [part % per_group * PACK + h for h in range(PACK)]
        query_pack, back_pack = (
            jnp.concatenate(
                [jnp.where(lane_head == h, rows_of, 0.0) for h in heads], axis=0
            ).astype(BF16)
            for rows_of in (group_queries, group_back)
        )
        logits = dot_t(kv[:, :GROUP], query_pack)
        return it, part, query_pack, back_pack, logits, dot_t(kv[:, GROUP:], back_pack)

    def middle(it, part, query_pack, back_pack, logits, back_weights):
        logits = jnp.concatenate(
            [
                jnp.where(rows < count, logits[index * BLOCK : (index + 1) * BLOCK], -1e30)
                for index, count in enumerate(it.counts)
            ],
            axis=0,
        )
        highest = jnp.max(logits, axis=0, keepdims=True)
        raised = jnp.exp2((logits - highest) * (factor * LOG2E))
        scale = 1.0 / jnp.sum(raised, axis=0, keepdims=True)
        weights = raised * scale
        center = jnp.sum(weights * back_weights, axis=0, keepdims=True)
        back_logits = (weights * ((back_weights - center) * factor)).astype(BF16)
        return it, part, query_pack, back_pack, weights.astype(BF16), back_logits

    def finish(it, part, query_pack, back_pack, weights_low, back_logits):
        group = part // per_group
        kv_cols = it.groups[group][2]
        it.values[group].append(dot(weights_low, back_pack))
        it.keys[group].append(dot(back_logits, query_pack))
        size = PACK * HD
        first = part % per_group * size
        out_t = dot(kv_cols[GROUP + first : GROUP + first + size, :], weights_low)
        query_grad_t = dot(kv_cols[first : first + size, :], back_logits)
        for h in range(PACK):
            lanes = slice(h * BLOCK, (h + 1) * BLOCK)
            it.outputs_t.append(out_t[h * HD : (h + 1) * HD, lanes])
            it.back_query_t.append(query_grad_t[h * HD : (h + 1) * HD, lanes])

    def end(it):
        inputs_t = it.inputs.T
        back_inputs = None
        for group, grad_ref in enumerate((grad_mine_ref, grad_other_ref)):
            kv_t = it.groups[group][0]
            keys, values = it.keys[group], it.values[group]
            back_kv = jnp.concatenate(
                [sum(keys[1:], keys[0]), sum(values[1:], values[0])], axis=1
            ).astype(BF16)
            term = dot(back_kv, kv_t)
            back_inputs = term if back_inputs is None else back_inputs + term
            grad_ref[0:256, :] += dot(inputs_t, back_kv)
        outputs_t = jnp.concatenate(it.outputs_t, axis=0).astype(BF16)
        back_query_t = jnp.concatenate(it.back_query_t, axis=0).astype(BF16)
        query_grad = dot(back_query_t, it.own)
        output_grad = dot(outputs_t, it.up)
        grad_mine_ref[256:384, :] += query_grad[:GROUP]
        grad_other_ref[256:384, :] += query_grad[GROUP:]
        grad_mine_ref[384:512, :] += output_grad[:GROUP]
        grad_other_ref[384:512, :] += output_grad[GROUP:]
        own_out_ref[it.place] = back_inputs[:BLOCK] + dot(back_query_t.T, query_t)
        home_ref[tab[lay.recv_of + it.item]] = back_inputs[BLOCK : 2 * BLOCK].astype(BF16)
        day_ref[it.place] = back_inputs[2 * BLOCK :].astype(BF16)

    parts = 2 * per_group
    items = [begin(0)]
    started = start(items[0], 0)
    waiting = None
    ended = 0
    for index in range(STEP_ITEMS * parts):
        following = None
        if index + 1 < STEP_ITEMS * parts:
            place, part = divmod(index + 1, parts)
            if part == 0:
                items.append(begin(place))
            following = start(items[place], part)
        if waiting is not None:
            finish(*waiting)
            if waiting[1] == parts - 1:
                end(waiting[0])
        waiting = middle(*started)
        started = following
    finish(*waiting)
    end(waiting[0])


def fold_kernel(lay, tab, homes, own_a, own_b, day_a, day_b, home_a, home_b, keep, give):
    core = tab[lay.core]
    half = keep.shape[2]

    def one(block, carry):
        item = tab[lay.item_of + block]
        mine = tab[lay.owner_of + block] == core
        place = homes[lay.home_of + block]
        asked = homes[lay.asker_of + block] == core
        early = homes[lay.chunk_of + block] == 0
        in_a = item < lay.chunk_items
        item_a = jnp.minimum(item, lay.chunk_items - 1)
        item_b = jnp.maximum(item - lay.chunk_items, 0)
        own = jnp.where(in_a, own_a[item_a], own_b[item_b])
        own += jnp.where(in_a, day_a[item_a].astype(F32), day_b[item_b].astype(F32))
        home = jnp.where(early, home_a[place].astype(F32), home_b[place].astype(F32))
        total = jnp.where(mine, own, 0.0) + jnp.where(asked, home, 0.0)
        low, high = total[:, :half], total[:, half:]
        keep[block] = jnp.where(core == 0, low, high)
        give[block] = jnp.where(core == 0, high, low)
        return carry

    lax.fori_loop(0, lay.blocks, one, 0)


def add_kernel(kept, got, out):
    out[...] = (kept[...] + got[...]).astype(BF16)


def attend(lay, chunk, tab, in_blocks, up_blocks, received, prior_inputs, pack, pack_other, carried):
    width = in_blocks.shape[-1]
    offset = chunk * lay.chunk_items

    def at_item(place):
        return lambda step, tab: (offset + step * STEP_ITEMS + place, 0, 0)

    def at_block(place):
        return lambda step, tab: (tab[lay.block_of + offset + step * STEP_ITEMS + place], 0, 0)

    def at_recv(place):
        return lambda step, tab: (tab[lay.recv_of + offset + step * STEP_ITEMS + place], 0, 0)

    def at_step(step, tab):
        return (step, 0, 0)

    def fixed(step, tab):
        return (0, 0)

    full_block = (1, BLOCK, width)
    weights_block = (4 * GROUP, width)
    in_specs, operands = [], []
    for place in range(STEP_ITEMS):
        in_specs += [
            pl.BlockSpec(full_block, at_block(place)),
            pl.BlockSpec(full_block, at_block(place)),
            pl.BlockSpec(full_block, at_recv(place)),
            pl.BlockSpec(full_block, at_item(place)),
        ]
        operands += [in_blocks, up_blocks, received, prior_inputs]
    in_specs += [pl.BlockSpec(weights_block, fixed)] * 2
    operands += [pack, pack_other]
    if chunk:
        in_specs += [pl.BlockSpec(weights_block, fixed)] * 2
        operands += carried
    pieces = lay.chunk_items
    flops = 2 * pieces * (23 * BLOCK * width * width + 24 * BLOCK * 3 * BLOCK * 512)
    return pl.pallas_call(
        lambda *refs: attention_kernel(lay, chunk, *refs),
        grid_spec=pltpu.PrefetchScalarGridSpec(
            num_scalar_prefetch=1,
            grid=(pieces // STEP_ITEMS,),
            in_specs=in_specs,
            out_specs=(
                pl.BlockSpec((STEP_ITEMS, BLOCK, width), at_step),
                pl.BlockSpec((STEP_ITEMS, BLOCK, width), at_step),
                pl.BlockSpec((lay.places, BLOCK, width), lambda step, tab: (0, 0, 0)),
                pl.BlockSpec(weights_block, fixed),
                pl.BlockSpec(weights_block, fixed),
            ),
        ),
        out_shape=(
            pltpu.HBM((pieces, BLOCK, width), F32),
            pltpu.HBM((pieces, BLOCK, width), BF16),
            pltpu.HBM((lay.places, BLOCK, width), BF16),
            pltpu.HBM(weights_block, F32),
            pltpu.HBM(weights_block, F32),
        ),
        compiler_params=pltpu.CompilerParams(vmem_limit_bytes=32 << 20),
        cost_estimate=pl.CostEstimate(
            flops=flops, bytes_accessed=5 << 20, transcendentals=pieces * 8 * BLOCK * 3 * BLOCK
        ),
        name=f"attention_{chunk}",
    )(
        tab,
        *[
            value
            if value is received
            else pltpu.with_memory_space_constraint(value, pltpu.HBM)
            for value in operands
        ],
    )


def exchanged(value, axis, bit):
    count = lax.axis_size(axis)
    return lax.ppermute(value, axis, [(place, place ^ bit) for place in range(count)])


def summed_over(value, axis, bit):
    low = value.astype(BF16)
    return low.astype(F32) + exchanged(low, axis, bit).astype(F32)


def sum_gradients(total, early, home_b, ring):
    half = total.shape[0] // 2
    first = lax.rem(lax.axis_index("day"), 2) == 0
    kept = jnp.where(first, total[:half], total[half:])
    given = jnp.where(first, total[half:], total[:half]).astype(BF16)
    given, early, home_b = lax.optimization_barrier((given, early, home_b))
    home_b = ring(home_b)
    part = kept.astype(BF16).astype(F32) + exchanged(given, "day", 1).astype(F32)
    bit = 2
    while bit < lax.axis_size("day"):
        part = summed_over(part, "day", bit)
        bit *= 2
    bit = 1
    while bit < lax.axis_size("reach"):
        part = summed_over(part, "reach", bit)
        bit *= 2
    part = part.astype(BF16)
    part, home_b = lax.optimization_barrier((part, home_b))
    return part, exchanged(part, "day", 1), early, home_b


def split_kernel(part, other, query_out, key_out, value_out, output_out):
    first = lax.rem(lax.axis_index("day"), 2) == 0
    mine, theirs = part[...].astype(F32), other[...].astype(F32)
    upper = jnp.where(first, mine, theirs)
    lower = jnp.where(first, theirs, mine)
    key_out[...] = upper[:, :GROUP]
    value_out[...] = upper[:, GROUP:]
    query_out[...] = lower[:GROUP].T
    output_out[...] = lower[GROUP:]


def on_device(
    inputs, upstream, query_weight, key_weight, value_weight, output_weight, partner, counts
):
    days_dev, rows_dev, width = inputs.shape
    assert days_dev == 1 and width == 2 * GROUP
    blocks_dev = rows_dev // BLOCK
    reach_total = lax.axis_size("reach")
    day_total = lax.axis_size("day")
    assert lax.axis_size("head") == CORES
    lay = Layout(blocks_dev, reach_total)
    half = width // 2
    in_blocks = inputs.reshape(blocks_dev, BLOCK, width)
    up_blocks = upstream.reshape(blocks_dev, BLOCK, width)
    pack = jnp.concatenate([key_weight.T, value_weight.T, query_weight.T, output_weight], axis=0)
    pack_other = exchanged(pack, "head", 1)

    smem = pl.BlockSpec(memory_space=pltpu.SMEM)
    in_vmem = pl.BlockSpec(memory_space=pltpu.VMEM)
    anywhere = pl.BlockSpec(memory_space=pl.ANY)
    sent_shape = jax.ShapeDtypeStruct((lay.places, BLOCK, width), BF16)
    sent_a, homes = pl.pallas_call(
        lambda *refs: pick_kernel(lay, *refs),
        out_shape=(sent_shape, jax.ShapeDtypeStruct((lay.homes_size,), jnp.int32)),
        in_specs=[anywhere, anywhere],
        out_specs=(in_vmem, smem),
        scratch_shapes=[
            pltpu.SMEM(partner.shape, jnp.int32),
            pltpu.VMEM((blocks_dev, BLOCK, width), BF16),
            pltpu.SemaphoreType.DMA((2,)),
        ],
        compiler_params=pltpu.CompilerParams(vmem_limit_bytes=16 << 20),
        name="pick",
    )(
        pltpu.with_memory_space_constraint(partner, pltpu.HBM),
        pltpu.with_memory_space_constraint(in_blocks, pltpu.HBM),
    )
    sent_b, prior, tab = pl.pallas_call(
        lambda *refs: deal_kernel(lay, *refs),
        out_shape=(
            sent_shape,
            jax.ShapeDtypeStruct((lay.items, BLOCK, width), BF16),
            jax.ShapeDtypeStruct((lay.size,), jnp.int32),
        ),
        in_specs=[smem, smem, smem, in_vmem],
        out_specs=(in_vmem, in_vmem, smem),
        scratch_shapes=[
            pltpu.SMEM((lay.reach,), jnp.int32),
            pltpu.SMEM((lay.reach,), jnp.int32),
        ],
        compiler_params=pltpu.CompilerParams(vmem_limit_bytes=16 << 20),
        name="deal",
    )(partner, counts, homes, in_blocks)

    def ring(value):
        shape = value.shape
        value = value.reshape(lay.reach, lay.slots * BLOCK, width)
        return lax.all_to_all(value, "reach", 0, 0, tiled=True).reshape(shape)

    next_day = [(d, d + 1) for d in range(day_total - 1)]
    last_day = [(d + 1, d) for d in range(day_total - 1)]
    received_a = ring(sent_a)
    prior_inputs = lax.ppermute(prior, "day", next_day)
    received_b = ring(sent_b)
    shared = (prior_inputs, pack, pack_other)
    own_a, day_a, home_a, *grads = attend(
        lay, 0, tab, in_blocks, up_blocks, received_a, *shared, None
    )
    home_a = ring(home_a)
    day_a = lax.ppermute(day_a, "day", last_day)
    own_b, day_b, home_b, grad_mine, grad_other = attend(
        lay, 1, tab, in_blocks, up_blocks, received_b, *shared, grads
    )
    grad_swapped = exchanged(grad_other, "head", 1)
    day_b = lax.ppermute(day_b, "day", last_day)
    half_shape = jax.ShapeDtypeStruct((blocks_dev, BLOCK, half), F32)

    part, other, home_a, home_b = sum_gradients(grad_mine + grad_swapped, home_a, home_b, ring)
    keep, give = pl.pallas_call(
        lambda *refs: fold_kernel(lay, *refs),
        out_shape=(half_shape, half_shape),
        in_specs=[smem] * 2 + [in_vmem] * 6,
        out_specs=[in_vmem] * 2,
        compiler_params=pltpu.CompilerParams(vmem_limit_bytes=16 << 20),
        name="fold",
    )(tab, homes, own_a, own_b, day_a, day_b, home_a, home_b)
    other, give = lax.optimization_barrier((other, give))
    got = exchanged(give, "head", 1)
    back_blocks = pl.pallas_call(
        add_kernel,
        out_shape=jax.ShapeDtypeStruct((blocks_dev, BLOCK, half), BF16),
        in_specs=[in_vmem] * 2,
        out_specs=in_vmem,
        compiler_params=pltpu.CompilerParams(vmem_limit_bytes=16 << 20),
        name="add",
    )(keep, got)
    weight_grads = pl.pallas_call(
        split_kernel,
        out_shape=(
            jax.ShapeDtypeStruct((width, half), F32),
            jax.ShapeDtypeStruct((width, half), F32),
            jax.ShapeDtypeStruct((width, half), F32),
            jax.ShapeDtypeStruct((half, width), F32),
        ),
        grid=(1,),
        name="split",
    )(part, other)

    return (back_blocks.reshape(1, rows_dev, half), *weight_grads)


def solution(mesh):
    placed = (
        P(("groups", "day"), "reach", None),
        P(("groups", "day"), "reach", None),
        P(None, "head"),
        P(None, "head"),
        P(None, "head"),
        P("head", None),
        P("groups"),
        P("groups"),
    )
    return jax.shard_map(
        on_device,
        mesh=mesh,
        in_specs=placed,
        out_specs=(
            P(("groups", "day"), "reach", "head"),
            P("groups", "head"),
            P("groups", "head"),
            P("groups", "head"),
            P(("groups", "head"), None),
        ),
        check_vma=False,
    )
```

```python
import jax
import jax.numpy as jnp
from jax import lax
from jax.experimental import pallas as pl
from jax.experimental.pallas import tpu as pltpu
from jax.sharding import PartitionSpec as P

HD = 32
BLOCK = 128
GROUP = 128
CORES = 2
CHUNKS = 2
WORKERS = CORES * CHUNKS
F32 = jnp.float32
BF16 = jnp.bfloat16
PACK = 4
STEP_ITEMS = 4
LOG2E = 1.4426950408889634


class Layout:
    def __init__(self, blocks_dev, reach_total):
        self.blocks = blocks_dev
        self.items = blocks_dev // CORES
        self.chunk_items = self.items // CHUNKS
        self.reach = reach_total
        self.slots = max(1, 2 * blocks_dev // reach_total // WORKERS)
        self.places = reach_total * self.slots
        self.block_of = 0
        self.recv_of = self.items
        self.count_own = 2 * self.items
        self.count_partner = 3 * self.items
        self.owner_of = 4 * self.items
        self.item_of = self.owner_of + blocks_dev
        self.core = self.item_of + blocks_dev
        self.later_day = self.core + 1
        self.size = -(-(self.core + 2) // 128) * 128
        self.spare = blocks_dev
        self.home_of = 0
        self.chunk_of = blocks_dev + 1
        self.asker_of = 2 * (blocks_dev + 1)
        self.picks = 3 * (blocks_dev + 1)
        self.spare_pick = self.picks + CHUNKS * self.places
        self.homes_size = -(-(self.spare_pick + 1) // 128) * 128


def pick_kernel(lay, partner_hbm, inputs, sent, homes, partner, held, sems):
    bd, slots = lay.blocks, lay.slots
    reach_pos, core = lax.axis_index("reach"), lax.axis_index("head")
    table_copy = pltpu.make_async_copy(partner_hbm, partner, sems.at[0])
    table_copy.start()
    copy = pltpu.make_async_copy(inputs, held, sems.at[1])
    copy.start()
    for place in range(CHUNKS * lay.places):
        homes[lay.picks + place] = 0
    table_copy.wait()

    def one_reach(peer, carry):
        base = jnp.int32(0)
        wanted = []
        for index in range(bd):
            block = partner[peer * bd + index]
            source = lax.div(block, bd)
            base = base + jnp.where(source < reach_pos, 1, 0)
            wanted.append((source == reach_pos, lax.rem(block, bd)))
        rank = jnp.int32(0)
        for hit, local in wanted:
            place = base + rank
            owner = lax.rem(place, CORES)
            chunk = lax.rem(lax.div(place, CORES), CHUNKS)
            slot = peer * slots + jnp.minimum(lax.div(rank, WORKERS), slots - 1)
            target = jnp.where(hit, local, lay.spare)
            homes[lay.home_of + target] = slot
            homes[lay.chunk_of + target] = chunk
            homes[lay.asker_of + target] = owner
            pick = lay.picks + chunk * lay.places + slot
            homes[jnp.where(hit & (owner == core), pick, lay.spare_pick)] = local
            rank = rank + jnp.where(hit, 1, 0)
        return carry

    lax.fori_loop(0, lay.reach, one_reach, 0)
    copy.wait()
    for place in range(lay.places):
        sent[place] = held[homes[lay.picks + place]]


def deal_kernel(lay, partner, counts, homes, inputs, sent, prior, tab, start, used):
    bd, slots = lay.blocks, lay.slots
    reach_pos, core = lax.axis_index("reach"), lax.axis_index("head")

    def clear(index, carry):
        used[index] = 0
        start[index] = 0
        return carry

    lax.fori_loop(0, lay.reach, clear, 0, unroll=True)

    def count(index, carry):
        source = lax.div(partner[reach_pos * bd + index], bd)
        start[source] = start[source] + 1
        return carry

    lax.fori_loop(0, bd, count, 0)

    def prefix(index, total):
        here = start[index]
        start[index] = total
        return total + here

    lax.fori_loop(0, lay.reach, prefix, jnp.int32(0))

    def assign(index, carry):
        wanted = partner[reach_pos * bd + index]
        source = lax.div(wanted, bd)
        rank = used[source]
        used[source] = rank + 1
        place = start[source] + rank
        owner = lax.rem(place, CORES)
        chunk = lax.rem(lax.div(place, CORES), CHUNKS)
        item = chunk * lay.chunk_items + lax.div(place, WORKERS)
        slot = jnp.minimum(lax.div(rank, WORKERS), slots - 1)
        tab[lay.owner_of + index] = owner
        tab[lay.item_of + index] = item

        @pl.when(owner == core)
        def _():
            tab[lay.block_of + item] = index
            tab[lay.recv_of + item] = source * slots + slot
            tab[lay.count_own + item] = counts[reach_pos * bd + index]
            tab[lay.count_partner + item] = counts[wanted]

        return carry

    lax.fori_loop(0, bd, assign, 0)
    tab[lay.core] = core
    tab[lay.later_day] = jnp.where(lax.axis_index("day") > 0, 1, 0)

    def pick(place, carry):
        sent[place] = inputs[homes[lay.picks + lay.places + place]]
        return carry

    def pick_prior(item, carry):
        prior[item] = inputs[tab[lay.block_of + item]]
        return carry

    lax.fori_loop(0, lay.places, pick, 0)
    lax.fori_loop(0, lay.items, pick_prior, 0)


def dot(left, right):
    return lax.dot_general(left, right, (((1,), (0,)), ((), ())), preferred_element_type=F32)


def dot_t(left, right):
    return lax.dot_general(left, right, (((1,), (1,)), ((), ())), preferred_element_type=F32)


def attention_kernel(lay, chunk, tab, *refs):
    step = pl.program_id(0)
    read, refs = refs[: 4 * STEP_ITEMS], refs[4 * STEP_ITEMS :]
    mine_ref, other_ref, *refs = refs
    if chunk:
        start_mine_ref, start_other_ref, *refs = refs
    own_out_ref, day_ref, home_ref, grad_mine_ref, grad_other_ref = refs
    factor = HD ** (-0.5)
    per_group = GROUP // HD // PACK

    @pl.when(step == 0)
    def _():
        if chunk:
            grad_mine_ref[...] = start_mine_ref[...]
            grad_other_ref[...] = start_other_ref[...]
        else:
            grad_mine_ref[...] = jnp.zeros_like(grad_mine_ref)
            grad_other_ref[...] = jnp.zeros_like(grad_other_ref)

    rows = lax.broadcasted_iota(jnp.int32, (BLOCK, PACK * BLOCK), 0)
    lane_head = lax.broadcasted_iota(jnp.int32, (BLOCK, GROUP), 1) // HD
    query_t = jnp.concatenate([mine_ref[256:384, :], other_ref[256:384, :]], axis=0)
    output_w = jnp.concatenate([mine_ref[384:512, :], other_ref[384:512, :]], axis=0)

    class Item:
        pass

    def begin(place):
        it = Item()
        own_ref, up_ref, partner_ref, prior_ref = read[4 * place : 4 * place + 4]
        it.place = place
        item = step * STEP_ITEMS + place + chunk * lay.chunk_items
        it.item = item
        it.own, it.up = own_ref[0], up_ref[0]
        it.inputs = jnp.concatenate([it.own, partner_ref[0], prior_ref[0]], axis=0)
        queries = dot_t(it.own, query_t)
        back_out = dot_t(it.up, output_w)
        count_own = tab[lay.count_own + item]
        it.counts = (count_own, tab[lay.count_partner + item], count_own * tab[lay.later_day])
        it.groups = []
        for group, weights_ref in enumerate((mine_ref, other_ref)):
            kv_t = weights_ref[0:256, :]
            kv = dot_t(it.inputs, kv_t).astype(BF16)
            lanes = slice(group * GROUP, (group + 1) * GROUP)
            it.groups.append((kv_t, kv, kv.T, queries[:, lanes], back_out[:, lanes]))
        it.outputs_t, it.back_query_t = [], []
        it.keys, it.values = ([], []), ([], [])
        return it

    def start(it, part):
        _, kv, _, group_queries, group_back = it.groups[part // per_group]
        heads = [part % per_group * PACK + h for h in range(PACK)]
        query_pack, back_pack = (
            jnp.concatenate(
                [jnp.where(lane_head == h, rows_of, 0.0) for h in heads], axis=0
            ).astype(BF16)
            for rows_of in (group_queries, group_back)
        )
        logits = dot_t(kv[:, :GROUP], query_pack)
        return it, part, query_pack, back_pack, logits, dot_t(kv[:, GROUP:], back_pack)

    def middle(it, part, query_pack, back_pack, logits, back_weights):
        logits = jnp.concatenate(
            [
                jnp.where(rows < count, logits[index * BLOCK : (index + 1) * BLOCK], -1e30)
                for index, count in enumerate(it.counts)
            ],
            axis=0,
        )
        highest = jnp.max(logits, axis=0, keepdims=True)
        raised = jnp.exp2((logits - highest) * (factor * LOG2E))
        scale = 1.0 / jnp.sum(raised, axis=0, keepdims=True)
        weights = raised * scale
        center = jnp.sum(weights * back_weights, axis=0, keepdims=True)
        back_logits = (weights * ((back_weights - center) * factor)).astype(BF16)
        return it, part, query_pack, back_pack, weights.astype(BF16), back_logits

    def finish(it, part, query_pack, back_pack, weights_low, back_logits):
        group = part // per_group
        kv_cols = it.groups[group][2]
        it.values[group].append(dot(weights_low, back_pack))
        it.keys[group].append(dot(back_logits, query_pack))
        size = PACK * HD
        first = part % per_group * size
        out_t = dot(kv_cols[GROUP + first : GROUP + first + size, :], weights_low)
        query_grad_t = dot(kv_cols[first : first + size, :], back_logits)
        for h in range(PACK):
            lanes = slice(h * BLOCK, (h + 1) * BLOCK)
            it.outputs_t.append(out_t[h * HD : (h + 1) * HD, lanes])
            it.back_query_t.append(query_grad_t[h * HD : (h + 1) * HD, lanes])

    def end(it):
        inputs_t = it.inputs.T
        back_inputs = None
        for group, grad_ref in enumerate((grad_mine_ref, grad_other_ref)):
            kv_t = it.groups[group][0]
            keys, values = it.keys[group], it.values[group]
            back_kv = jnp.concatenate(
                [sum(keys[1:], keys[0]), sum(values[1:], values[0])], axis=1
            ).astype(BF16)
            term = dot(back_kv, kv_t)
            back_inputs = term if back_inputs is None else back_inputs + term
            grad_ref[0:256, :] += dot(inputs_t, back_kv)
        outputs_t = jnp.concatenate(it.outputs_t, axis=0).astype(BF16)
        back_query_t = jnp.concatenate(it.back_query_t, axis=0).astype(BF16)
        query_grad = dot(back_query_t, it.own)
        output_grad = dot(outputs_t, it.up)
        grad_mine_ref[256:384, :] += query_grad[:GROUP]
        grad_other_ref[256:384, :] += query_grad[GROUP:]
        grad_mine_ref[384:512, :] += output_grad[:GROUP]
        grad_other_ref[384:512, :] += output_grad[GROUP:]
        own_out_ref[it.place] = back_inputs[:BLOCK] + dot(back_query_t.T, query_t)
        home_ref[tab[lay.recv_of + it.item]] = back_inputs[BLOCK : 2 * BLOCK].astype(BF16)
        day_ref[it.place] = back_inputs[2 * BLOCK :].astype(BF16)

    parts = 2 * per_group
    items = [begin(0)]
    started = start(items[0], 0)
    waiting = None
    ended = 0
    for index in range(STEP_ITEMS * parts):
        following = None
        if index + 1 < STEP_ITEMS * parts:
            place, part = divmod(index + 1, parts)
            if part == 0:
                items.append(begin(place))
            following = start(items[place], part)
        if waiting is not None:
            finish(*waiting)
            if waiting[1] == parts - 1:
                end(waiting[0])
        waiting = middle(*started)
        started = following
    finish(*waiting)
    end(waiting[0])


def fold_kernel(lay, tab, homes, own_a, own_b, day_a, day_b, home_a, home_b, keep, give):
    core = tab[lay.core]
    half = keep.shape[2]

    def one(block, carry):
        item = tab[lay.item_of + block]
        mine = tab[lay.owner_of + block] == core
        place = homes[lay.home_of + block]
        asked = homes[lay.asker_of + block] == core
        early = homes[lay.chunk_of + block] == 0
        in_a = item < lay.chunk_items
        item_a = jnp.minimum(item, lay.chunk_items - 1)
        item_b = jnp.maximum(item - lay.chunk_items, 0)
        own = jnp.where(in_a, own_a[item_a], own_b[item_b])
        own += jnp.where(in_a, day_a[item_a].astype(F32), day_b[item_b].astype(F32))
        home = jnp.where(early, home_a[place].astype(F32), home_b[place].astype(F32))
        total = jnp.where(mine, own, 0.0) + jnp.where(asked, home, 0.0)
        low, high = total[:, :half], total[:, half:]
        keep[block] = jnp.where(core == 0, low, high)
        give[block] = jnp.where(core == 0, high, low)
        return carry

    lax.fori_loop(0, lay.blocks, one, 0)


def add_kernel(kept, got, out):
    out[...] = (kept[...] + got[...]).astype(BF16)


def attend(lay, chunk, tab, in_blocks, up_blocks, received, prior_inputs, pack, pack_other, carried):
    width = in_blocks.shape[-1]
    offset = chunk * lay.chunk_items

    def at_item(place):
        return lambda step, tab: (offset + step * STEP_ITEMS + place, 0, 0)

    def at_block(place):
        return lambda step, tab: (tab[lay.block_of + offset + step * STEP_ITEMS + place], 0, 0)

    def at_recv(place):
        return lambda step, tab: (tab[lay.recv_of + offset + step * STEP_ITEMS + place], 0, 0)

    def at_step(step, tab):
        return (step, 0, 0)

    def fixed(step, tab):
        return (0, 0)

    full_block = (1, BLOCK, width)
    weights_block = (4 * GROUP, width)
    in_specs, operands = [], []
    for place in range(STEP_ITEMS):
        in_specs += [
            pl.BlockSpec(full_block, at_block(place)),
            pl.BlockSpec(full_block, at_block(place)),
            pl.BlockSpec(full_block, at_recv(place)),
            pl.BlockSpec(full_block, at_item(place)),
        ]
        operands += [in_blocks, up_blocks, received, prior_inputs]
    in_specs += [pl.BlockSpec(weights_block, fixed)] * 2
    operands += [pack, pack_other]
    if chunk:
        in_specs += [pl.BlockSpec(weights_block, fixed)] * 2
        operands += carried
    pieces = lay.chunk_items
    flops = 2 * pieces * (23 * BLOCK * width * width + 24 * BLOCK * 3 * BLOCK * 512)
    return pl.pallas_call(
        lambda *refs: attention_kernel(lay, chunk, *refs),
        grid_spec=pltpu.PrefetchScalarGridSpec(
            num_scalar_prefetch=1,
            grid=(pieces // STEP_ITEMS,),
            in_specs=in_specs,
            out_specs=(
                pl.BlockSpec((STEP_ITEMS, BLOCK, width), at_step),
                pl.BlockSpec((STEP_ITEMS, BLOCK, width), at_step),
                pl.BlockSpec((lay.places, BLOCK, width), lambda step, tab: (0, 0, 0)),
                pl.BlockSpec(weights_block, fixed),
                pl.BlockSpec(weights_block, fixed),
            ),
        ),
        out_shape=(
            pltpu.HBM((pieces, BLOCK, width), F32),
            pltpu.HBM((pieces, BLOCK, width), BF16),
            pltpu.HBM((lay.places, BLOCK, width), BF16),
            pltpu.HBM(weights_block, F32),
            pltpu.HBM(weights_block, F32),
        ),
        compiler_params=pltpu.CompilerParams(vmem_limit_bytes=32 << 20),
        cost_estimate=pl.CostEstimate(
            flops=flops, bytes_accessed=5 << 20, transcendentals=pieces * 8 * BLOCK * 3 * BLOCK
        ),
        name=f"attention_{chunk}",
    )(
        tab,
        *[
            value
            if value is received
            else pltpu.with_memory_space_constraint(value, pltpu.HBM)
            for value in operands
        ],
    )


def exchanged(value, axis, bit):
    count = lax.axis_size(axis)
    return lax.ppermute(value, axis, [(place, place ^ bit) for place in range(count)])


def summed_over(value, axis, bit):
    low = value.astype(BF16)
    return low.astype(F32) + exchanged(low, axis, bit).astype(F32)


def halved_over(value, axis):
    half = value.shape[0] // 2
    first = lax.rem(lax.axis_index(axis), 2) == 0
    low = value.astype(BF16)
    kept = jnp.where(first, low[:half], low[half:])
    given = jnp.where(first, low[half:], low[:half])
    return kept.astype(F32) + exchanged(given, axis, 1).astype(F32)


def sum_gradients(total, home_b, fold):
    part = halved_over(total, "day")
    bit = 2
    while bit < lax.axis_size("day"):
        part = summed_over(part, "day", bit)
        bit *= 2
    part = halved_over(part, "reach")
    part, home_b = lax.optimization_barrier((part, home_b))
    bit = 2
    while bit < lax.axis_size("reach"):
        part = summed_over(part, "reach", bit)
        bit *= 2
    part, folded = lax.optimization_barrier((part.astype(BF16), fold(home_b)))
    days = lax.axis_size("day")
    both = [
        (reach * days + day, (reach ^ 1) * days + (day ^ 1))
        for reach in range(lax.axis_size("reach"))
        for day in range(days)
    ]
    quarters = (
        part,
        exchanged(part, "reach", 1),
        exchanged(part, "day", 1),
        lax.ppermute(part, ("reach", "day"), both),
    )
    return quarters, folded


def split_kernel(mine, along_reach, along_day, along_both, query_out, key_out, value_out, output_out):
    day_half = lax.rem(lax.axis_index("day"), 2) == 0
    reach_half = lax.rem(lax.axis_index("reach"), 2) == 0

    def quarter(by_day, by_reach):
        near = jnp.where(reach_half == by_reach, mine[...], along_reach[...])
        far = jnp.where(reach_half == by_reach, along_day[...], along_both[...])
        return jnp.where(day_half == by_day, near, far).astype(F32)

    for place, by_reach in enumerate((True, False)):
        rows = quarter(True, by_reach)
        key_out[place * GROUP : (place + 1) * GROUP] = rows[:, :GROUP]
        value_out[place * GROUP : (place + 1) * GROUP] = rows[:, GROUP:]
    query_out[...] = quarter(False, True).T
    output_out[...] = quarter(False, False)


def on_device(
    inputs, upstream, query_weight, key_weight, value_weight, output_weight, partner, counts
):
    days_dev, rows_dev, width = inputs.shape
    assert days_dev == 1 and width == 2 * GROUP
    blocks_dev = rows_dev // BLOCK
    reach_total = lax.axis_size("reach")
    day_total = lax.axis_size("day")
    assert lax.axis_size("head") == CORES
    lay = Layout(blocks_dev, reach_total)
    half = width // 2
    in_blocks = inputs.reshape(blocks_dev, BLOCK, width)
    up_blocks = upstream.reshape(blocks_dev, BLOCK, width)
    pack = jnp.concatenate([key_weight.T, value_weight.T, query_weight.T, output_weight], axis=0)
    pack_other = exchanged(pack, "head", 1)

    smem = pl.BlockSpec(memory_space=pltpu.SMEM)
    in_vmem = pl.BlockSpec(memory_space=pltpu.VMEM)
    anywhere = pl.BlockSpec(memory_space=pl.ANY)
    sent_shape = jax.ShapeDtypeStruct((lay.places, BLOCK, width), BF16)
    sent_a, homes = pl.pallas_call(
        lambda *refs: pick_kernel(lay, *refs),
        out_shape=(sent_shape, jax.ShapeDtypeStruct((lay.homes_size,), jnp.int32)),
        in_specs=[anywhere, anywhere],
        out_specs=(in_vmem, smem),
        scratch_shapes=[
            pltpu.SMEM(partner.shape, jnp.int32),
            pltpu.VMEM((blocks_dev, BLOCK, width), BF16),
            pltpu.SemaphoreType.DMA((2,)),
        ],
        compiler_params=pltpu.CompilerParams(vmem_limit_bytes=16 << 20),
        name="pick",
    )(
        pltpu.with_memory_space_constraint(partner, pltpu.HBM),
        pltpu.with_memory_space_constraint(in_blocks, pltpu.HBM),
    )
    sent_b, prior, tab = pl.pallas_call(
        lambda *refs: deal_kernel(lay, *refs),
        out_shape=(
            sent_shape,
            jax.ShapeDtypeStruct((lay.items, BLOCK, width), BF16),
            jax.ShapeDtypeStruct((lay.size,), jnp.int32),
        ),
        in_specs=[smem, smem, smem, in_vmem],
        out_specs=(in_vmem, in_vmem, smem),
        scratch_shapes=[
            pltpu.SMEM((lay.reach,), jnp.int32),
            pltpu.SMEM((lay.reach,), jnp.int32),
        ],
        compiler_params=pltpu.CompilerParams(vmem_limit_bytes=16 << 20),
        name="deal",
    )(partner, counts, homes, in_blocks)

    def ring(value):
        shape = value.shape
        value = value.reshape(lay.reach, lay.slots * BLOCK, width)
        return lax.all_to_all(value, "reach", 0, 0, tiled=True).reshape(shape)

    next_day = [(d, d + 1) for d in range(day_total - 1)]
    last_day = [(d + 1, d) for d in range(day_total - 1)]
    received_a = ring(sent_a)
    prior_inputs = lax.ppermute(prior, "day", next_day)
    received_b = ring(sent_b)
    shared = (prior_inputs, pack, pack_other)
    own_a, day_a, home_a, *grads = attend(
        lay, 0, tab, in_blocks, up_blocks, received_a, *shared, None
    )
    home_a = ring(home_a)
    day_a = lax.ppermute(day_a, "day", last_day)
    own_b, day_b, home_b, grad_mine, grad_other = attend(
        lay, 1, tab, in_blocks, up_blocks, received_b, *shared, grads
    )
    grad_swapped = exchanged(grad_other, "head", 1)
    home_a, home_b, grad_swapped = lax.optimization_barrier((home_a, home_b, grad_swapped))
    home_b = ring(home_b)
    day_b = lax.ppermute(day_b, "day", last_day)
    half_shape = jax.ShapeDtypeStruct((blocks_dev, BLOCK, half), F32)

    def fold(home_b):
        return pl.pallas_call(
            lambda *refs: fold_kernel(lay, *refs),
            out_shape=(half_shape, half_shape),
            in_specs=[smem] * 2 + [in_vmem] * 6,
            out_specs=[in_vmem] * 2,
            compiler_params=pltpu.CompilerParams(vmem_limit_bytes=16 << 20),
            name="fold",
        )(tab, homes, own_a, own_b, day_a, day_b, home_a, home_b)

    quarters, (keep, give) = sum_gradients(grad_mine + grad_swapped, home_b, fold)
    got = exchanged(give, "head", 1)
    back_blocks = pl.pallas_call(
        add_kernel,
        out_shape=jax.ShapeDtypeStruct((blocks_dev, BLOCK, half), BF16),
        in_specs=[in_vmem] * 2,
        out_specs=in_vmem,
        compiler_params=pltpu.CompilerParams(vmem_limit_bytes=16 << 20),
        name="add",
    )(keep, got)
    back_blocks, quarters = lax.optimization_barrier((back_blocks, quarters))
    weight_grads = pl.pallas_call(
        split_kernel,
        out_shape=(
            jax.ShapeDtypeStruct((width, half), F32),
            jax.ShapeDtypeStruct((width, half), F32),
            jax.ShapeDtypeStruct((width, half), F32),
            jax.ShapeDtypeStruct((half, width), F32),
        ),
        grid=(1,),
        name="split",
    )(*quarters)

    return (back_blocks.reshape(1, rows_dev, half), *weight_grads)


def solution(mesh):
    placed = (
        P(("groups", "day"), "reach", None),
        P(("groups", "day"), "reach", None),
        P(None, "head"),
        P(None, "head"),
        P(None, "head"),
        P("head", None),
        P("groups"),
        P("groups"),
    )
    return jax.shard_map(
        on_device,
        mesh=mesh,
        in_specs=placed,
        out_specs=(
            P(("groups", "day"), "reach", "head"),
            P("groups", "head"),
            P("groups", "head"),
            P("groups", "head"),
            P(("groups", "head"), None),
        ),
        check_vma=False,
    )
```

```python
import jax
import jax.numpy as jnp
from jax import lax
from jax.experimental import pallas as pl
from jax.experimental.pallas import tpu as pltpu
from jax.sharding import PartitionSpec as P

HD = 32
BLOCK = 128
GROUP = 128
CORES = 2
CHUNKS = 2
WORKERS = CORES * CHUNKS
F32 = jnp.float32
BF16 = jnp.bfloat16
PACK = 4
STEP_ITEMS = 4
LOG2E = 1.4426950408889634


class Layout:
    def __init__(self, blocks_dev, reach_total):
        self.blocks = blocks_dev
        self.items = blocks_dev // CORES
        self.chunk_items = self.items // CHUNKS
        self.reach = reach_total
        self.slots = max(1, 2 * blocks_dev // reach_total // WORKERS)
        self.places = reach_total * self.slots
        self.block_of = 0
        self.recv_of = self.items
        self.count_own = 2 * self.items
        self.count_partner = 3 * self.items
        self.owner_of = 4 * self.items
        self.item_of = self.owner_of + blocks_dev
        self.core = self.item_of + blocks_dev
        self.later_day = self.core + 1
        self.size = -(-(self.core + 2) // 128) * 128
        self.spare = blocks_dev
        self.home_of = 0
        self.chunk_of = blocks_dev + 1
        self.asker_of = 2 * (blocks_dev + 1)
        self.picks = 3 * (blocks_dev + 1)
        self.spare_pick = self.picks + CHUNKS * self.places
        self.homes_size = -(-(self.spare_pick + 1) // 128) * 128


def pick_kernel(lay, partner_hbm, inputs, sent, homes, partner, held, sems):
    bd, slots = lay.blocks, lay.slots
    reach_pos, core = lax.axis_index("reach"), lax.axis_index("head")
    table_copy = pltpu.make_async_copy(partner_hbm, partner, sems.at[0])
    table_copy.start()
    copy = pltpu.make_async_copy(inputs, held, sems.at[1])
    copy.start()
    for place in range(CHUNKS * lay.places):
        homes[lay.picks + place] = 0
    table_copy.wait()

    def one_reach(peer, carry):
        base = jnp.int32(0)
        wanted = []
        for index in range(bd):
            block = partner[peer * bd + index]
            source = lax.div(block, bd)
            base = base + jnp.where(source < reach_pos, 1, 0)
            wanted.append((source == reach_pos, lax.rem(block, bd)))
        rank = jnp.int32(0)
        for hit, local in wanted:
            place = base + rank
            owner = lax.rem(place, CORES)
            chunk = lax.rem(lax.div(place, CORES), CHUNKS)
            slot = peer * slots + jnp.minimum(lax.div(rank, WORKERS), slots - 1)
            target = jnp.where(hit, local, lay.spare)
            homes[lay.home_of + target] = slot
            homes[lay.chunk_of + target] = chunk
            homes[lay.asker_of + target] = owner
            pick = lay.picks + chunk * lay.places + slot
            homes[jnp.where(hit & (owner == core), pick, lay.spare_pick)] = local
            rank = rank + jnp.where(hit, 1, 0)
        return carry

    lax.fori_loop(0, lay.reach, one_reach, 0)
    copy.wait()
    for place in range(lay.places):
        sent[place] = held[homes[lay.picks + place]]


def deal_kernel(lay, partner, counts, homes, inputs, sent, prior, tab, start, used):
    bd, slots = lay.blocks, lay.slots
    reach_pos, core = lax.axis_index("reach"), lax.axis_index("head")

    def clear(index, carry):
        used[index] = 0
        start[index] = 0
        return carry

    lax.fori_loop(0, lay.reach, clear, 0, unroll=True)

    def count(index, carry):
        source = lax.div(partner[reach_pos * bd + index], bd)
        start[source] = start[source] + 1
        return carry

    lax.fori_loop(0, bd, count, 0)

    def prefix(index, total):
        here = start[index]
        start[index] = total
        return total + here

    lax.fori_loop(0, lay.reach, prefix, jnp.int32(0))

    def assign(index, carry):
        wanted = partner[reach_pos * bd + index]
        source = lax.div(wanted, bd)
        rank = used[source]
        used[source] = rank + 1
        place = start[source] + rank
        owner = lax.rem(place, CORES)
        chunk = lax.rem(lax.div(place, CORES), CHUNKS)
        item = chunk * lay.chunk_items + lax.div(place, WORKERS)
        slot = jnp.minimum(lax.div(rank, WORKERS), slots - 1)
        tab[lay.owner_of + index] = owner
        tab[lay.item_of + index] = item

        @pl.when(owner == core)
        def _():
            tab[lay.block_of + item] = index
            tab[lay.recv_of + item] = source * slots + slot
            tab[lay.count_own + item] = counts[reach_pos * bd + index]
            tab[lay.count_partner + item] = counts[wanted]

        return carry

    lax.fori_loop(0, bd, assign, 0)
    tab[lay.core] = core
    tab[lay.later_day] = jnp.where(lax.axis_index("day") > 0, 1, 0)

    def pick(place, carry):
        sent[place] = inputs[homes[lay.picks + lay.places + place]]
        return carry

    def pick_prior(item, carry):
        prior[item] = inputs[tab[lay.block_of + item]]
        return carry

    lax.fori_loop(0, lay.places, pick, 0)
    lax.fori_loop(0, lay.items, pick_prior, 0)


def dot(left, right):
    return lax.dot_general(left, right, (((1,), (0,)), ((), ())), preferred_element_type=F32)


def dot_t(left, right):
    return lax.dot_general(left, right, (((1,), (1,)), ((), ())), preferred_element_type=F32)


def attention_kernel(lay, chunk, tab, *refs):
    step = pl.program_id(0)
    read, refs = refs[: 4 * STEP_ITEMS], refs[4 * STEP_ITEMS :]
    mine_ref, other_ref, *refs = refs
    if chunk:
        start_mine_ref, start_other_ref, *refs = refs
        own_out_ref, day_ref, home_ref, *piece_refs, grad_mine_ref, grad_other_ref = refs
    else:
        own_out_ref, day_ref, home_ref, grad_mine_ref, grad_other_ref = refs
    factor = HD ** (-0.5)
    per_group = GROUP // HD // PACK

    @pl.when(step == 0)
    def _():
        if chunk:
            grad_mine_ref[...] = start_mine_ref[...]
            grad_other_ref[...] = start_other_ref[...]
        else:
            grad_mine_ref[...] = jnp.zeros_like(grad_mine_ref)
            grad_other_ref[...] = jnp.zeros_like(grad_other_ref)

    rows = lax.broadcasted_iota(jnp.int32, (BLOCK, PACK * BLOCK), 0)
    lane_head = lax.broadcasted_iota(jnp.int32, (BLOCK, GROUP), 1) // HD
    query_t = jnp.concatenate([mine_ref[256:384, :], other_ref[256:384, :]], axis=0)
    output_w = jnp.concatenate([mine_ref[384:512, :], other_ref[384:512, :]], axis=0)

    class Item:
        pass

    def begin(place):
        it = Item()
        own_ref, up_ref, partner_ref, prior_ref = read[4 * place : 4 * place + 4]
        it.place = place
        item = step * STEP_ITEMS + place + chunk * lay.chunk_items
        it.item = item
        it.own, it.up = own_ref[0], up_ref[0]
        it.inputs = jnp.concatenate([it.own, partner_ref[0], prior_ref[0]], axis=0)
        queries = dot_t(it.own, query_t)
        back_out = dot_t(it.up, output_w)
        count_own = tab[lay.count_own + item]
        it.counts = (count_own, tab[lay.count_partner + item], count_own * tab[lay.later_day])
        it.groups = []
        for group, weights_ref in enumerate((mine_ref, other_ref)):
            kv_t = weights_ref[0:256, :]
            kv = dot_t(it.inputs, kv_t).astype(BF16)
            lanes = slice(group * GROUP, (group + 1) * GROUP)
            it.groups.append((kv_t, kv, kv.T, queries[:, lanes], back_out[:, lanes]))
        it.outputs_t, it.back_query_t = [], []
        it.keys, it.values = ([], []), ([], [])
        return it

    def start(it, part):
        _, kv, _, group_queries, group_back = it.groups[part // per_group]
        heads = [part % per_group * PACK + h for h in range(PACK)]
        query_pack, back_pack = (
            jnp.concatenate(
                [jnp.where(lane_head == h, rows_of, 0.0) for h in heads], axis=0
            ).astype(BF16)
            for rows_of in (group_queries, group_back)
        )
        logits = dot_t(kv[:, :GROUP], query_pack)
        return it, part, query_pack, back_pack, logits, dot_t(kv[:, GROUP:], back_pack)

    def middle(it, part, query_pack, back_pack, logits, back_weights):
        logits = jnp.concatenate(
            [
                jnp.where(rows < count, logits[index * BLOCK : (index + 1) * BLOCK], -1e30)
                for index, count in enumerate(it.counts)
            ],
            axis=0,
        )
        highest = jnp.max(logits, axis=0, keepdims=True)
        raised = jnp.exp2((logits - highest) * (factor * LOG2E))
        scale = 1.0 / jnp.sum(raised, axis=0, keepdims=True)
        weights = raised * scale
        center = jnp.sum(weights * back_weights, axis=0, keepdims=True)
        back_logits = (weights * ((back_weights - center) * factor)).astype(BF16)
        return it, part, query_pack, back_pack, weights.astype(BF16), back_logits

    def finish(it, part, query_pack, back_pack, weights_low, back_logits):
        group = part // per_group
        kv_cols = it.groups[group][2]
        it.values[group].append(dot(weights_low, back_pack))
        it.keys[group].append(dot(back_logits, query_pack))
        size = PACK * HD
        first = part % per_group * size
        out_t = dot(kv_cols[GROUP + first : GROUP + first + size, :], weights_low)
        query_grad_t = dot(kv_cols[first : first + size, :], back_logits)
        for h in range(PACK):
            lanes = slice(h * BLOCK, (h + 1) * BLOCK)
            it.outputs_t.append(out_t[h * HD : (h + 1) * HD, lanes])
            it.back_query_t.append(query_grad_t[h * HD : (h + 1) * HD, lanes])

    def end(it):
        inputs_t = it.inputs.T
        back_inputs = None
        for group, grad_ref in enumerate((grad_mine_ref, grad_other_ref)):
            kv_t = it.groups[group][0]
            keys, values = it.keys[group], it.values[group]
            back_kv = jnp.concatenate(
                [sum(keys[1:], keys[0]), sum(values[1:], values[0])], axis=1
            ).astype(BF16)
            term = dot(back_kv, kv_t)
            back_inputs = term if back_inputs is None else back_inputs + term
            grad_ref[0:256, :] += dot(inputs_t, back_kv)
        outputs_t = jnp.concatenate(it.outputs_t, axis=0).astype(BF16)
        back_query_t = jnp.concatenate(it.back_query_t, axis=0).astype(BF16)
        query_grad = dot(back_query_t, it.own)
        output_grad = dot(outputs_t, it.up)
        grad_mine_ref[256:384, :] += query_grad[:GROUP]
        grad_other_ref[256:384, :] += query_grad[GROUP:]
        grad_mine_ref[384:512, :] += output_grad[:GROUP]
        grad_other_ref[384:512, :] += output_grad[GROUP:]
        own_out_ref[it.place] = back_inputs[:BLOCK] + dot(back_query_t.T, query_t)
        home_ref[tab[lay.recv_of + it.item]] = back_inputs[BLOCK : 2 * BLOCK].astype(BF16)
        day_ref[it.place] = back_inputs[2 * BLOCK :].astype(BF16)

    parts = 2 * per_group
    items = [begin(0)]
    started = start(items[0], 0)
    waiting = None
    ended = 0
    for index in range(STEP_ITEMS * parts):
        following = None
        if index + 1 < STEP_ITEMS * parts:
            place, part = divmod(index + 1, parts)
            if part == 0:
                items.append(begin(place))
            following = start(items[place], part)
        if waiting is not None:
            finish(*waiting)
            if waiting[1] == parts - 1:
                end(waiting[0])
        waiting = middle(*started)
        started = following
    finish(*waiting)
    end(waiting[0])

    if chunk:
        @pl.when(step == pl.num_programs(0) - 1)
        def _():
            first = lax.rem(lax.axis_index("day"), 2) == 0
            for place, grad_ref in enumerate((grad_mine_ref, grad_other_ref)):
                half = grad_ref.shape[0] // 2
                low, high = grad_ref[:half], grad_ref[half:]
                piece_refs[2 * place][...] = jnp.where(first, low, high).astype(BF16)
                piece_refs[2 * place + 1][...] = jnp.where(first, high, low).astype(BF16)


def fold_kernel(lay, tab, homes, own_a, own_b, day_a, day_b, home_a, home_b, keep, give):
    core = tab[lay.core]
    half = keep.shape[2]

    def one(block, carry):
        item = tab[lay.item_of + block]
        mine = tab[lay.owner_of + block] == core
        place = homes[lay.home_of + block]
        asked = homes[lay.asker_of + block] == core
        early = homes[lay.chunk_of + block] == 0
        in_a = item < lay.chunk_items
        item_a = jnp.minimum(item, lay.chunk_items - 1)
        item_b = jnp.maximum(item - lay.chunk_items, 0)
        own = jnp.where(in_a, own_a[item_a], own_b[item_b])
        own += jnp.where(in_a, day_a[item_a].astype(F32), day_b[item_b].astype(F32))
        home = jnp.where(early, home_a[place].astype(F32), home_b[place].astype(F32))
        total = jnp.where(mine, own, 0.0) + jnp.where(asked, home, 0.0)
        low, high = total[:, :half], total[:, half:]
        keep[block] = jnp.where(core == 0, low, high)
        give[block] = jnp.where(core == 0, high, low)
        return carry

    lax.fori_loop(0, lay.blocks, one, 0)


def add_kernel(kept, got, out):
    out[...] = (kept[...] + got[...]).astype(BF16)


def attend(lay, chunk, tab, in_blocks, up_blocks, received, prior_inputs, pack, pack_other, carried):
    width = in_blocks.shape[-1]
    offset = chunk * lay.chunk_items

    def at_item(place):
        return lambda step, tab: (offset + step * STEP_ITEMS + place, 0, 0)

    def at_block(place):
        return lambda step, tab: (tab[lay.block_of + offset + step * STEP_ITEMS + place], 0, 0)

    def at_recv(place):
        return lambda step, tab: (tab[lay.recv_of + offset + step * STEP_ITEMS + place], 0, 0)

    def at_step(step, tab):
        return (step, 0, 0)

    def fixed(step, tab):
        return (0, 0)

    full_block = (1, BLOCK, width)
    weights_block = (4 * GROUP, width)
    in_specs, operands = [], []
    for place in range(STEP_ITEMS):
        in_specs += [
            pl.BlockSpec(full_block, at_block(place)),
            pl.BlockSpec(full_block, at_block(place)),
            pl.BlockSpec(full_block, at_recv(place)),
            pl.BlockSpec(full_block, at_item(place)),
        ]
        operands += [in_blocks, up_blocks, received, prior_inputs]
    in_specs += [pl.BlockSpec(weights_block, fixed)] * 2
    operands += [pack, pack_other]
    if chunk:
        in_specs += [pl.BlockSpec(weights_block, fixed)] * 2
        operands += carried
    pieces = lay.chunk_items
    grads = [pltpu.HBM(weights_block, F32)] * 2
    if chunk:
        grads = [jax.ShapeDtypeStruct((2 * GROUP, width), BF16)] * 4
    flops = 2 * pieces * (23 * BLOCK * width * width + 24 * BLOCK * 3 * BLOCK * 512)
    return pl.pallas_call(
        lambda *refs: attention_kernel(lay, chunk, *refs),
        grid_spec=pltpu.PrefetchScalarGridSpec(
            num_scalar_prefetch=1,
            grid=(pieces // STEP_ITEMS,),
            in_specs=in_specs,
            out_specs=(
                pl.BlockSpec((STEP_ITEMS, BLOCK, width), at_step),
                pl.BlockSpec((STEP_ITEMS, BLOCK, width), at_step),
                pl.BlockSpec((lay.places, BLOCK, width), lambda step, tab: (0, 0, 0)),
                *[pl.BlockSpec(grad.shape, fixed) for grad in grads],
            ),
            scratch_shapes=[pltpu.VMEM(weights_block, F32)] * (2 if chunk else 0),
        ),
        out_shape=(
            pltpu.HBM((pieces, BLOCK, width), F32),
            pltpu.HBM((pieces, BLOCK, width), BF16),
            pltpu.HBM((lay.places, BLOCK, width), BF16),
            *grads,
        ),
        compiler_params=pltpu.CompilerParams(vmem_limit_bytes=32 << 20),
        cost_estimate=pl.CostEstimate(
            flops=flops, bytes_accessed=5 << 20, transcendentals=pieces * 8 * BLOCK * 3 * BLOCK
        ),
        name=f"attention_{chunk}",
    )(
        tab,
        *[
            value
            if value is received
            else pltpu.with_memory_space_constraint(value, pltpu.HBM)
            for value in operands
        ],
    )


def exchanged(value, axis, bit):
    count = lax.axis_size(axis)
    return lax.ppermute(value, axis, [(place, place ^ bit) for place in range(count)])


def summed_over(value, axis, bit):
    low = value.astype(BF16)
    return low.astype(F32) + exchanged(low, axis, bit).astype(F32)


def neighbours(axis, other):
    size = lax.axis_size(other)
    return [
        (place * size + at, (place ^ 1) * size + (at ^ 1))
        for place in range(lax.axis_size(axis))
        for at in range(size)
    ]


def sum_gradients(part, home_b, fold):
    bit = 2
    while bit < lax.axis_size("day"):
        part = summed_over(part, "day", bit)
        bit *= 2
    half = part.shape[0] // 2
    first = lax.rem(lax.axis_index("reach"), 2) == 0
    low = part.astype(BF16)
    kept = jnp.where(first, low[:half], low[half:])
    given = jnp.where(first, low[half:], low[:half])
    part = kept.astype(F32) + exchanged(given, "reach", 1).astype(F32)
    part, home_b = lax.optimization_barrier((part, home_b))
    bit = 2
    while bit < lax.axis_size("reach"):
        part = summed_over(part, "reach", bit)
        bit *= 2
    part, folded = lax.optimization_barrier((part.astype(BF16), fold(home_b)))
    quarters = (
        part,
        exchanged(part, "reach", 1),
        exchanged(part, "day", 1),
        lax.ppermute(part, ("reach", "day"), neighbours("reach", "day")),
    )
    return quarters, folded


def split_kernel(mine, along_reach, along_day, along_both, query_out, key_out, value_out, output_out):
    day_half = lax.rem(lax.axis_index("day"), 2) == 0
    reach_half = lax.rem(lax.axis_index("reach"), 2) == 0

    def quarter(by_day, by_reach):
        near = jnp.where(reach_half == by_reach, mine[...], along_reach[...])
        far = jnp.where(reach_half == by_reach, along_day[...], along_both[...])
        return jnp.where(day_half == by_day, near, far).astype(F32)

    for place, by_reach in enumerate((True, False)):
        rows = quarter(True, by_reach)
        key_out[place * GROUP : (place + 1) * GROUP] = rows[:, :GROUP]
        value_out[place * GROUP : (place + 1) * GROUP] = rows[:, GROUP:]
    query_out[...] = quarter(False, True).T
    output_out[...] = quarter(False, False)


def on_device(
    inputs, upstream, query_weight, key_weight, value_weight, output_weight, partner, counts
):
    days_dev, rows_dev, width = inputs.shape
    assert days_dev == 1 and width == 2 * GROUP
    blocks_dev = rows_dev // BLOCK
    reach_total = lax.axis_size("reach")
    day_total = lax.axis_size("day")
    assert lax.axis_size("head") == CORES
    lay = Layout(blocks_dev, reach_total)
    half = width // 2
    in_blocks = inputs.reshape(blocks_dev, BLOCK, width)
    up_blocks = upstream.reshape(blocks_dev, BLOCK, width)
    pack = jnp.concatenate([key_weight.T, value_weight.T, query_weight.T, output_weight], axis=0)
    pack_other = exchanged(pack, "head", 1)

    smem = pl.BlockSpec(memory_space=pltpu.SMEM)
    in_vmem = pl.BlockSpec(memory_space=pltpu.VMEM)
    anywhere = pl.BlockSpec(memory_space=pl.ANY)
    sent_shape = jax.ShapeDtypeStruct((lay.places, BLOCK, width), BF16)
    sent_a, homes = pl.pallas_call(
        lambda *refs: pick_kernel(lay, *refs),
        out_shape=(sent_shape, jax.ShapeDtypeStruct((lay.homes_size,), jnp.int32)),
        in_specs=[anywhere, anywhere],
        out_specs=(in_vmem, smem),
        scratch_shapes=[
            pltpu.SMEM(partner.shape, jnp.int32),
            pltpu.VMEM((blocks_dev, BLOCK, width), BF16),
            pltpu.SemaphoreType.DMA((2,)),
        ],
        compiler_params=pltpu.CompilerParams(vmem_limit_bytes=16 << 20),
        name="pick",
    )(
        pltpu.with_memory_space_constraint(partner, pltpu.HBM),
        pltpu.with_memory_space_constraint(in_blocks, pltpu.HBM),
    )
    sent_b, prior, tab = pl.pallas_call(
        lambda *refs: deal_kernel(lay, *refs),
        out_shape=(
            sent_shape,
            jax.ShapeDtypeStruct((lay.items, BLOCK, width), BF16),
            jax.ShapeDtypeStruct((lay.size,), jnp.int32),
        ),
        in_specs=[smem, smem, smem, in_vmem],
        out_specs=(in_vmem, in_vmem, smem),
        scratch_shapes=[
            pltpu.SMEM((lay.reach,), jnp.int32),
            pltpu.SMEM((lay.reach,), jnp.int32),
        ],
        compiler_params=pltpu.CompilerParams(vmem_limit_bytes=16 << 20),
        name="deal",
    )(partner, counts, homes, in_blocks)

    def ring(value):
        shape = value.shape
        value = value.reshape(lay.reach, lay.slots * BLOCK, width)
        return lax.all_to_all(value, "reach", 0, 0, tiled=True).reshape(shape)

    next_day = [(d, d + 1) for d in range(day_total - 1)]
    last_day = [(d + 1, d) for d in range(day_total - 1)]
    received_a = ring(sent_a)
    prior_inputs = lax.ppermute(prior, "day", next_day)
    received_b = ring(sent_b)
    shared = (prior_inputs, pack, pack_other)
    own_a, day_a, home_a, *grads = attend(
        lay, 0, tab, in_blocks, up_blocks, received_a, *shared, None
    )
    home_a = ring(home_a)
    day_a = lax.ppermute(day_a, "day", last_day)
    own_b, day_b, home_b, kept, to_day, to_core, to_both = attend(
        lay, 1, tab, in_blocks, up_blocks, received_b, *shared, grads
    )
    pieces = (
        exchanged(to_day, "day", 1),
        exchanged(to_core, "head", 1),
        lax.ppermute(to_both, ("day", "head"), neighbours("day", "head")),
    )
    home_a, home_b, kept = lax.optimization_barrier((home_a, home_b, kept))
    pieces = (kept, *pieces)
    home_b = ring(home_b)
    day_b = lax.ppermute(day_b, "day", last_day)
    half_shape = jax.ShapeDtypeStruct((blocks_dev, BLOCK, half), F32)

    def fold(home_b):
        return pl.pallas_call(
            lambda *refs: fold_kernel(lay, *refs),
            out_shape=(half_shape, half_shape),
            in_specs=[smem] * 2 + [in_vmem] * 6,
            out_specs=[in_vmem] * 2,
            compiler_params=pltpu.CompilerParams(vmem_limit_bytes=16 << 20),
            name="fold",
        )(tab, homes, own_a, own_b, day_a, day_b, home_a, home_b)

    quarters, (keep, give) = sum_gradients(
        sum(piece.astype(F32) for piece in pieces), home_b, fold
    )
    got = exchanged(give, "head", 1)
    back_blocks = pl.pallas_call(
        add_kernel,
        out_shape=jax.ShapeDtypeStruct((blocks_dev, BLOCK, half), BF16),
        in_specs=[in_vmem] * 2,
        out_specs=in_vmem,
        compiler_params=pltpu.CompilerParams(vmem_limit_bytes=16 << 20),
        name="add",
    )(keep, got)
    back_blocks, quarters = lax.optimization_barrier((back_blocks, quarters))
    weight_grads = pl.pallas_call(
        split_kernel,
        out_shape=(
            jax.ShapeDtypeStruct((width, half), F32),
            jax.ShapeDtypeStruct((width, half), F32),
            jax.ShapeDtypeStruct((width, half), F32),
            jax.ShapeDtypeStruct((half, width), F32),
        ),
        grid=(1,),
        compiler_params=pltpu.CompilerParams(vmem_limit_bytes=16 << 20),
        name="split",
    )(*quarters)

    return (back_blocks.reshape(1, rows_dev, half), *weight_grads)


def solution(mesh):
    placed = (
        P(("groups", "day"), "reach", None),
        P(("groups", "day"), "reach", None),
        P(None, "head"),
        P(None, "head"),
        P(None, "head"),
        P("head", None),
        P("groups"),
        P("groups"),
    )
    return jax.shard_map(
        on_device,
        mesh=mesh,
        in_specs=placed,
        out_specs=(
            P(("groups", "day"), "reach", "head"),
            P("groups", "head"),
            P("groups", "head"),
            P("groups", "head"),
            P(("groups", "head"), None),
        ),
        check_vma=False,
    )
```

```python
import jax
import jax.numpy as jnp
from jax import lax
from jax.experimental import pallas as pl
from jax.experimental.pallas import tpu as pltpu
from jax.sharding import PartitionSpec as P

HD = 32
BLOCK = 128
GROUP = 128
CORES = 2
CHUNKS = 2
WORKERS = CORES * CHUNKS
F32 = jnp.float32
BF16 = jnp.bfloat16
PACK = 4
STEP_ITEMS = 4
LOG2E = 1.4426950408889634


class Layout:
    def __init__(self, blocks_dev, reach_total):
        self.blocks = blocks_dev
        self.items = blocks_dev // CORES
        self.chunk_items = self.items // CHUNKS
        self.reach = reach_total
        self.slots = max(1, 2 * blocks_dev // reach_total // WORKERS)
        self.places = reach_total * self.slots
        self.block_of = 0
        self.recv_of = self.items
        self.count_own = 2 * self.items
        self.count_partner = 3 * self.items
        self.owner_of = 4 * self.items
        self.item_of = self.owner_of + blocks_dev
        self.core = self.item_of + blocks_dev
        self.later_day = self.core + 1
        self.size = -(-(self.core + 2) // 128) * 128
        self.spare = blocks_dev
        self.home_of = 0
        self.chunk_of = blocks_dev + 1
        self.asker_of = 2 * (blocks_dev + 1)
        self.picks = 3 * (blocks_dev + 1)
        self.spare_pick = self.picks + CHUNKS * self.places
        self.homes_size = -(-(self.spare_pick + 1) // 128) * 128


def quotient(value, count):
    if count & (count - 1) == 0:
        return lax.shift_right_logical(value, jnp.int32(count.bit_length() - 1))
    return lax.div(value, count)


def remainder(value, count):
    if count & (count - 1) == 0:
        return lax.bitwise_and(value, jnp.int32(count - 1))
    return lax.rem(value, count)


def pick_kernel(lay, partner_hbm, inputs, sent, homes, partner, held, sems):
    bd, slots = lay.blocks, lay.slots
    reach_pos, core = lax.axis_index("reach"), lax.axis_index("head")
    table_copy = pltpu.make_async_copy(partner_hbm, partner, sems.at[0])
    table_copy.start()
    copy = pltpu.make_async_copy(inputs, held, sems.at[1])
    copy.start()
    for place in range(CHUNKS * lay.places):
        homes[lay.picks + place] = 0
    table_copy.wait()

    def one_reach(peer, carry):
        base = jnp.int32(0)
        wanted = []
        for index in range(bd):
            block = partner[peer * bd + index]
            source = quotient(block, bd)
            base = base + jnp.where(source < reach_pos, 1, 0)
            wanted.append((source == reach_pos, remainder(block, bd)))
        rank = jnp.int32(0)
        for hit, local in wanted:
            place = base + rank
            owner = remainder(place, CORES)
            chunk = remainder(quotient(place, CORES), CHUNKS)
            slot = peer * slots + jnp.minimum(quotient(rank, WORKERS), slots - 1)
            target = jnp.where(hit, local, lay.spare)
            homes[lay.home_of + target] = slot
            homes[lay.chunk_of + target] = chunk
            homes[lay.asker_of + target] = owner
            pick = lay.picks + chunk * lay.places + slot
            homes[jnp.where(hit & (owner == core), pick, lay.spare_pick)] = local
            rank = rank + jnp.where(hit, 1, 0)
        return carry

    lax.fori_loop(0, lay.reach, one_reach, 0)
    copy.wait()
    for place in range(lay.places):
        sent[place] = held[homes[lay.picks + place]]


def deal_kernel(lay, partner, counts, homes, inputs, sent, prior, tab, start, used):
    bd, slots = lay.blocks, lay.slots
    reach_pos, core = lax.axis_index("reach"), lax.axis_index("head")

    def clear(index, carry):
        used[index] = 0
        start[index] = 0
        return carry

    lax.fori_loop(0, lay.reach, clear, 0, unroll=True)

    def count(index, carry):
        source = quotient(partner[reach_pos * bd + index], bd)
        start[source] = start[source] + 1
        return carry

    lax.fori_loop(0, bd, count, 0)

    def prefix(index, total):
        here = start[index]
        start[index] = total
        return total + here

    lax.fori_loop(0, lay.reach, prefix, jnp.int32(0))

    def assign(index, carry):
        wanted = partner[reach_pos * bd + index]
        source = quotient(wanted, bd)
        rank = used[source]
        used[source] = rank + 1
        place = start[source] + rank
        owner = remainder(place, CORES)
        chunk = remainder(quotient(place, CORES), CHUNKS)
        item = chunk * lay.chunk_items + quotient(place, WORKERS)
        slot = jnp.minimum(quotient(rank, WORKERS), slots - 1)
        tab[lay.owner_of + index] = owner
        tab[lay.item_of + index] = item

        @pl.when(owner == core)
        def _():
            tab[lay.block_of + item] = index
            tab[lay.recv_of + item] = source * slots + slot
            tab[lay.count_own + item] = counts[reach_pos * bd + index]
            tab[lay.count_partner + item] = counts[wanted]

        return carry

    lax.fori_loop(0, bd, assign, 0)
    tab[lay.core] = core
    tab[lay.later_day] = jnp.where(lax.axis_index("day") > 0, 1, 0)

    def pick(place, carry):
        sent[place] = inputs[homes[lay.picks + lay.places + place]]
        return carry

    def pick_prior(item, carry):
        prior[item] = inputs[tab[lay.block_of + item]]
        return carry

    lax.fori_loop(0, lay.places, pick, 0)
    lax.fori_loop(0, lay.items, pick_prior, 0)


def dot(left, right):
    return lax.dot_general(left, right, (((1,), (0,)), ((), ())), preferred_element_type=F32)


def dot_t(left, right):
    return lax.dot_general(left, right, (((1,), (1,)), ((), ())), preferred_element_type=F32)


def attention_kernel(lay, chunk, tab, *refs):
    step = pl.program_id(0)
    read, refs = refs[: 4 * STEP_ITEMS], refs[4 * STEP_ITEMS :]
    mine_ref, other_ref, *refs = refs
    if chunk:
        start_mine_ref, start_other_ref, *refs = refs
        own_out_ref, day_ref, home_ref, *piece_refs, grad_mine_ref, grad_other_ref = refs
    else:
        own_out_ref, day_ref, home_ref, grad_mine_ref, grad_other_ref = refs
    factor = HD ** (-0.5)
    per_group = GROUP // HD // PACK

    @pl.when(step == 0)
    def _():
        if chunk:
            grad_mine_ref[...] = start_mine_ref[...]
            grad_other_ref[...] = start_other_ref[...]
        else:
            grad_mine_ref[...] = jnp.zeros_like(grad_mine_ref)
            grad_other_ref[...] = jnp.zeros_like(grad_other_ref)

    rows = lax.broadcasted_iota(jnp.int32, (BLOCK, PACK * BLOCK), 0)
    lane_head = lax.broadcasted_iota(jnp.int32, (BLOCK, GROUP), 1) // HD
    query_t = jnp.concatenate([mine_ref[256:384, :], other_ref[256:384, :]], axis=0)
    output_w = jnp.concatenate([mine_ref[384:512, :], other_ref[384:512, :]], axis=0)

    class Item:
        pass

    def begin(place):
        it = Item()
        own_ref, up_ref, partner_ref, prior_ref = read[4 * place : 4 * place + 4]
        it.place = place
        item = step * STEP_ITEMS + place + chunk * lay.chunk_items
        it.item = item
        it.own, it.up = own_ref[0], up_ref[0]
        it.inputs = jnp.concatenate([it.own, partner_ref[0], prior_ref[0]], axis=0)
        queries = dot_t(it.own, query_t)
        back_out = dot_t(it.up, output_w)
        count_own = tab[lay.count_own + item]
        it.counts = (count_own, tab[lay.count_partner + item], count_own * tab[lay.later_day])
        it.groups = []
        for group, weights_ref in enumerate((mine_ref, other_ref)):
            kv_t = weights_ref[0:256, :]
            kv = dot_t(it.inputs, kv_t).astype(BF16)
            lanes = slice(group * GROUP, (group + 1) * GROUP)
            it.groups.append((kv_t, kv, kv.T, queries[:, lanes], back_out[:, lanes]))
        it.outputs_t, it.back_query_t = [], []
        it.keys, it.values = ([], []), ([], [])
        return it

    def start(it, part):
        _, kv, _, group_queries, group_back = it.groups[part // per_group]
        heads = [part % per_group * PACK + h for h in range(PACK)]
        query_pack, back_pack = (
            jnp.concatenate(
                [jnp.where(lane_head == h, rows_of, 0.0) for h in heads], axis=0
            ).astype(BF16)
            for rows_of in (group_queries, group_back)
        )
        logits = dot_t(kv[:, :GROUP], query_pack)
        return it, part, query_pack, back_pack, logits, dot_t(kv[:, GROUP:], back_pack)

    def middle(it, part, query_pack, back_pack, logits, back_weights):
        logits = jnp.concatenate(
            [
                jnp.where(rows < count, logits[index * BLOCK : (index + 1) * BLOCK], -1e30)
                for index, count in enumerate(it.counts)
            ],
            axis=0,
        )
        highest = jnp.max(logits, axis=0, keepdims=True)
        raised = jnp.exp2((logits - highest) * (factor * LOG2E))
        scale = 1.0 / jnp.sum(raised, axis=0, keepdims=True)
        weights = raised * scale
        center = jnp.sum(weights * back_weights, axis=0, keepdims=True)
        back_logits = (weights * ((back_weights - center) * factor)).astype(BF16)
        return it, part, query_pack, back_pack, weights.astype(BF16), back_logits

    def finish(it, part, query_pack, back_pack, weights_low, back_logits):
        group = part // per_group
        kv_cols = it.groups[group][2]
        it.values[group].append(dot(weights_low, back_pack))
        it.keys[group].append(dot(back_logits, query_pack))
        size = PACK * HD
        first = part % per_group * size
        out_t = dot(kv_cols[GROUP + first : GROUP + first + size, :], weights_low)
        query_grad_t = dot(kv_cols[first : first + size, :], back_logits)
        for h in range(PACK):
            lanes = slice(h * BLOCK, (h + 1) * BLOCK)
            it.outputs_t.append(out_t[h * HD : (h + 1) * HD, lanes])
            it.back_query_t.append(query_grad_t[h * HD : (h + 1) * HD, lanes])

    def end(it):
        inputs_t = it.inputs.T
        back_inputs = None
        for group, grad_ref in enumerate((grad_mine_ref, grad_other_ref)):
            kv_t = it.groups[group][0]
            keys, values = it.keys[group], it.values[group]
            back_kv = jnp.concatenate(
                [sum(keys[1:], keys[0]), sum(values[1:], values[0])], axis=1
            ).astype(BF16)
            term = dot(back_kv, kv_t)
            back_inputs = term if back_inputs is None else back_inputs + term
            grad_ref[0:256, :] += dot(inputs_t, back_kv)
        outputs_t = jnp.concatenate(it.outputs_t, axis=0).astype(BF16)
        back_query_t = jnp.concatenate(it.back_query_t, axis=0).astype(BF16)
        query_grad = dot(back_query_t, it.own)
        output_grad = dot(outputs_t, it.up)
        grad_mine_ref[256:384, :] += query_grad[:GROUP]
        grad_other_ref[256:384, :] += query_grad[GROUP:]
        grad_mine_ref[384:512, :] += output_grad[:GROUP]
        grad_other_ref[384:512, :] += output_grad[GROUP:]
        own_out_ref[it.place] = back_inputs[:BLOCK] + dot(back_query_t.T, query_t)
        home_ref[tab[lay.recv_of + it.item]] = back_inputs[BLOCK : 2 * BLOCK].astype(BF16)
        day_ref[it.place] = back_inputs[2 * BLOCK :].astype(BF16)

    parts = 2 * per_group
    items = [begin(0)]
    started = start(items[0], 0)
    waiting = None
    ended = 0
    for index in range(STEP_ITEMS * parts):
        following = None
        if index + 1 < STEP_ITEMS * parts:
            place, part = divmod(index + 1, parts)
            if part == 0:
                items.append(begin(place))
            following = start(items[place], part)
        if waiting is not None:
            finish(*waiting)
            if waiting[1] == parts - 1:
                end(waiting[0])
        waiting = middle(*started)
        started = following
    finish(*waiting)
    end(waiting[0])

    if chunk:
        @pl.when(step == pl.num_programs(0) - 1)
        def _():
            first = lax.rem(lax.axis_index("day"), 2) == 0
            for place, grad_ref in enumerate((grad_mine_ref, grad_other_ref)):
                half = grad_ref.shape[0] // 2
                low, high = grad_ref[:half], grad_ref[half:]
                piece_refs[2 * place][...] = jnp.where(first, low, high).astype(BF16)
                piece_refs[2 * place + 1][...] = jnp.where(first, high, low).astype(BF16)


def fold_kernel(lay, tab, homes, own_a, own_b, day_a, day_b, home_a, home_b, keep, give):
    core = tab[lay.core]
    half = keep.shape[2]

    def one(block, carry):
        item = tab[lay.item_of + block]
        mine = tab[lay.owner_of + block] == core
        place = homes[lay.home_of + block]
        asked = homes[lay.asker_of + block] == core
        early = homes[lay.chunk_of + block] == 0
        in_a = item < lay.chunk_items
        item_a = jnp.minimum(item, lay.chunk_items - 1)
        item_b = jnp.maximum(item - lay.chunk_items, 0)
        own = jnp.where(in_a, own_a[item_a], own_b[item_b])
        own += jnp.where(in_a, day_a[item_a].astype(F32), day_b[item_b].astype(F32))
        home = jnp.where(early, home_a[place].astype(F32), home_b[place].astype(F32))
        total = jnp.where(mine, own, 0.0) + jnp.where(asked, home, 0.0)
        low, high = total[:, :half], total[:, half:]
        keep[block] = jnp.where(core == 0, low, high)
        give[block] = jnp.where(core == 0, high, low)
        return carry

    lax.fori_loop(0, lay.blocks, one, 0)


def add_kernel(kept, got, out):
    out[...] = (kept[...] + got[...]).astype(BF16)


def attend(lay, chunk, tab, in_blocks, up_blocks, received, prior_inputs, pack, pack_other, carried):
    width = in_blocks.shape[-1]
    offset = chunk * lay.chunk_items

    def at_item(place):
        return lambda step, tab: (offset + step * STEP_ITEMS + place, 0, 0)

    def at_block(place):
        return lambda step, tab: (tab[lay.block_of + offset + step * STEP_ITEMS + place], 0, 0)

    def at_recv(place):
        return lambda step, tab: (tab[lay.recv_of + offset + step * STEP_ITEMS + place], 0, 0)

    def at_step(step, tab):
        return (step, 0, 0)

    def fixed(step, tab):
        return (0, 0)

    full_block = (1, BLOCK, width)
    weights_block = (4 * GROUP, width)
    in_specs, operands = [], []
    for place in range(STEP_ITEMS):
        in_specs += [
            pl.BlockSpec(full_block, at_block(place)),
            pl.BlockSpec(full_block, at_block(place)),
            pl.BlockSpec(full_block, at_recv(place)),
            pl.BlockSpec(full_block, at_item(place)),
        ]
        operands += [in_blocks, up_blocks, received, prior_inputs]
    in_specs += [pl.BlockSpec(weights_block, fixed)] * 2
    operands += [pack, pack_other]
    if chunk:
        in_specs += [pl.BlockSpec(weights_block, fixed)] * 2
        operands += carried
    pieces = lay.chunk_items
    grads = [pltpu.HBM(weights_block, F32)] * 2
    if chunk:
        grads = [jax.ShapeDtypeStruct((2 * GROUP, width), BF16)] * 4
    flops = 2 * pieces * (23 * BLOCK * width * width + 24 * BLOCK * 3 * BLOCK * 512)
    return pl.pallas_call(
        lambda *refs: attention_kernel(lay, chunk, *refs),
        grid_spec=pltpu.PrefetchScalarGridSpec(
            num_scalar_prefetch=1,
            grid=(pieces // STEP_ITEMS,),
            in_specs=in_specs,
            out_specs=(
                pl.BlockSpec((STEP_ITEMS, BLOCK, width), at_step),
                pl.BlockSpec((STEP_ITEMS, BLOCK, width), at_step),
                pl.BlockSpec((lay.places, BLOCK, width), lambda step, tab: (0, 0, 0)),
                *[pl.BlockSpec(grad.shape, fixed) for grad in grads],
            ),
            scratch_shapes=[pltpu.VMEM(weights_block, F32)] * (2 if chunk else 0),
        ),
        out_shape=(
            pltpu.HBM((pieces, BLOCK, width), F32),
            pltpu.HBM((pieces, BLOCK, width), BF16),
            pltpu.HBM((lay.places, BLOCK, width), BF16),
            *grads,
        ),
        compiler_params=pltpu.CompilerParams(vmem_limit_bytes=32 << 20),
        cost_estimate=pl.CostEstimate(
            flops=flops, bytes_accessed=5 << 20, transcendentals=pieces * 8 * BLOCK * 3 * BLOCK
        ),
        name=f"attention_{chunk}",
    )(
        tab,
        *[
            value
            if value is received
            else pltpu.with_memory_space_constraint(value, pltpu.HBM)
            for value in operands
        ],
    )


def exchanged(value, axis, bit):
    count = lax.axis_size(axis)
    return lax.ppermute(value, axis, [(place, place ^ bit) for place in range(count)])


def summed_over(value, axis, bit):
    low = value.astype(BF16)
    return low.astype(F32) + exchanged(low, axis, bit).astype(F32)


def neighbours(axis, other):
    size = lax.axis_size(other)
    return [
        (place * size + at, (place ^ 1) * size + (at ^ 1))
        for place in range(lax.axis_size(axis))
        for at in range(size)
    ]


def sum_gradients(part, home_b, day_b, fold):
    bit = 2
    while bit < lax.axis_size("day"):
        part = summed_over(part, "day", bit)
        bit *= 2
    half = part.shape[0] // 2
    first = lax.rem(lax.axis_index("reach"), 2) == 0
    low = part.astype(BF16)
    kept = jnp.where(first, low[:half], low[half:])
    given = jnp.where(first, low[half:], low[:half])
    part = kept.astype(F32) + exchanged(given, "reach", 1).astype(F32)
    part, day_b = lax.optimization_barrier((part, day_b))
    bit = 2
    while bit < lax.axis_size("reach"):
        part = summed_over(part, "reach", bit)
        bit *= 2
    part, home_b = lax.optimization_barrier((part.astype(BF16), home_b))
    quarters = (
        part,
        exchanged(part, "reach", 1),
        exchanged(part, "day", 1),
        lax.ppermute(part, ("reach", "day"), neighbours("reach", "day")),
    )
    keep, give = fold(home_b, day_b)
    quarters, give = lax.optimization_barrier((quarters, give))
    return quarters, (keep, give)


def split_kernel(mine, along_reach, along_day, along_both, query_out, key_out, value_out, output_out):
    day_half = lax.rem(lax.axis_index("day"), 2) == 0
    reach_half = lax.rem(lax.axis_index("reach"), 2) == 0

    def quarter(by_day, by_reach):
        near = jnp.where(reach_half == by_reach, mine[...], along_reach[...])
        far = jnp.where(reach_half == by_reach, along_day[...], along_both[...])
        return jnp.where(day_half == by_day, near, far).astype(F32)

    for place, by_reach in enumerate((True, False)):
        rows = quarter(True, by_reach)
        key_out[place * GROUP : (place + 1) * GROUP] = rows[:, :GROUP]
        value_out[place * GROUP : (place + 1) * GROUP] = rows[:, GROUP:]
    query_out[...] = quarter(False, True).T
    output_out[...] = quarter(False, False)


def on_device(
    inputs, upstream, query_weight, key_weight, value_weight, output_weight, partner, counts
):
    days_dev, rows_dev, width = inputs.shape
    assert days_dev == 1 and width == 2 * GROUP
    blocks_dev = rows_dev // BLOCK
    reach_total = lax.axis_size("reach")
    day_total = lax.axis_size("day")
    assert lax.axis_size("head") == CORES
    lay = Layout(blocks_dev, reach_total)
    half = width // 2
    in_blocks = inputs.reshape(blocks_dev, BLOCK, width)
    up_blocks = upstream.reshape(blocks_dev, BLOCK, width)
    pack = jnp.concatenate([key_weight.T, value_weight.T, query_weight.T, output_weight], axis=0)
    pack_other = exchanged(pack, "head", 1)

    smem = pl.BlockSpec(memory_space=pltpu.SMEM)
    in_vmem = pl.BlockSpec(memory_space=pltpu.VMEM)
    anywhere = pl.BlockSpec(memory_space=pl.ANY)
    sent_shape = jax.ShapeDtypeStruct((lay.places, BLOCK, width), BF16)
    sent_a, homes = pl.pallas_call(
        lambda *refs: pick_kernel(lay, *refs),
        out_shape=(sent_shape, jax.ShapeDtypeStruct((lay.homes_size,), jnp.int32)),
        in_specs=[anywhere, anywhere],
        out_specs=(in_vmem, smem),
        scratch_shapes=[
            pltpu.SMEM(partner.shape, jnp.int32),
            pltpu.VMEM((blocks_dev, BLOCK, width), BF16),
            pltpu.SemaphoreType.DMA((2,)),
        ],
        compiler_params=pltpu.CompilerParams(vmem_limit_bytes=16 << 20),
        name="pick",
    )(
        pltpu.with_memory_space_constraint(partner, pltpu.HBM),
        pltpu.with_memory_space_constraint(in_blocks, pltpu.HBM),
    )
    sent_b, prior, tab = pl.pallas_call(
        lambda *refs: deal_kernel(lay, *refs),
        out_shape=(
            sent_shape,
            jax.ShapeDtypeStruct((lay.items, BLOCK, width), BF16),
            jax.ShapeDtypeStruct((lay.size,), jnp.int32),
        ),
        in_specs=[smem, smem, smem, in_vmem],
        out_specs=(in_vmem, in_vmem, smem),
        scratch_shapes=[
            pltpu.SMEM((lay.reach,), jnp.int32),
            pltpu.SMEM((lay.reach,), jnp.int32),
        ],
        compiler_params=pltpu.CompilerParams(vmem_limit_bytes=16 << 20),
        name="deal",
    )(partner, counts, homes, in_blocks)

    def ring(value):
        shape = value.shape
        value = value.reshape(lay.reach, lay.slots * BLOCK, width)
        return lax.all_to_all(value, "reach", 0, 0, tiled=True).reshape(shape)

    next_day = [(d, d + 1) for d in range(day_total - 1)]
    last_day = [(d + 1, d) for d in range(day_total - 1)]
    received_a = ring(sent_a)
    prior_inputs = lax.ppermute(prior, "day", next_day)
    received_b = ring(sent_b)
    shared = (prior_inputs, pack, pack_other)
    own_a, day_a, home_a, *grads = attend(
        lay, 0, tab, in_blocks, up_blocks, received_a, *shared, None
    )
    home_a = ring(home_a)
    day_a = lax.ppermute(day_a, "day", last_day)
    own_b, day_b, home_b, kept, to_day, to_core, to_both = attend(
        lay, 1, tab, in_blocks, up_blocks, received_b, *shared, grads
    )
    pieces = (
        exchanged(to_day, "day", 1),
        exchanged(to_core, "head", 1),
        lax.ppermute(to_both, ("day", "head"), neighbours("day", "head")),
    )
    home_a, day_a, home_b, kept = lax.optimization_barrier((home_a, day_a, home_b, kept))
    pieces = (kept, *pieces)
    home_b = ring(home_b)
    day_b = lax.ppermute(day_b, "day", last_day)
    half_shape = jax.ShapeDtypeStruct((blocks_dev, BLOCK, half), F32)

    def fold(home_b, day_b):
        return pl.pallas_call(
            lambda *refs: fold_kernel(lay, *refs),
            out_shape=(half_shape, half_shape),
            in_specs=[smem] * 2 + [in_vmem] * 6,
            out_specs=[in_vmem] * 2,
            compiler_params=pltpu.CompilerParams(vmem_limit_bytes=16 << 20),
            name="fold",
        )(tab, homes, own_a, own_b, day_a, day_b, home_a, home_b)

    quarters, (keep, give) = sum_gradients(
        sum(piece.astype(F32) for piece in pieces), home_b, day_b, fold
    )
    got = exchanged(give, "head", 1)
    back_blocks = pl.pallas_call(
        add_kernel,
        out_shape=jax.ShapeDtypeStruct((blocks_dev, BLOCK, half), BF16),
        in_specs=[in_vmem] * 2,
        out_specs=in_vmem,
        compiler_params=pltpu.CompilerParams(vmem_limit_bytes=16 << 20),
        name="add",
    )(keep, got)
    weight_grads = pl.pallas_call(
        split_kernel,
        out_shape=(
            jax.ShapeDtypeStruct((width, half), F32),
            jax.ShapeDtypeStruct((width, half), F32),
            jax.ShapeDtypeStruct((width, half), F32),
            jax.ShapeDtypeStruct((half, width), F32),
        ),
        grid=(1,),
        compiler_params=pltpu.CompilerParams(vmem_limit_bytes=16 << 20),
        name="split",
    )(*quarters)

    return (back_blocks.reshape(1, rows_dev, half), *weight_grads)


def solution(mesh):
    placed = (
        P(("groups", "day"), "reach", None),
        P(("groups", "day"), "reach", None),
        P(None, "head"),
        P(None, "head"),
        P(None, "head"),
        P("head", None),
        P("groups"),
        P("groups"),
    )
    return jax.shard_map(
        on_device,
        mesh=mesh,
        in_specs=placed,
        out_specs=(
            P(("groups", "day"), "reach", "head"),
            P("groups", "head"),
            P("groups", "head"),
            P("groups", "head"),
            P(("groups", "head"), None),
        ),
        check_vma=False,
    )
```

```python
import jax
import jax.numpy as jnp
from jax import lax
from jax.experimental import pallas as pl
from jax.experimental.pallas import tpu as pltpu
from jax.sharding import PartitionSpec as P

HD = 32
BLOCK = 128
GROUP = 128
CORES = 2
CHUNKS = 2
WORKERS = CORES * CHUNKS
F32 = jnp.float32
BF16 = jnp.bfloat16
PACK = 4
STEP_ITEMS = 4
LOG2E = 1.4426950408889634


class Layout:
    def __init__(self, blocks_dev, reach_total):
        self.blocks = blocks_dev
        self.items = blocks_dev // CORES
        self.chunk_items = self.items // CHUNKS
        self.reach = reach_total
        self.slots = max(1, 2 * blocks_dev // reach_total // WORKERS)
        self.places = reach_total * self.slots
        self.block_of = 0
        self.recv_of = self.items
        self.count_own = 2 * self.items
        self.count_partner = 3 * self.items
        self.owner_of = 4 * self.items
        self.item_of = self.owner_of + blocks_dev
        self.core = self.item_of + blocks_dev
        self.later_day = self.core + 1
        self.size = -(-(self.core + 2) // 128) * 128
        self.spare = blocks_dev
        self.home_of = 0
        self.chunk_of = blocks_dev + 1
        self.asker_of = 2 * (blocks_dev + 1)
        self.picks = 3 * (blocks_dev + 1)
        self.spare_pick = self.picks + CHUNKS * self.places
        self.homes_size = -(-(self.spare_pick + 1) // 128) * 128


def quotient(value, count):
    if count & (count - 1) == 0:
        return lax.shift_right_logical(value, jnp.int32(count.bit_length() - 1))
    return lax.div(value, count)


def remainder(value, count):
    if count & (count - 1) == 0:
        return lax.bitwise_and(value, jnp.int32(count - 1))
    return lax.rem(value, count)


def pick_kernel(lay, partner_hbm, inputs, sent, homes, partner, held, sems):
    bd, slots = lay.blocks, lay.slots
    reach_pos, core = lax.axis_index("reach"), lax.axis_index("head")
    table_copy = pltpu.make_async_copy(partner_hbm, partner, sems.at[0])
    table_copy.start()
    copy = pltpu.make_async_copy(inputs, held, sems.at[1])
    copy.start()
    for place in range(CHUNKS * lay.places):
        homes[lay.picks + place] = 0
    table_copy.wait()

    def one_reach(peer, carry):
        base = jnp.int32(0)
        wanted = []
        for index in range(bd):
            block = partner[peer * bd + index]
            source = quotient(block, bd)
            base = base + jnp.where(source < reach_pos, 1, 0)
            wanted.append((source == reach_pos, remainder(block, bd)))
        rank = jnp.int32(0)
        for hit, local in wanted:
            place = base + rank
            owner = remainder(place, CORES)
            chunk = remainder(quotient(place, CORES), CHUNKS)
            slot = peer * slots + jnp.minimum(quotient(rank, WORKERS), slots - 1)
            target = jnp.where(hit, local, lay.spare)
            homes[lay.home_of + target] = slot
            homes[lay.chunk_of + target] = chunk
            homes[lay.asker_of + target] = owner
            pick = lay.picks + chunk * lay.places + slot
            homes[jnp.where(hit & (owner == core), pick, lay.spare_pick)] = local
            rank = rank + jnp.where(hit, 1, 0)
        return carry

    lax.fori_loop(0, lay.reach, one_reach, 0)
    copy.wait()
    for place in range(lay.places):
        sent[place] = held[homes[lay.picks + place]]


def deal_kernel(lay, partner, counts, homes, inputs, sent, prior, tab, start, used):
    bd, slots = lay.blocks, lay.slots
    reach_pos, core = lax.axis_index("reach"), lax.axis_index("head")

    def clear(index, carry):
        used[index] = 0
        start[index] = 0
        return carry

    lax.fori_loop(0, lay.reach, clear, 0, unroll=True)

    def count(index, carry):
        source = quotient(partner[reach_pos * bd + index], bd)
        start[source] = start[source] + 1
        return carry

    lax.fori_loop(0, bd, count, 0)

    def prefix(index, total):
        here = start[index]
        start[index] = total
        return total + here

    lax.fori_loop(0, lay.reach, prefix, jnp.int32(0))

    def assign(index, carry):
        wanted = partner[reach_pos * bd + index]
        source = quotient(wanted, bd)
        rank = used[source]
        used[source] = rank + 1
        place = start[source] + rank
        owner = remainder(place, CORES)
        chunk = remainder(quotient(place, CORES), CHUNKS)
        item = chunk * lay.chunk_items + quotient(place, WORKERS)
        slot = jnp.minimum(quotient(rank, WORKERS), slots - 1)
        tab[lay.owner_of + index] = owner
        tab[lay.item_of + index] = item

        @pl.when(owner == core)
        def _():
            tab[lay.block_of + item] = index
            tab[lay.recv_of + item] = source * slots + slot
            tab[lay.count_own + item] = counts[reach_pos * bd + index]
            tab[lay.count_partner + item] = counts[wanted]

        return carry

    lax.fori_loop(0, bd, assign, 0)
    tab[lay.core] = core
    tab[lay.later_day] = jnp.where(lax.axis_index("day") > 0, 1, 0)

    def pick(place, carry):
        sent[place] = inputs[homes[lay.picks + lay.places + place]]
        return carry

    def pick_prior(item, carry):
        prior[item] = inputs[tab[lay.block_of + item]]
        return carry

    lax.fori_loop(0, lay.places, pick, 0)
    lax.fori_loop(0, lay.items, pick_prior, 0)


def dot(left, right):
    return lax.dot_general(left, right, (((1,), (0,)), ((), ())), preferred_element_type=F32)


def dot_t(left, right):
    return lax.dot_general(left, right, (((1,), (1,)), ((), ())), preferred_element_type=F32)


def attention_kernel(lay, chunk, tab, *refs):
    step = pl.program_id(0)
    read, refs = refs[: 4 * STEP_ITEMS], refs[4 * STEP_ITEMS :]
    mine_ref, other_ref, *refs = refs
    if chunk:
        start_mine_ref, start_other_ref, *refs = refs
        own_out_ref, day_ref, home_ref, *piece_refs, grad_mine_ref, grad_other_ref = refs
    else:
        own_out_ref, day_ref, home_ref, grad_mine_ref, grad_other_ref = refs
    factor = HD ** (-0.5)
    per_group = GROUP // HD // PACK

    @pl.when(step == 0)
    def _():
        if chunk:
            grad_mine_ref[...] = start_mine_ref[...]
            grad_other_ref[...] = start_other_ref[...]
        else:
            grad_mine_ref[...] = jnp.zeros_like(grad_mine_ref)
            grad_other_ref[...] = jnp.zeros_like(grad_other_ref)

    rows = lax.broadcasted_iota(jnp.int32, (BLOCK, PACK * BLOCK), 0)
    lane_head = lax.broadcasted_iota(jnp.int32, (BLOCK, GROUP), 1) // HD
    query_t = jnp.concatenate([mine_ref[256:384, :], other_ref[256:384, :]], axis=0)
    output_w = jnp.concatenate([mine_ref[384:512, :], other_ref[384:512, :]], axis=0)

    class Item:
        pass

    def begin(place):
        it = Item()
        own_ref, up_ref, partner_ref, prior_ref = read[4 * place : 4 * place + 4]
        it.place = place
        item = step * STEP_ITEMS + place + chunk * lay.chunk_items
        it.item = item
        it.own, it.up = own_ref[0], up_ref[0]
        it.inputs = jnp.concatenate([it.own, partner_ref[0], prior_ref[0]], axis=0)
        queries = dot_t(it.own, query_t)
        back_out = dot_t(it.up, output_w)
        count_own = tab[lay.count_own + item]
        it.counts = (count_own, tab[lay.count_partner + item], count_own * tab[lay.later_day])
        it.groups = []
        for group, weights_ref in enumerate((mine_ref, other_ref)):
            kv_t = weights_ref[0:256, :]
            kv = dot_t(it.inputs, kv_t).astype(BF16)
            lanes = slice(group * GROUP, (group + 1) * GROUP)
            it.groups.append((kv_t, kv, kv.T, queries[:, lanes], back_out[:, lanes]))
        it.outputs_t, it.back_query_t = [], []
        it.keys, it.values = ([], []), ([], [])
        return it

    def start(it, part):
        _, kv, _, group_queries, group_back = it.groups[part // per_group]
        heads = [part % per_group * PACK + h for h in range(PACK)]
        query_pack, back_pack = (
            jnp.concatenate(
                [jnp.where(lane_head == h, rows_of, 0.0) for h in heads], axis=0
            ).astype(BF16)
            for rows_of in (group_queries, group_back)
        )
        logits = dot_t(kv[:, :GROUP], query_pack)
        return it, part, query_pack, back_pack, logits, dot_t(kv[:, GROUP:], back_pack)

    def middle(it, part, query_pack, back_pack, logits, back_weights):
        logits = jnp.concatenate(
            [
                jnp.where(rows < count, logits[index * BLOCK : (index + 1) * BLOCK], -1e30)
                for index, count in enumerate(it.counts)
            ],
            axis=0,
        )
        highest = jnp.max(logits, axis=0, keepdims=True)
        raised = jnp.exp2((logits - highest) * (factor * LOG2E))
        scale = 1.0 / jnp.sum(raised, axis=0, keepdims=True)
        weights = raised * scale
        center = jnp.sum(weights * back_weights, axis=0, keepdims=True)
        back_logits = (weights * ((back_weights - center) * factor)).astype(BF16)
        return it, part, query_pack, back_pack, weights.astype(BF16), back_logits

    def finish(it, part, query_pack, back_pack, weights_low, back_logits):
        group = part // per_group
        kv_cols = it.groups[group][2]
        it.values[group].append(dot(weights_low, back_pack))
        it.keys[group].append(dot(back_logits, query_pack))
        size = PACK * HD
        first = part % per_group * size
        out_t = dot(kv_cols[GROUP + first : GROUP + first + size, :], weights_low)
        query_grad_t = dot(kv_cols[first : first + size, :], back_logits)
        for h in range(PACK):
            lanes = slice(h * BLOCK, (h + 1) * BLOCK)
            it.outputs_t.append(out_t[h * HD : (h + 1) * HD, lanes])
            it.back_query_t.append(query_grad_t[h * HD : (h + 1) * HD, lanes])

    def end(it):
        inputs_t = it.inputs.T
        back_inputs = None
        for group, grad_ref in enumerate((grad_mine_ref, grad_other_ref)):
            kv_t = it.groups[group][0]
            keys, values = it.keys[group], it.values[group]
            back_kv = jnp.concatenate(
                [sum(keys[1:], keys[0]), sum(values[1:], values[0])], axis=1
            ).astype(BF16)
            term = dot(back_kv, kv_t)
            back_inputs = term if back_inputs is None else back_inputs + term
            grad_ref[0:256, :] += dot(inputs_t, back_kv)
        outputs_t = jnp.concatenate(it.outputs_t, axis=0).astype(BF16)
        back_query_t = jnp.concatenate(it.back_query_t, axis=0).astype(BF16)
        query_grad = dot(back_query_t, it.own)
        output_grad = dot(outputs_t, it.up)
        grad_mine_ref[256:384, :] += query_grad[:GROUP]
        grad_other_ref[256:384, :] += query_grad[GROUP:]
        grad_mine_ref[384:512, :] += output_grad[:GROUP]
        grad_other_ref[384:512, :] += output_grad[GROUP:]
        own_out_ref[it.place] = back_inputs[:BLOCK] + dot(back_query_t.T, query_t)
        home_ref[tab[lay.recv_of + it.item]] = back_inputs[BLOCK : 2 * BLOCK].astype(BF16)
        day_ref[it.place] = back_inputs[2 * BLOCK :].astype(BF16)

    parts = 2 * per_group
    items = [begin(0)]
    started = start(items[0], 0)
    waiting = None
    ended = 0
    for index in range(STEP_ITEMS * parts):
        following = None
        if index + 1 < STEP_ITEMS * parts:
            place, part = divmod(index + 1, parts)
            if part == 0:
                items.append(begin(place))
            following = start(items[place], part)
        if waiting is not None:
            finish(*waiting)
            if waiting[1] == parts - 1:
                end(waiting[0])
        waiting = middle(*started)
        started = following
    finish(*waiting)
    end(waiting[0])

    if chunk:
        @pl.when(step == pl.num_programs(0) - 1)
        def _():
            first = lax.rem(lax.axis_index("day"), 2) == 0
            for place, grad_ref in enumerate((grad_mine_ref, grad_other_ref)):
                half = grad_ref.shape[0] // 2
                low, high = grad_ref[:half], grad_ref[half:]
                piece_refs[2 * place][...] = jnp.where(first, low, high).astype(BF16)
                piece_refs[2 * place + 1][...] = jnp.where(first, high, low).astype(BF16)


def fold_kernel(lay, tab, homes, own_a, own_b, day_a, day_b, home_a, home_b, keep, give):
    core = tab[lay.core]
    half = keep.shape[2]

    def one(block, carry):
        item = tab[lay.item_of + block]
        mine = tab[lay.owner_of + block] == core
        place = homes[lay.home_of + block]
        asked = homes[lay.asker_of + block] == core
        early = homes[lay.chunk_of + block] == 0
        in_a = item < lay.chunk_items
        item_a = jnp.minimum(item, lay.chunk_items - 1)
        item_b = jnp.maximum(item - lay.chunk_items, 0)
        own = jnp.where(in_a, own_a[item_a], own_b[item_b])
        own += jnp.where(in_a, day_a[item_a].astype(F32), day_b[item_b].astype(F32))
        home = jnp.where(early, home_a[place].astype(F32), home_b[place].astype(F32))
        total = jnp.where(mine, own, 0.0) + jnp.where(asked, home, 0.0)
        low, high = total[:, :half], total[:, half:]
        keep[block] = jnp.where(core == 0, low, high)
        give[block] = jnp.where(core == 0, high, low)
        return carry

    lax.fori_loop(0, lay.blocks, one, 0)


def add_kernel(kept, got, out):
    out[...] = (kept[...] + got[...]).astype(BF16)


def attend(lay, chunk, tab, in_blocks, up_blocks, received, prior_inputs, pack, pack_other, carried):
    width = in_blocks.shape[-1]
    offset = chunk * lay.chunk_items

    def at_item(place):
        return lambda step, tab: (offset + step * STEP_ITEMS + place, 0, 0)

    def at_block(place):
        return lambda step, tab: (tab[lay.block_of + offset + step * STEP_ITEMS + place], 0, 0)

    def at_recv(place):
        return lambda step, tab: (tab[lay.recv_of + offset + step * STEP_ITEMS + place], 0, 0)

    def at_step(step, tab):
        return (step, 0, 0)

    def fixed(step, tab):
        return (0, 0)

    full_block = (1, BLOCK, width)
    weights_block = (4 * GROUP, width)
    in_specs, operands = [], []
    for place in range(STEP_ITEMS):
        in_specs += [
            pl.BlockSpec(full_block, at_block(place)),
            pl.BlockSpec(full_block, at_block(place)),
            pl.BlockSpec(full_block, at_recv(place)),
            pl.BlockSpec(full_block, at_item(place)),
        ]
        operands += [in_blocks, up_blocks, received, prior_inputs]
    in_specs += [pl.BlockSpec(weights_block, fixed)] * 2
    operands += [pack, pack_other]
    if chunk:
        in_specs += [pl.BlockSpec(weights_block, fixed)] * 2
        operands += carried
    pieces = lay.chunk_items
    grads = [pltpu.HBM(weights_block, F32)] * 2
    if chunk:
        grads = [jax.ShapeDtypeStruct((2 * GROUP, width), BF16)] * 4
    flops = 2 * pieces * (23 * BLOCK * width * width + 24 * BLOCK * 3 * BLOCK * 512)
    return pl.pallas_call(
        lambda *refs: attention_kernel(lay, chunk, *refs),
        grid_spec=pltpu.PrefetchScalarGridSpec(
            num_scalar_prefetch=1,
            grid=(pieces // STEP_ITEMS,),
            in_specs=in_specs,
            out_specs=(
                pl.BlockSpec((STEP_ITEMS, BLOCK, width), at_step),
                pl.BlockSpec((STEP_ITEMS, BLOCK, width), at_step),
                pl.BlockSpec((lay.places, BLOCK, width), lambda step, tab: (0, 0, 0)),
                *[pl.BlockSpec(grad.shape, fixed) for grad in grads],
            ),
            scratch_shapes=[pltpu.VMEM(weights_block, F32)] * (2 if chunk else 0),
        ),
        out_shape=(
            pltpu.HBM((pieces, BLOCK, width), F32),
            pltpu.HBM((pieces, BLOCK, width), BF16),
            pltpu.HBM((lay.places, BLOCK, width), BF16),
            *grads,
        ),
        compiler_params=pltpu.CompilerParams(vmem_limit_bytes=32 << 20),
        cost_estimate=pl.CostEstimate(
            flops=flops, bytes_accessed=5 << 20, transcendentals=pieces * 8 * BLOCK * 3 * BLOCK
        ),
        name=f"attention_{chunk}",
    )(
        tab,
        *[
            value
            if value is received
            else pltpu.with_memory_space_constraint(value, pltpu.HBM)
            for value in operands
        ],
    )


def exchanged(value, axis, bit):
    count = lax.axis_size(axis)
    return lax.ppermute(value, axis, [(place, place ^ bit) for place in range(count)])


def summed_over(value, axis, bit):
    low = value.astype(BF16)
    return low.astype(F32) + exchanged(low, axis, bit).astype(F32)


def neighbours(axis, other):
    size = lax.axis_size(other)
    return [
        (place * size + at, (place ^ 1) * size + (at ^ 1))
        for place in range(lax.axis_size(axis))
        for at in range(size)
    ]


def sum_gradients(part, home_b, fold):
    bit = 2
    while bit < lax.axis_size("day"):
        part = summed_over(part, "day", bit)
        bit *= 2
    half = part.shape[0] // 2
    first = lax.rem(lax.axis_index("reach"), 2) == 0
    low = part.astype(BF16)
    kept = jnp.where(first, low[:half], low[half:])
    given = jnp.where(first, low[half:], low[:half])
    part = kept.astype(F32) + exchanged(given, "reach", 1).astype(F32)
    part, home_b = lax.optimization_barrier((part, home_b))
    bit = 2
    while bit < lax.axis_size("reach"):
        part = summed_over(part, "reach", bit)
        bit *= 2
    part, folded = lax.optimization_barrier((part.astype(BF16), fold(home_b)))
    quarters = (
        part,
        exchanged(part, "reach", 1),
        exchanged(part, "day", 1),
        lax.ppermute(part, ("reach", "day"), neighbours("reach", "day")),
    )
    return quarters, folded


def split_kernel(mine, along_reach, along_day, along_both, query_out, key_out, value_out, output_out):
    day_half = lax.rem(lax.axis_index("day"), 2) == 0
    reach_half = lax.rem(lax.axis_index("reach"), 2) == 0

    def quarter(by_day, by_reach):
        near = jnp.where(reach_half == by_reach, mine[...], along_reach[...])
        far = jnp.where(reach_half == by_reach, along_day[...], along_both[...])
        return jnp.where(day_half == by_day, near, far).astype(F32)

    for place, by_reach in enumerate((True, False)):
        rows = quarter(True, by_reach)
        key_out[place * GROUP : (place + 1) * GROUP] = rows[:, :GROUP]
        value_out[place * GROUP : (place + 1) * GROUP] = rows[:, GROUP:]
    query_out[...] = quarter(False, True).T
    output_out[...] = quarter(False, False)


def on_device(
    inputs, upstream, query_weight, key_weight, value_weight, output_weight, partner, counts
):
    days_dev, rows_dev, width = inputs.shape
    assert days_dev == 1 and width == 2 * GROUP
    blocks_dev = rows_dev // BLOCK
    reach_total = lax.axis_size("reach")
    day_total = lax.axis_size("day")
    assert lax.axis_size("head") == CORES
    lay = Layout(blocks_dev, reach_total)
    half = width // 2
    in_blocks = inputs.reshape(blocks_dev, BLOCK, width)
    up_blocks = upstream.reshape(blocks_dev, BLOCK, width)
    pack = jnp.concatenate([key_weight.T, value_weight.T, query_weight.T, output_weight], axis=0)
    pack_other = exchanged(pack, "head", 1)

    smem = pl.BlockSpec(memory_space=pltpu.SMEM)
    in_vmem = pl.BlockSpec(memory_space=pltpu.VMEM)
    anywhere = pl.BlockSpec(memory_space=pl.ANY)
    sent_shape = jax.ShapeDtypeStruct((lay.places, BLOCK, width), BF16)
    sent_a, homes = pl.pallas_call(
        lambda *refs: pick_kernel(lay, *refs),
        out_shape=(sent_shape, jax.ShapeDtypeStruct((lay.homes_size,), jnp.int32)),
        in_specs=[anywhere, anywhere],
        out_specs=(in_vmem, smem),
        scratch_shapes=[
            pltpu.SMEM(partner.shape, jnp.int32),
            pltpu.VMEM((blocks_dev, BLOCK, width), BF16),
            pltpu.SemaphoreType.DMA((2,)),
        ],
        compiler_params=pltpu.CompilerParams(vmem_limit_bytes=16 << 20),
        name="pick",
    )(
        pltpu.with_memory_space_constraint(partner, pltpu.HBM),
        pltpu.with_memory_space_constraint(in_blocks, pltpu.HBM),
    )
    sent_b, prior, tab = pl.pallas_call(
        lambda *refs: deal_kernel(lay, *refs),
        out_shape=(
            sent_shape,
            jax.ShapeDtypeStruct((lay.items, BLOCK, width), BF16),
            jax.ShapeDtypeStruct((lay.size,), jnp.int32),
        ),
        in_specs=[smem, smem, smem, in_vmem],
        out_specs=(in_vmem, in_vmem, smem),
        scratch_shapes=[
            pltpu.SMEM((lay.reach,), jnp.int32),
            pltpu.SMEM((lay.reach,), jnp.int32),
        ],
        compiler_params=pltpu.CompilerParams(vmem_limit_bytes=16 << 20),
        name="deal",
    )(partner, counts, homes, in_blocks)

    def ring(value):
        shape = value.shape
        value = value.reshape(lay.reach, lay.slots * BLOCK, width)
        return lax.all_to_all(value, "reach", 0, 0, tiled=True).reshape(shape)

    next_day = [(d, d + 1) for d in range(day_total - 1)]
    last_day = [(d + 1, d) for d in range(day_total - 1)]
    received_a = ring(sent_a)
    prior_inputs = lax.ppermute(prior, "day", next_day)
    received_b = ring(sent_b)
    shared = (prior_inputs, pack, pack_other)
    own_a, day_a, home_a, *grads = attend(
        lay, 0, tab, in_blocks, up_blocks, received_a, *shared, None
    )
    home_a = ring(home_a)
    day_a = lax.ppermute(day_a, "day", last_day)
    own_b, day_b, home_b, kept, to_day, to_core, to_both = attend(
        lay, 1, tab, in_blocks, up_blocks, received_b, *shared, grads
    )
    pieces = (
        exchanged(to_day, "day", 1),
        exchanged(to_core, "head", 1),
        lax.ppermute(to_both, ("day", "head"), neighbours("day", "head")),
    )
    home_a, home_b, kept = lax.optimization_barrier((home_a, home_b, kept))
    pieces = (kept, *pieces)
    home_b = ring(home_b)
    day_b = lax.ppermute(day_b, "day", last_day)
    half_shape = jax.ShapeDtypeStruct((blocks_dev, BLOCK, half), F32)

    def fold(home_b):
        return pl.pallas_call(
            lambda *refs: fold_kernel(lay, *refs),
            out_shape=(half_shape, half_shape),
            in_specs=[smem] * 2 + [in_vmem] * 6,
            out_specs=[in_vmem] * 2,
            compiler_params=pltpu.CompilerParams(vmem_limit_bytes=16 << 20),
            name="fold",
        )(tab, homes, own_a, own_b, day_a, day_b, home_a, home_b)

    quarters, (keep, give) = sum_gradients(
        sum(piece.astype(F32) for piece in pieces), home_b, fold
    )
    got = exchanged(give, "head", 1)
    back_blocks = pl.pallas_call(
        add_kernel,
        out_shape=jax.ShapeDtypeStruct((blocks_dev, BLOCK, half), BF16),
        in_specs=[in_vmem] * 2,
        out_specs=in_vmem,
        compiler_params=pltpu.CompilerParams(vmem_limit_bytes=16 << 20),
        name="add",
    )(keep, got)
    back_blocks, quarters = lax.optimization_barrier((back_blocks, quarters))
    weight_grads = pl.pallas_call(
        split_kernel,
        out_shape=(
            jax.ShapeDtypeStruct((width, half), F32),
            jax.ShapeDtypeStruct((width, half), F32),
            jax.ShapeDtypeStruct((width, half), F32),
            jax.ShapeDtypeStruct((half, width), F32),
        ),
        grid=(1,),
        compiler_params=pltpu.CompilerParams(vmem_limit_bytes=16 << 20),
        name="split",
    )(*quarters)

    return (back_blocks.reshape(1, rows_dev, half), *weight_grads)


def solution(mesh):
    placed = (
        P(("groups", "day"), "reach", None),
        P(("groups", "day"), "reach", None),
        P(None, "head"),
        P(None, "head"),
        P(None, "head"),
        P("head", None),
        P("groups"),
        P("groups"),
    )
    return jax.shard_map(
        on_device,
        mesh=mesh,
        in_specs=placed,
        out_specs=(
            P(("groups", "day"), "reach", "head"),
            P("groups", "head"),
            P("groups", "head"),
            P("groups", "head"),
            P(("groups", "head"), None),
        ),
        check_vma=False,
    )
```

```python
import jax
import jax.numpy as jnp
from jax import lax
from jax.experimental import pallas as pl
from jax.experimental.pallas import tpu as pltpu
from jax.sharding import PartitionSpec as P

HD = 32
BLOCK = 128
GROUP = 128
CORES = 2
CHUNKS = 2
WORKERS = CORES * CHUNKS
F32 = jnp.float32
BF16 = jnp.bfloat16
PACK = 4
STEP_ITEMS = 4
LOG2E = 1.4426950408889634


class Layout:
    def __init__(self, blocks_dev, reach_total):
        self.blocks = blocks_dev
        self.items = blocks_dev // CORES
        self.chunk_items = self.items // CHUNKS
        self.reach = reach_total
        self.slots = max(1, 2 * blocks_dev // reach_total // WORKERS)
        self.places = reach_total * self.slots
        self.block_of = 0
        self.recv_of = self.items
        self.count_own = 2 * self.items
        self.count_partner = 3 * self.items
        self.owner_of = 4 * self.items
        self.item_of = self.owner_of + blocks_dev
        self.core = self.item_of + blocks_dev
        self.later_day = self.core + 1
        self.size = -(-(self.core + 2) // 128) * 128
        self.spare = blocks_dev
        self.home_of = 0
        self.chunk_of = blocks_dev + 1
        self.asker_of = 2 * (blocks_dev + 1)
        self.picks = 3 * (blocks_dev + 1)
        self.spare_pick = self.picks + CHUNKS * self.places
        self.homes_size = -(-(self.spare_pick + 1) // 128) * 128


def quotient(value, count):
    if count & (count - 1) == 0:
        return lax.shift_right_logical(value, jnp.int32(count.bit_length() - 1))
    return lax.div(value, count)


def remainder(value, count):
    if count & (count - 1) == 0:
        return lax.bitwise_and(value, jnp.int32(count - 1))
    return lax.rem(value, count)


def pick_kernel(lay, partner_hbm, inputs, sent, homes, partner, held, sems):
    bd, slots = lay.blocks, lay.slots
    reach_pos, core = lax.axis_index("reach"), lax.axis_index("head")
    table_copy = pltpu.make_async_copy(partner_hbm, partner, sems.at[0])
    table_copy.start()
    copy = pltpu.make_async_copy(inputs, held, sems.at[1])
    copy.start()
    for place in range(CHUNKS * lay.places):
        homes[lay.picks + place] = 0
    table_copy.wait()

    def one_reach(peer, carry):
        base = jnp.int32(0)
        wanted = []
        for index in range(bd):
            block = partner[peer * bd + index]
            source = quotient(block, bd)
            base = base + jnp.where(source < reach_pos, 1, 0)
            wanted.append((source == reach_pos, remainder(block, bd)))
        rank = jnp.int32(0)
        for hit, local in wanted:
            place = base + rank
            owner = remainder(place, CORES)
            chunk = remainder(quotient(place, CORES), CHUNKS)
            slot = peer * slots + jnp.minimum(quotient(rank, WORKERS), slots - 1)
            target = jnp.where(hit, local, lay.spare)
            homes[lay.home_of + target] = slot
            homes[lay.chunk_of + target] = chunk
            homes[lay.asker_of + target] = owner
            pick = lay.picks + chunk * lay.places + slot
            homes[jnp.where(hit & (owner == core), pick, lay.spare_pick)] = local
            rank = rank + jnp.where(hit, 1, 0)
        return carry

    lax.fori_loop(0, lay.reach, one_reach, 0)
    copy.wait()
    for place in range(lay.places):
        sent[place] = held[homes[lay.picks + place]]


def deal_kernel(lay, partner, counts, homes, inputs, sent, prior, tab, start, used):
    bd, slots = lay.blocks, lay.slots
    reach_pos, core = lax.axis_index("reach"), lax.axis_index("head")

    def clear(index, carry):
        used[index] = 0
        start[index] = 0
        return carry

    lax.fori_loop(0, lay.reach, clear, 0, unroll=True)

    def count(index, carry):
        source = quotient(partner[reach_pos * bd + index], bd)
        start[source] = start[source] + 1
        return carry

    lax.fori_loop(0, bd, count, 0)

    def prefix(index, total):
        here = start[index]
        start[index] = total
        return total + here

    lax.fori_loop(0, lay.reach, prefix, jnp.int32(0))

    def assign(index, carry):
        wanted = partner[reach_pos * bd + index]
        source = quotient(wanted, bd)
        rank = used[source]
        used[source] = rank + 1
        place = start[source] + rank
        owner = remainder(place, CORES)
        chunk = remainder(quotient(place, CORES), CHUNKS)
        item = chunk * lay.chunk_items + quotient(place, WORKERS)
        slot = jnp.minimum(quotient(rank, WORKERS), slots - 1)
        tab[lay.owner_of + index] = owner
        tab[lay.item_of + index] = item

        @pl.when(owner == core)
        def _():
            tab[lay.block_of + item] = index
            tab[lay.recv_of + item] = source * slots + slot
            tab[lay.count_own + item] = counts[reach_pos * bd + index]
            tab[lay.count_partner + item] = counts[wanted]

        return carry

    lax.fori_loop(0, bd, assign, 0)
    tab[lay.core] = core
    tab[lay.later_day] = jnp.where(lax.axis_index("day") > 0, 1, 0)

    def pick(place, carry):
        sent[place] = inputs[homes[lay.picks + lay.places + place]]
        return carry

    def pick_prior(item, carry):
        prior[item] = inputs[tab[lay.block_of + item]]
        return carry

    lax.fori_loop(0, lay.places, pick, 0)
    lax.fori_loop(0, lay.items, pick_prior, 0)


def dot(left, right):
    return lax.dot_general(left, right, (((1,), (0,)), ((), ())), preferred_element_type=F32)


def dot_t(left, right):
    return lax.dot_general(left, right, (((1,), (1,)), ((), ())), preferred_element_type=F32)


def attention_kernel(lay, chunk, tab, *refs):
    step = pl.program_id(0)
    read, refs = refs[: 4 * STEP_ITEMS], refs[4 * STEP_ITEMS :]
    mine_ref, other_ref, *refs = refs
    if chunk:
        start_mine_ref, start_other_ref, *refs = refs
        own_out_ref, day_ref, home_ref, *piece_refs, grad_mine_ref, grad_other_ref = refs
    else:
        own_out_ref, day_ref, home_ref, grad_mine_ref, grad_other_ref = refs
    factor = HD ** (-0.5)
    per_group = GROUP // HD // PACK

    @pl.when(step == 0)
    def _():
        if chunk:
            grad_mine_ref[...] = start_mine_ref[...]
            grad_other_ref[...] = start_other_ref[...]
        else:
            grad_mine_ref[...] = jnp.zeros_like(grad_mine_ref)
            grad_other_ref[...] = jnp.zeros_like(grad_other_ref)

    rows = lax.broadcasted_iota(jnp.int32, (BLOCK, PACK * BLOCK), 0)
    lane_head = lax.broadcasted_iota(jnp.int32, (BLOCK, GROUP), 1) // HD
    query_t = jnp.concatenate([mine_ref[256:384, :], other_ref[256:384, :]], axis=0)
    output_w = jnp.concatenate([mine_ref[384:512, :], other_ref[384:512, :]], axis=0)

    class Item:
        pass

    def begin(place):
        it = Item()
        own_ref, up_ref, partner_ref, prior_ref = read[4 * place : 4 * place + 4]
        it.place = place
        item = step * STEP_ITEMS + place + chunk * lay.chunk_items
        it.item = item
        it.own, it.up = own_ref[0], up_ref[0]
        it.inputs = jnp.concatenate([it.own, partner_ref[0], prior_ref[0]], axis=0)
        queries = dot_t(it.own, query_t)
        back_out = dot_t(it.up, output_w)
        count_own = tab[lay.count_own + item]
        it.counts = (count_own, tab[lay.count_partner + item], count_own * tab[lay.later_day])
        it.groups = []
        for group, weights_ref in enumerate((mine_ref, other_ref)):
            kv_t = weights_ref[0:256, :]
            kv = dot_t(it.inputs, kv_t).astype(BF16)
            lanes = slice(group * GROUP, (group + 1) * GROUP)
            it.groups.append((kv_t, kv, kv.T, queries[:, lanes], back_out[:, lanes]))
        it.outputs_t, it.back_query_t = [], []
        it.keys, it.values = ([], []), ([], [])
        return it

    def start(it, part):
        _, kv, _, group_queries, group_back = it.groups[part // per_group]
        heads = [part % per_group * PACK + h for h in range(PACK)]
        query_pack, back_pack = (
            jnp.concatenate(
                [jnp.where(lane_head == h, rows_of, 0.0) for h in heads], axis=0
            ).astype(BF16)
            for rows_of in (group_queries, group_back)
        )
        logits = dot_t(kv[:, :GROUP], query_pack)
        return it, part, query_pack, back_pack, logits, dot_t(kv[:, GROUP:], back_pack)

    def middle(it, part, query_pack, back_pack, logits, back_weights):
        logits = jnp.concatenate(
            [
                jnp.where(rows < count, logits[index * BLOCK : (index + 1) * BLOCK], -1e30)
                for index, count in enumerate(it.counts)
            ],
            axis=0,
        )
        highest = jnp.max(logits, axis=0, keepdims=True)
        raised = jnp.exp2((logits - highest) * (factor * LOG2E))
        scale = 1.0 / jnp.sum(raised, axis=0, keepdims=True)
        weights = raised * scale
        center = jnp.sum(weights * back_weights, axis=0, keepdims=True)
        back_logits = (weights * ((back_weights - center) * factor)).astype(BF16)
        return it, part, query_pack, back_pack, weights.astype(BF16), back_logits

    def finish(it, part, query_pack, back_pack, weights_low, back_logits):
        group = part // per_group
        kv_cols = it.groups[group][2]
        it.values[group].append(dot(weights_low, back_pack))
        it.keys[group].append(dot(back_logits, query_pack))
        size = PACK * HD
        first = part % per_group * size
        out_t = dot(kv_cols[GROUP + first : GROUP + first + size, :], weights_low)
        query_grad_t = dot(kv_cols[first : first + size, :], back_logits)
        for h in range(PACK):
            lanes = slice(h * BLOCK, (h + 1) * BLOCK)
            it.outputs_t.append(out_t[h * HD : (h + 1) * HD, lanes])
            it.back_query_t.append(query_grad_t[h * HD : (h + 1) * HD, lanes])

    def end(it):
        inputs_t = it.inputs.T
        back_inputs = None
        for group, grad_ref in enumerate((grad_mine_ref, grad_other_ref)):
            kv_t = it.groups[group][0]
            keys, values = it.keys[group], it.values[group]
            back_kv = jnp.concatenate(
                [sum(keys[1:], keys[0]), sum(values[1:], values[0])], axis=1
            ).astype(BF16)
            term = dot(back_kv, kv_t)
            back_inputs = term if back_inputs is None else back_inputs + term
            grad_ref[0:256, :] += dot(inputs_t, back_kv)
        outputs_t = jnp.concatenate(it.outputs_t, axis=0).astype(BF16)
        back_query_t = jnp.concatenate(it.back_query_t, axis=0).astype(BF16)
        query_grad = dot(back_query_t, it.own)
        output_grad = dot(outputs_t, it.up)
        grad_mine_ref[256:384, :] += query_grad[:GROUP]
        grad_other_ref[256:384, :] += query_grad[GROUP:]
        grad_mine_ref[384:512, :] += output_grad[:GROUP]
        grad_other_ref[384:512, :] += output_grad[GROUP:]
        own_out_ref[it.place] = back_inputs[:BLOCK] + dot(back_query_t.T, query_t)
        home_ref[tab[lay.recv_of + it.item]] = back_inputs[BLOCK : 2 * BLOCK].astype(BF16)
        day_ref[it.place] = back_inputs[2 * BLOCK :].astype(BF16)

    parts = 2 * per_group
    items = [begin(0)]
    started = start(items[0], 0)
    waiting = None
    ended = 0
    for index in range(STEP_ITEMS * parts):
        following = None
        if index + 1 < STEP_ITEMS * parts:
            place, part = divmod(index + 1, parts)
            if part == 0:
                items.append(begin(place))
            following = start(items[place], part)
        if waiting is not None:
            finish(*waiting)
            if waiting[1] == parts - 1:
                end(waiting[0])
        waiting = middle(*started)
        started = following
    finish(*waiting)
    end(waiting[0])

    if chunk:
        @pl.when(step == pl.num_programs(0) - 1)
        def _():
            first = lax.rem(lax.axis_index("day"), 2) == 0
            for place, grad_ref in enumerate((grad_mine_ref, grad_other_ref)):
                half = grad_ref.shape[0] // 2
                low, high = grad_ref[:half], grad_ref[half:]
                piece_refs[2 * place][...] = jnp.where(first, low, high).astype(BF16)
                piece_refs[2 * place + 1][...] = jnp.where(first, high, low).astype(BF16)


def fold_kernel(lay, tab, homes, own_a, own_b, day_a, day_b, home_a, home_b, keep, give):
    core = tab[lay.core]
    half = keep.shape[2]

    def one(block, carry):
        item = tab[lay.item_of + block]
        mine = tab[lay.owner_of + block] == core
        place = homes[lay.home_of + block]
        asked = homes[lay.asker_of + block] == core
        early = homes[lay.chunk_of + block] == 0
        in_a = item < lay.chunk_items
        item_a = jnp.minimum(item, lay.chunk_items - 1)
        item_b = jnp.maximum(item - lay.chunk_items, 0)
        own = jnp.where(in_a, own_a[item_a], own_b[item_b])
        own += jnp.where(in_a, day_a[item_a].astype(F32), day_b[item_b].astype(F32))
        home = jnp.where(early, home_a[place].astype(F32), home_b[place].astype(F32))
        total = jnp.where(mine, own, 0.0) + jnp.where(asked, home, 0.0)
        low, high = total[:, :half], total[:, half:]
        keep[block] = jnp.where(core == 0, low, high)
        give[block] = jnp.where(core == 0, high, low)
        return carry

    lax.fori_loop(0, lay.blocks, one, 0)


def add_kernel(kept, got, out):
    out[...] = (kept[...] + got[...]).astype(BF16)


def attend(lay, chunk, tab, in_blocks, up_blocks, received, prior_inputs, pack, pack_other, carried):
    width = in_blocks.shape[-1]
    offset = chunk * lay.chunk_items

    def at_item(place):
        return lambda step, tab: (offset + step * STEP_ITEMS + place, 0, 0)

    def at_block(place):
        return lambda step, tab: (tab[lay.block_of + offset + step * STEP_ITEMS + place], 0, 0)

    def at_recv(place):
        return lambda step, tab: (tab[lay.recv_of + offset + step * STEP_ITEMS + place], 0, 0)

    def at_step(step, tab):
        return (step, 0, 0)

    def fixed(step, tab):
        return (0, 0)

    full_block = (1, BLOCK, width)
    weights_block = (4 * GROUP, width)
    in_specs, operands = [], []
    for place in range(STEP_ITEMS):
        in_specs += [
            pl.BlockSpec(full_block, at_block(place)),
            pl.BlockSpec(full_block, at_block(place)),
            pl.BlockSpec(full_block, at_recv(place)),
            pl.BlockSpec(full_block, at_item(place)),
        ]
        operands += [in_blocks, up_blocks, received, prior_inputs]
    in_specs += [pl.BlockSpec(weights_block, fixed)] * 2
    operands += [pack, pack_other]
    if chunk:
        in_specs += [pl.BlockSpec(weights_block, fixed)] * 2
        operands += carried
    pieces = lay.chunk_items
    grads = [pltpu.HBM(weights_block, F32)] * 2
    if chunk:
        grads = [jax.ShapeDtypeStruct((2 * GROUP, width), BF16)] * 4
    flops = 2 * pieces * (23 * BLOCK * width * width + 24 * BLOCK * 3 * BLOCK * 512)
    return pl.pallas_call(
        lambda *refs: attention_kernel(lay, chunk, *refs),
        grid_spec=pltpu.PrefetchScalarGridSpec(
            num_scalar_prefetch=1,
            grid=(pieces // STEP_ITEMS,),
            in_specs=in_specs,
            out_specs=(
                pl.BlockSpec((STEP_ITEMS, BLOCK, width), at_step),
                pl.BlockSpec((STEP_ITEMS, BLOCK, width), at_step),
                pl.BlockSpec((lay.places, BLOCK, width), lambda step, tab: (0, 0, 0)),
                *[pl.BlockSpec(grad.shape, fixed) for grad in grads],
            ),
            scratch_shapes=[pltpu.VMEM(weights_block, F32)] * (2 if chunk else 0),
        ),
        out_shape=(
            pltpu.HBM((pieces, BLOCK, width), F32),
            pltpu.HBM((pieces, BLOCK, width), BF16),
            pltpu.HBM((lay.places, BLOCK, width), BF16),
            *grads,
        ),
        compiler_params=pltpu.CompilerParams(vmem_limit_bytes=32 << 20),
        cost_estimate=pl.CostEstimate(
            flops=flops, bytes_accessed=5 << 20, transcendentals=pieces * 8 * BLOCK * 3 * BLOCK
        ),
        name=f"attention_{chunk}",
    )(
        tab,
        *[
            value
            if value is received
            else pltpu.with_memory_space_constraint(value, pltpu.HBM)
            for value in operands
        ],
    )


def exchanged(value, axis, bit):
    count = lax.axis_size(axis)
    return lax.ppermute(value, axis, [(place, place ^ bit) for place in range(count)])


def summed_over(value, axis, bit):
    low = value.astype(BF16)
    return low.astype(F32) + exchanged(low, axis, bit).astype(F32)


def neighbours(axis, other):
    size = lax.axis_size(other)
    return [
        (place * size + at, (place ^ 1) * size + (at ^ 1))
        for place in range(lax.axis_size(axis))
        for at in range(size)
    ]


def sum_gradients(part, home_b, fold):
    bit = 2
    while bit < lax.axis_size("day"):
        part = summed_over(part, "day", bit)
        bit *= 2
    half = part.shape[0] // 2
    first = lax.rem(lax.axis_index("reach"), 2) == 0
    low = part.astype(BF16)
    kept = jnp.where(first, low[:half], low[half:])
    given = jnp.where(first, low[half:], low[:half])
    part = kept.astype(F32) + exchanged(given, "reach", 1).astype(F32)
    part, home_b = lax.optimization_barrier((part, home_b))
    bit = 2
    while bit < lax.axis_size("reach"):
        part = summed_over(part, "reach", bit)
        bit *= 2
    part, folded = lax.optimization_barrier((part.astype(BF16), fold(home_b)))
    quarters = (
        part,
        exchanged(part, "reach", 1),
        exchanged(part, "day", 1),
        lax.ppermute(part, ("reach", "day"), neighbours("reach", "day")),
    )
    return quarters, folded


def split_kernel(mine, along_reach, along_day, along_both, query_out, key_out, value_out, output_out):
    day_half = lax.rem(lax.axis_index("day"), 2) == 0
    reach_half = lax.rem(lax.axis_index("reach"), 2) == 0

    def quarter(by_day, by_reach):
        near = jnp.where(reach_half == by_reach, mine[...], along_reach[...])
        far = jnp.where(reach_half == by_reach, along_day[...], along_both[...])
        return jnp.where(day_half == by_day, near, far).astype(F32)

    for place, by_reach in enumerate((True, False)):
        rows = quarter(True, by_reach)
        key_out[place * GROUP : (place + 1) * GROUP] = rows[:, :GROUP]
        value_out[place * GROUP : (place + 1) * GROUP] = rows[:, GROUP:]
    query_out[...] = quarter(False, True).T
    output_out[...] = quarter(False, False)


def on_device(
    inputs, upstream, query_weight, key_weight, value_weight, output_weight, partner, counts
):
    days_dev, rows_dev, width = inputs.shape
    assert days_dev == 1 and width == 2 * GROUP
    blocks_dev = rows_dev // BLOCK
    reach_total = lax.axis_size("reach")
    day_total = lax.axis_size("day")
    assert lax.axis_size("head") == CORES
    lay = Layout(blocks_dev, reach_total)
    half = width // 2
    in_blocks = inputs.reshape(blocks_dev, BLOCK, width)
    up_blocks = upstream.reshape(blocks_dev, BLOCK, width)
    pack = jnp.concatenate([key_weight.T, value_weight.T, query_weight.T, output_weight], axis=0)
    pack_other = exchanged(pack, "head", 1)

    smem = pl.BlockSpec(memory_space=pltpu.SMEM)
    in_vmem = pl.BlockSpec(memory_space=pltpu.VMEM)
    anywhere = pl.BlockSpec(memory_space=pl.ANY)
    sent_shape = jax.ShapeDtypeStruct((lay.places, BLOCK, width), BF16)
    sent_a, homes = pl.pallas_call(
        lambda *refs: pick_kernel(lay, *refs),
        out_shape=(sent_shape, jax.ShapeDtypeStruct((lay.homes_size,), jnp.int32)),
        in_specs=[anywhere, anywhere],
        out_specs=(in_vmem, smem),
        scratch_shapes=[
            pltpu.SMEM(partner.shape, jnp.int32),
            pltpu.VMEM((blocks_dev, BLOCK, width), BF16),
            pltpu.SemaphoreType.DMA((2,)),
        ],
        compiler_params=pltpu.CompilerParams(vmem_limit_bytes=16 << 20),
        name="pick",
    )(
        pltpu.with_memory_space_constraint(partner, pltpu.HBM),
        pltpu.with_memory_space_constraint(in_blocks, pltpu.HBM),
    )
    sent_b, prior, tab = pl.pallas_call(
        lambda *refs: deal_kernel(lay, *refs),
        out_shape=(
            sent_shape,
            jax.ShapeDtypeStruct((lay.items, BLOCK, width), BF16),
            jax.ShapeDtypeStruct((lay.size,), jnp.int32),
        ),
        in_specs=[smem, smem, smem, in_vmem],
        out_specs=(in_vmem, in_vmem, smem),
        scratch_shapes=[
            pltpu.SMEM((lay.reach,), jnp.int32),
            pltpu.SMEM((lay.reach,), jnp.int32),
        ],
        compiler_params=pltpu.CompilerParams(vmem_limit_bytes=16 << 20),
        name="deal",
    )(partner, counts, homes, in_blocks)

    def ring(value):
        shape = value.shape
        value = value.reshape(lay.reach, lay.slots * BLOCK, width)
        return lax.all_to_all(value, "reach", 0, 0, tiled=True).reshape(shape)

    next_day = [(d, d + 1) for d in range(day_total - 1)]
    last_day = [(d + 1, d) for d in range(day_total - 1)]
    received_a = ring(sent_a)
    prior_inputs = lax.ppermute(prior, "day", next_day)
    received_b = ring(sent_b)
    shared = (prior_inputs, pack, pack_other)
    own_a, day_a, home_a, *grads = attend(
        lay, 0, tab, in_blocks, up_blocks, received_a, *shared, None
    )
    home_a = ring(home_a)
    day_a = lax.ppermute(day_a, "day", last_day)
    own_b, day_b, home_b, kept, to_day, to_core, to_both = attend(
        lay, 1, tab, in_blocks, up_blocks, received_b, *shared, grads
    )
    pieces = (
        exchanged(to_day, "day", 1),
        exchanged(to_core, "head", 1),
        lax.ppermute(to_both, ("day", "head"), neighbours("day", "head")),
    )
    home_a, home_b, kept = lax.optimization_barrier((home_a, home_b, kept))
    pieces = (kept, *pieces)
    home_b = ring(home_b)
    day_b = lax.ppermute(day_b, "day", last_day)
    half_shape = jax.ShapeDtypeStruct((blocks_dev, BLOCK, half), F32)

    def fold(home_b):
        return pl.pallas_call(
            lambda *refs: fold_kernel(lay, *refs),
            out_shape=(half_shape, half_shape),
            in_specs=[smem] * 2 + [in_vmem] * 6,
            out_specs=[in_vmem] * 2,
            compiler_params=pltpu.CompilerParams(vmem_limit_bytes=16 << 20),
            name="fold",
        )(tab, homes, own_a, own_b, day_a, day_b, home_a, home_b)

    quarters, (keep, give) = sum_gradients(
        sum(piece.astype(F32) for piece in pieces), home_b, fold
    )
    got = exchanged(give, "head", 1)
    got, along_both = lax.optimization_barrier((got, quarters[3]))
    quarters = (*quarters[:3], along_both)
    back_blocks = pl.pallas_call(
        add_kernel,
        out_shape=jax.ShapeDtypeStruct((blocks_dev, BLOCK, half), BF16),
        in_specs=[in_vmem] * 2,
        out_specs=in_vmem,
        compiler_params=pltpu.CompilerParams(vmem_limit_bytes=16 << 20),
        name="add",
    )(keep, got)
    back_blocks, quarters = lax.optimization_barrier((back_blocks, quarters))
    weight_grads = pl.pallas_call(
        split_kernel,
        out_shape=(
            jax.ShapeDtypeStruct((width, half), F32),
            jax.ShapeDtypeStruct((width, half), F32),
            jax.ShapeDtypeStruct((width, half), F32),
            jax.ShapeDtypeStruct((half, width), F32),
        ),
        grid=(1,),
        compiler_params=pltpu.CompilerParams(vmem_limit_bytes=16 << 20),
        name="split",
    )(*quarters)

    return (back_blocks.reshape(1, rows_dev, half), *weight_grads)


def solution(mesh):
    placed = (
        P(("groups", "day"), "reach", None),
        P(("groups", "day"), "reach", None),
        P(None, "head"),
        P(None, "head"),
        P(None, "head"),
        P("head", None),
        P("groups"),
        P("groups"),
    )
    return jax.shard_map(
        on_device,
        mesh=mesh,
        in_specs=placed,
        out_specs=(
            P(("groups", "day"), "reach", "head"),
            P("groups", "head"),
            P("groups", "head"),
            P("groups", "head"),
            P(("groups", "head"), None),
        ),
        check_vma=False,
    )
```
